32 devices in a mesh: particle: 8 (over y, x, core), slab: 4 (over z).
Axes of the slice: x: 2, y: 2, z: 4, core: 2. Of those that a mesh axis runs over, the one named last changes fastest.
Arguments:
- vel_coarse: float32 [8, 16, 8, 64], P('particle', 'slab'), may hold values from 1.5 to 3.5
- fwd_prev: float32 [8, 32, 16, 128], P('particle', 'slab'), may hold values from -6 to 6
- fwd_cur: float32 [8, 32, 16, 128], P('particle', 'slab'), may hold values from -6 to 6
- adj_far: float32 [8, 32, 16, 128], P('particle', 'slab'), may hold values from -6 to 6
- adj_near: float32 [8, 32, 16, 128], P('particle', 'slab'), may hold values from -6 to 6
- src_cell: int32 [8], P('particle'), may hold values from 0 to 65535
- src_step: int32 [8], P('particle'), may hold values from 0 to 61
- wavelet: float32 [64], replicated, may hold values from -24 to 24
- rec_cell: int32 [256], replicated, may hold values from 0 to 65535
- observed: float32 [2, 256], replicated, may hold values from -6 to 6
Outputs:
- update: float32 [8, 16, 8, 64], P('particle', 'slab')
- misfit: float32 [8, 2, 256], P('particle')
The draws below stay inside these ranges and needn't reach their ends.
Inputs may be any that keep to these rules, and one draw needn't show every extreme that they name: `src_cell`: a flat index (x 16 + y) * 128 + z of the grid. The wavelet samples used are src_step + 1 and src_step + 2. `rec_cell`: flat indices as for src_cell; cells may repeat.
All inputs are finite; a program needn't handle non-finite values.
Results may differ from the reference program's by a relative error of at most 0.00028.
Values sent between devices are 32-bit elements; how exact they have to be, the bound alone decides.
No kernel may reach another device: no remote copies, remote signals or barrier semaphores. Data moves between devices by JAX's collectives and lax.ppermute only.
A program may use at most 64 MiB of HBM per device.

```python
import jax
import jax.numpy as jnp
from jax import lax

NY = 16
NZ = 128
NREC = 256
NT = 64
PARTICLES = 8
NX = 32


def plant(drawn, own_key, smallest, high):
    dims = drawn.shape
    place = [jax.random.randint(jax.random.fold_in(own_key, axis), (), 0, dims[axis]) for axis in range(len(dims))]
    drawn = drawn.at[tuple(place)].set(smallest)
    longest = dims.index(max(dims))
    place[longest] = (place[longest] + 1) % dims[longest]
    return drawn.at[tuple(place)].set(high)


def levels(key, dims, pieces, least, top_value):
    loudness = 1.0
    for axis_at, parts in pieces:
        heights = jax.random.uniform(jax.random.fold_in(jax.random.fold_in(key, 6), axis_at), (parts,), jnp.float32, least / len(pieces), top_value / len(pieces))
        loudness = loudness * jnp.repeat(jnp.exp(heights), dims[axis_at] // parts).reshape((-1,) + (1,) * (len(dims) - 1 - axis_at))
    return loudness


def scatter_about(own_key, shape, spread, most, shards=(), kind=jnp.bfloat16):
    level = levels(own_key, shape, shards, -0.22, 0.18) if shards else 1.0
    values = jax.random.normal(own_key, shape, jnp.float32) * spread * level
    return jnp.minimum(jnp.maximum(values, -most), most).astype(kind)


def setup_inputs(seed: int = 0) -> dict:
    seeds = jax.random.split(jax.random.key(seed), 11)
    vel_coarse = jnp.clip(1.5 + 2.0 * jax.random.uniform(seeds[0], (PARTICLES, NX // 2, NY // 2, NZ // 2), jnp.float32) ** levels(seeds[0], (PARTICLES, NX // 2, NY // 2, NZ // 2), ((0, 8), (1, 4)), -0.2, 0.2), 1.5, 3.5)
    fwd_prev = scatter_about(seeds[1], (PARTICLES, NX, NY, NZ), 1.0, 6.0, ((0, 8), (1, 4)), jnp.float32)
    fwd_cur = scatter_about(seeds[2], (PARTICLES, NX, NY, NZ), 1.0, 6.0, ((0, 8), (1, 4)), jnp.float32)
    adj_far = scatter_about(seeds[3], (PARTICLES, NX, NY, NZ), 1.0, 6.0, ((0, 8), (1, 4)), jnp.float32)
    adj_near = scatter_about(seeds[4], (PARTICLES, NX, NY, NZ), 1.0, 6.0, ((0, 8), (1, 4)), jnp.float32)
    src_cell = plant(jax.random.randint(seeds[5], (PARTICLES,), 0, NX * NY * NZ), jax.random.fold_in(seeds[5], 1), 0, (NX * NY * NZ) - 1).astype(jnp.int32)
    src_step = plant(jax.random.randint(seeds[6], (PARTICLES,), 0, NT - 2), jax.random.fold_in(seeds[6], 1), 0, (NT - 2) - 1).astype(jnp.int32)
    wavelet = scatter_about(seeds[7], (NT,), 4.0, 24.0, (), jnp.float32)
    rec_cell = plant(jax.random.randint(seeds[8], (NREC,), 0, NX * NY * NZ), jax.random.fold_in(seeds[8], 1), 0, (NX * NY * NZ) - 1).astype(jnp.int32)
    observed = scatter_about(seeds[9], (2, NREC), 1.0, 6.0, (), jnp.float32)
    return dict(vel_coarse=vel_coarse, fwd_prev=fwd_prev, fwd_cur=fwd_cur, adj_far=adj_far, adj_near=adj_near, src_cell=src_cell, src_step=src_step, wavelet=wavelet, rec_cell=rec_cell, observed=observed)


STENCIL_WEIGHTS = (-205.0 / 72.0, 8.0 / 5.0, -1.0 / 5.0, 8.0 / 315.0, -1.0 / 560.0)
COURANT_FACTOR = 0.1


def laplace(extended):
    length = extended.shape[0] - 8
    size_y = extended.shape[1]
    size_z = extended.shape[2]
    padded = jnp.pad(extended, ((0, 0), (4, 4), (4, 4)))

    def window(shift_x, shift_y, shift_z):
        return padded[4 + shift_x:4 + shift_x + length, 4 + shift_y:4 + shift_y + size_y, 4 + shift_z:4 + shift_z + size_z]

    result = (3.0 * STENCIL_WEIGHTS[0]) * window(0, 0, 0)
    for offset in range(1, 5):
        pairs = (window(offset, 0, 0) + window(-offset, 0, 0)) + (window(0, offset, 0) + window(0, -offset, 0)) + (window(0, 0, offset) + window(0, 0, -offset))
        result = result + STENCIL_WEIGHTS[offset] * pairs
    return result


def advance(older, newer, courant_sq):
    extended = jnp.pad(newer, ((4, 4), (0, 0), (0, 0)))
    return 2.0 * newer - older + courant_sq * laplace(extended)


def add_at(field, cells, values):
    return field.reshape(-1).at[cells].add(values).reshape(field.shape)


def one_particle(model, prev_field, cur_field, far_field, near_field, source, step_now, wavelet, rec_cell, observed):
    speed = jnp.repeat(jnp.repeat(jnp.repeat(model, 2, axis=0), 2, axis=1), 2, axis=2)
    courant_sq = (COURANT_FACTOR * speed) ** 2
    first = add_at(advance(prev_field, cur_field, courant_sq), source, jnp.take(wavelet, step_now + 1))
    second = add_at(advance(cur_field, first, courant_sq), source, jnp.take(wavelet, step_now + 2))
    samples = jnp.stack([first.reshape(-1)[rec_cell], second.reshape(-1)[rec_cell]])
    residual = samples - observed
    adj_two = add_at(advance(far_field, near_field, courant_sq), rec_cell, residual[1])
    adj_one = add_at(advance(near_field, adj_two, courant_sq), rec_cell, residual[0])
    image = adj_two * (second - 2.0 * first + cur_field) + adj_one * (first - 2.0 * cur_field + prev_field)
    fine_grad = (-2.0 / (speed * speed * speed)) * image
    size_x, size_y, size_z = model.shape
    coarse = fine_grad.reshape(size_x, 2, size_y, 2, size_z, 2).sum(axis=(1, 3, 5))
    return coarse, residual


def reference(vel_coarse, fwd_prev, fwd_cur, adj_far, adj_near, src_cell, src_step, wavelet, rec_cell, observed):
    def per_particle(items):
        return one_particle(items[0], items[1], items[2], items[3], items[4], items[5], items[6], wavelet, rec_cell, observed)

    grads, misfit = lax.map(per_particle, (vel_coarse, fwd_prev, fwd_cur, adj_far, adj_near, src_cell, src_step))
    count = vel_coarse.shape[0]

    def distance_row(index):
        own = lax.dynamic_index_in_dim(vel_coarse, index, 0, keepdims=True)
        return jnp.sum((vel_coarse - own) ** 2, axis=(1, 2, 3))

    dist = lax.map(distance_row, jnp.arange(count, dtype=jnp.int32))
    band = jnp.sum(dist) / (count * (count - 1))
    kernel = jnp.exp(-dist / band)
    cells_coarse = vel_coarse.shape[1] * vel_coarse.shape[2] * vel_coarse.shape[3]
    mix_grad = jnp.einsum('pq,qxyz->pxyz', kernel, -grads, precision=lax.Precision.HIGHEST)
    mix_model = jnp.einsum('pq,qxyz->pxyz', kernel, vel_coarse, precision=lax.Precision.HIGHEST)
    kernel_sum = jnp.sum(kernel, axis=1)
    coef = 2.0 * cells_coarse / band
    update = (mix_grad + coef * (vel_coarse * kernel_sum[:, None, None, None] - mix_model)) / count
    return update, misfit
```

```python
import jax
import jax.numpy as jnp
from jax import lax
from jax.experimental import pallas as pl
from jax.experimental.pallas import tpu as pltpu
from jax.sharding import PartitionSpec as P

STENCIL_WEIGHTS = (-205.0 / 72.0, 8.0 / 5.0, -1.0 / 5.0, 8.0 / 315.0, -1.0 / 560.0)
COURANT_FACTOR = 0.1
REACH = 4
PITCH = 32
HIGHEST = lax.Precision.HIGHEST


def swap(block, axis, pairs):
    both = [(a, b) for a, b in pairs] + [(b, a) for a, b in pairs]
    return lax.ppermute(block, axis, both)


def twice(model):
    flat = model.reshape(model.shape[0] * model.shape[1], model.shape[2])
    return jnp.concatenate([flat, flat], axis=1)


def pack_kernel(prev, cur, near, far, vel, to_one, to_two, to_far):
    width = prev.shape[0]
    place = lax.axis_index("slab")
    odd = place % 2
    top = width - REACH
    model = twice(vel[...]).reshape(-1, prev.shape[1], prev.shape[2])
    for ref, low in ((to_one, odd), (to_two, 1 - odd)):
        ref[0:width] = prev[...]
        ref[width : 2 * width] = cur[...]
        ref[2 * width : 3 * width] = near[...]
        ref[3 * width : 3 * width + REACH] = far[pl.ds((1 - low) * top, REACH)]
        ref[3 * width + REACH :] = model
    to_far[0:REACH] = cur[pl.ds((1 - (place % 4) // 2) * top, REACH)]
    to_far[REACH:] = model


def split3(values):
    high = values.astype(jnp.bfloat16)
    rest = values - high.astype(jnp.float32)
    middle = rest.astype(jnp.bfloat16)
    low = (rest - middle.astype(jnp.float32)).astype(jnp.bfloat16)
    return (high, middle, low)


def wave_kernel(
    src_cell, src_step, wavelet, prev, cur, far, near, vel, rec, obs, one, two, *rest, n_far, with_models
):
    fars = rest[:n_far]
    rest = rest[n_far:]
    if with_models:
        ends, rest = rest[0], rest[1:]
    pay, samples = rest[:2]
    cur_s, prev_s, near_s, far_s, first_s, sec_s, two_s, vel_s, c2_s, img_s = rest[2:]
    width, size_y, size_z = prev.shape
    half = width // 2
    coarse_y = size_y // 2
    place = lax.axis_index("slab")
    odd = place % 2
    f32 = jnp.float32
    data = pl.ds(8, size_y)
    for ref in (cur_s, first_s, near_s, two_s):
        ref[:, 0:8, :] = jnp.zeros((ref.shape[0], 8, size_z), f32)
        ref[:, 8 + size_y : PITCH, :] = jnp.zeros((ref.shape[0], PITCH - 8 - size_y, size_z), f32)
    wide = 2 * REACH
    cur_s[wide + REACH : wide + REACH + width, data, :] = cur[...]
    prev_s[wide : wide + width] = prev[...]
    near_s[wide : wide + width, data, :] = near[...]
    far_s[REACH : REACH + width] = far[...]
    own_vel = twice(vel[...])
    rows = half * coarse_y
    vel_s[rows : 2 * rows] = own_vel

    def put(block, high):
        base = high * (width + wide)
        prev_s[pl.ds(base, width)] = block[0:width]
        cur_s[pl.ds(base + REACH, width), data, :] = block[width : 2 * width]
        near_s[pl.ds(base, width), data, :] = block[2 * width : 3 * width]
        far_s[pl.ds(high * (width + REACH), REACH)] = block[3 * width : 3 * width + REACH]
        model = block[3 * width + REACH :].reshape(rows, size_z)
        vel_s[pl.ds(high * 2 * rows, rows)] = model
        return model

    model_one = put(one, 1 - odd)
    put(two, odd)
    far_high = 1 - (place % 4) // 2
    edge = 2 * wide + width + REACH
    models_far = []
    if n_far == 1:
        zero = jnp.zeros((REACH, size_y, size_z), f32)
        cur_s[pl.ds((1 - far_high) * edge, REACH), data, :] = zero
    for index, block in enumerate(fars):
        high = far_high if index == 0 else 1 - far_high
        cur_s[pl.ds(high * edge, REACH), data, :] = block[0:REACH]
        models_far.append(block[REACH:].reshape(rows, size_z))

    lane = lax.broadcasted_iota(jnp.int32, (1, size_z), 1)
    up_w = [None] + [jnp.where(lane >= k, STENCIL_WEIGHTS[k], 0.0).astype(f32) for k in range(1, 5)]
    down_w = [None] + [
        jnp.where(lane < size_z - k, STENCIL_WEIGHTS[k], 0.0).astype(f32) for k in range(1, 5)
    ]

    grid_r = lax.broadcasted_iota(jnp.int32, (size_z, size_z), 0)
    grid_c = lax.broadcasted_iota(jnp.int32, (size_z, size_z), 1)
    spread = jnp.where(grid_r == grid_c // 2, 1.0, 0.0).astype(f32)
    gather = jnp.where(grid_r // 2 == grid_c, 1.0, 0.0).astype(f32)
    scaled = COURANT_FACTOR * vel_s[...]
    fine_z = jnp.dot(scaled * scaled, spread, precision=HIGHEST, preferred_element_type=f32)
    count = fine_z.shape[0]
    c2_s[pl.ds(0, count, stride=2), :] = fine_z
    c2_s[pl.ds(1, count, stride=2), :] = fine_z

    step = 4

    def courant(layer):
        block = c2_s[layer // 2 * size_y : (layer + step) // 2 * size_y, :]
        block = block.reshape(step // 2, 1, size_y, size_z)
        return jnp.broadcast_to(block, (step // 2, 2, size_y, size_z)).reshape(step, size_y, size_z)

    def laplace(ref, at):
        centre = ref[at : at + step, data, :]
        flat = centre.reshape(step * size_y, size_z)
        total = (3.0 * STENCIL_WEIGHTS[0]) * centre
        for k in range(1, 5):
            pairs = (
                ref[at + k : at + k + step, data, :]
                + ref[at - k : at - k + step, data, :]
                + (ref[at : at + step, pl.ds(8 + k, size_y), :] + ref[at : at + step, pl.ds(8 - k, size_y), :])
            )
            along = pltpu.roll(flat, k, 1) * up_w[k] + pltpu.roll(flat, size_z - k, 1) * down_w[k]
            total = total + STENCIL_WEIGHTS[k] * pairs + along.reshape(step, size_y, size_z)
        return centre, total

    plane = size_y * size_z
    cell = src_cell[0]
    now = src_step[0]
    src_y = (cell % plane) // size_z
    src_z = cell % size_z

    def inject(ref, start, layers, offset, pulse):
        layer = cell // plane - (place * width - start)
        inside = (layer >= 0) & (layer < layers)
        layer = jnp.clip(layer, 0, layers - 1)
        value = jnp.where(inside, pulse, 0.0)
        at = pl.ds(offset + src_y, 1)
        ref[layer, at, :] = ref[layer, at, :] + jnp.where(lane == src_z, value, 0.0)

    for ch in range(0, width + 2 * wide, step):
        centre, total = laplace(cur_s, ch + REACH)
        first_s[ch : ch + step, data, :] = 2.0 * centre - prev_s[ch : ch + step] + courant(ch) * total
    inject(first_s, wide, width + 2 * wide, 8, wavelet[now + 1])
    for ch in range(0, width + 2 * REACH, step):
        centre, total = laplace(first_s, ch + REACH)
        older = cur_s[ch + wide : ch + wide + step, data, :]
        sec_s[ch : ch + step] = 2.0 * centre - older + courant(ch + REACH) * total
    inject(sec_s, REACH, width + 2 * REACH, 0, wavelet[now + 2])

    region = (width + 2 * REACH) * size_y
    cells = rec[...]
    row = (cells - (place * width - REACH) * plane) // size_z
    hot = row == lax.broadcasted_iota(jnp.int32, (region, cells.shape[1]), 0)
    hot = jnp.where(hot, 1.0, 0.0).astype(jnp.bfloat16)
    lanes = lax.broadcasted_iota(jnp.int32, (size_z, cells.shape[1]), 0) == cells % size_z
    lo = REACH * size_y
    hi = lo + width * size_y
    own = (row >= lo) & (row < hi)

    def read(field, marks):
        turned = field.T
        total = sum(jnp.dot(part, marks, preferred_element_type=f32) for part in split3(turned))
        return jnp.sum(jnp.where(lanes, total, 0.0), axis=0, keepdims=True)

    def spread_out(values, marks):
        placed = jnp.where(lanes, values, 0.0)
        dims = (((1,), (1,)), ((), ()))
        return sum(lax.dot_general(marks, part, dims, preferred_element_type=f32) for part in split3(placed))

    first_own = first_s[wide : wide + width, data, :].reshape(width * size_y, size_z)
    read_one = read(first_own, hot[lo:hi])
    read_two = read(sec_s[...].reshape(region, size_z), hot)
    samples[0:1, :] = read_one
    samples[1:2, :] = jnp.where(own, read_two, 0.0)
    add_one = spread_out(read_one - obs[0:1, :], hot[lo:hi])
    add_two = spread_out(read_two - obs[1:2, :], hot)

    for ch in range(0, width + 2 * REACH, step):
        centre, total = laplace(near_s, ch + REACH)
        extra = add_two[ch * size_y : (ch + step) * size_y].reshape(step, size_y, size_z)
        two_s[ch : ch + step, data, :] = (
            2.0 * centre - far_s[ch : ch + step] + courant(ch + REACH) * total + extra
        )
    for ch in range(0, width, step):
        centre, total = laplace(two_s, ch + REACH)
        extra = add_one[ch * size_y : (ch + step) * size_y].reshape(step, size_y, size_z)
        older = near_s[ch + wide : ch + wide + step, data, :]
        adj_one = 2.0 * centre - older + courant(ch + wide) * total + extra
        first = first_s[ch + wide : ch + wide + step, data, :]
        now_field = cur_s[ch + wide + REACH : ch + wide + REACH + step, data, :]
        bend_two = sec_s[ch + REACH : ch + REACH + step] - 2.0 * first + now_field
        bend_one = first - 2.0 * now_field + prev_s[ch + wide : ch + wide + step]
        image = centre * bend_two + adj_one * bend_one
        image = image.reshape(step // 2, 2, size_y, size_z)
        image = image[:, 0] + image[:, 1]
        img_s[ch // 2 * size_y : (ch + step) // 2 * size_y, :] = image.reshape(step // 2 * size_y, size_z)
    folded = img_s[pl.ds(0, rows, stride=2), :] + img_s[pl.ds(1, rows, stride=2), :]
    blocks = jnp.dot(folded, gather, precision=HIGHEST, preferred_element_type=f32)
    factor = 2.0 / (own_vel * own_vel * own_vel)
    left = lane < size_z // 2
    pay[0:rows, :] = jnp.where(left, factor * blocks, own_vel)
    if with_models:
        pay[rows : 2 * rows, :] = jnp.where(left, model_one, models_far[0])
        pay[2 * rows : 3 * rows, :] = jnp.where(left, twice(ends[...]), 0.0)


def mix_kernel(*refs, cells):
    count = len(refs) - 5
    pays = refs[:count]
    part, other, obs, update, misfit = refs[count:]
    f32 = jnp.float32
    misfit[...] = part[...] + other[...] - obs[...]
    rows = update.shape[0] * update.shape[1]
    lane = lax.broadcasted_iota(jnp.int32, (1, pays[0].shape[1]), 1)
    half = update.shape[2]
    model_lane = lane >= half
    total = pays[0].shape[0]
    mean = sum(ref[...] for ref in pays[1:]) + pays[0][...]
    mean = mean * (1.0 / count)

    def norm(diff):
        sq = diff * diff
        sq = jnp.concatenate([jnp.where(model_lane, sq[0:rows], 0.0), sq[rows:]], axis=0)
        sq = jnp.sum(sq.reshape(total // 8, 8, sq.shape[1]), axis=0)
        return jnp.sum(jnp.sum(sq, axis=1, keepdims=True), axis=0, keepdims=True)

    spread = jnp.zeros(mean.shape, f32)
    for ref in pays:
        diff = ref[...] - mean
        spread = spread + diff * diff
    spread = jnp.concatenate([jnp.where(model_lane, spread[0:rows], 0.0), spread[rows:]], axis=0)
    spread = jnp.sum(spread.reshape(total // 8, 8, spread.shape[1]), axis=0)
    spread = jnp.sum(jnp.sum(spread, axis=1, keepdims=True), axis=0, keepdims=True)
    band = (2.0 * count / (count * (count - 1))) * spread
    own = pays[0][...]
    mixed = own[0:rows]
    kernel_sum = jnp.ones((1, 1), f32)
    for ref in pays[1:]:
        weight = jnp.exp(-norm(ref[...] - own) / band)
        mixed = mixed + weight * ref[0:rows, :]
        kernel_sum = kernel_sum + weight
    coef = (2.0 * cells) / band
    pull = coef * (own[0:rows, half:] * kernel_sum - mixed[:, half:])
    update[...] = ((mixed[:, 0:half] + pull) * (1.0 / count)).reshape(update.shape)


def on_device(
    vel_coarse,
    fwd_prev,
    fwd_cur,
    adj_far,
    adj_near,
    src_cell,
    src_step,
    wavelet,
    rec_cell,
    observed,
):
    f32 = jnp.float32
    slabs = lax.axis_size("slab")
    count = lax.axis_size("particle")
    fast = slabs == 4 and count == 8
    model = vel_coarse[0]
    prev, cur, far, near = fwd_prev[0], fwd_cur[0], adj_far[0], adj_near[0]
    width, size_y, size_z = prev.shape
    half, coarse_y, coarse_z = model.shape
    rows = half * coarse_y
    model_layers = rows // size_y
    near_layers = 3 * width + REACH + model_layers
    far_layers = REACH + model_layers
    in_vmem = pl.BlockSpec(memory_space=pltpu.VMEM)
    if fast:
        beside = swap(model, "slab", [(0, 1), (2, 3)])
    to_one, to_two, to_far = pl.pallas_call(
        pack_kernel,
        out_shape=(
            jax.ShapeDtypeStruct((near_layers, size_y, size_z), f32),
            jax.ShapeDtypeStruct((near_layers, size_y, size_z), f32),
            jax.ShapeDtypeStruct((far_layers, size_y, size_z), f32),
        ),
        in_specs=[in_vmem] * 5,
        out_specs=(in_vmem,) * 3,
        name="pack_halos",
    )(prev, cur, near, far, model)
    one = swap(to_one, "slab", [(i, i + 1) for i in range(0, slabs - 1, 2)])
    two = swap(to_two, "slab", [(i, i + 1) for i in range(1, slabs - 1, 2)])
    fars = [swap(to_far, "slab", [(i, i + 2) for i in range(slabs - 2) if i % 4 < 2])]
    others = [(i, i + 2) for i in range(slabs - 2) if i % 4 >= 2]
    if others:
        fars.append(swap(other_side(cur, to_far), "slab", others))
    extra = []
    if fast:
        extra = [swap(beside, "slab", [(0, 2), (1, 3)])]
    in_smem = pl.BlockSpec(memory_space=pltpu.SMEM)
    receivers = rec_cell.shape[0]
    wide = 2 * REACH
    pay_rows = 3 * rows if fast else rows
    pay, samples = pl.pallas_call(
        lambda *refs: wave_kernel(*refs, n_far=len(fars), with_models=fast),
        out_shape=(
            jax.ShapeDtypeStruct((pay_rows, size_z), f32),
            jax.ShapeDtypeStruct((2, receivers), f32),
        ),
        in_specs=[in_smem] * 3 + [in_vmem] * (9 + len(fars) + len(extra)),
        out_specs=(in_vmem, in_vmem),
        scratch_shapes=[
            pltpu.VMEM((width + 2 * (wide + REACH), PITCH, size_z), f32),
            pltpu.VMEM((width + 2 * wide, size_y, size_z), f32),
            pltpu.VMEM((width + 2 * wide, PITCH, size_z), f32),
            pltpu.VMEM((width + 2 * REACH, size_y, size_z), f32),
            pltpu.VMEM((width + 2 * wide, PITCH, size_z), f32),
            pltpu.VMEM((width + 2 * REACH, size_y, size_z), f32),
            pltpu.VMEM((width + 2 * REACH, PITCH, size_z), f32),
            pltpu.VMEM((3 * rows, size_z), f32),
            pltpu.VMEM((6 * rows, size_z), f32),
            pltpu.VMEM((2 * rows, size_z), f32),
        ],
        name="wave_steps",
    )(
        src_cell, src_step, wavelet, prev, cur, far, near, model, rec_cell[None], observed,
        one, two, *fars, *extra,
    )
    cells_coarse = rows * slabs * coarse_z
    if not fast:
        residual = lax.psum(samples, "slab") - observed
        gathered = lax.all_gather(pay, "particle", axis=0)
        models = gathered[:, :, coarse_z:]
        deltas = models[:, None] - models[None]
        dist = lax.psum(jnp.sum(deltas * deltas, axis=(2, 3)), "slab")
        band = jnp.sum(dist) / (count * (count - 1))
        row = lax.dynamic_index_in_dim(dist, lax.axis_index("particle"), 0, keepdims=False)
        weights = jnp.exp(-row / band)
        mixed = jnp.einsum("q,qrz->rz", weights, gathered, precision=HIGHEST)
        own = pay[:, coarse_z:]
        pull = (2.0 * cells_coarse / band) * (own * jnp.sum(weights) - mixed[:, coarse_z:])
        update = (mixed[:, :coarse_z] + pull) / count
        return (update.reshape(model.shape)[None], residual[None])

    blocks = {0: pay}
    for flip in (6, 4, 2):
        blocks[flip] = swap(pay, "particle", [(i, i ^ flip) for i in range(count) if i < i ^ flip])
    for flip in (0, 6, 4, 2):
        pairs = [(i, i ^ 1) for i in range(0, count, 2)]
        blocks[flip + 1] = swap(blocks[flip], "particle", pairs)
    part = samples + swap(samples, "slab", [(0, 1), (2, 3)])
    other = swap(part, "slab", [(0, 2), (1, 3)])
    update, residual = pl.pallas_call(
        lambda *refs: mix_kernel(*refs, cells=cells_coarse),
        out_shape=(
            jax.ShapeDtypeStruct(model.shape, f32),
            jax.ShapeDtypeStruct((2, receivers), f32),
        ),
        in_specs=[in_vmem] * 11,
        out_specs=(in_vmem, in_vmem),
        name="mix_particles",
    )(*[blocks[i] for i in range(count)], part, other, observed)
    return (update[None], residual[None])


def other_side(cur, sent):
    top = cur.shape[0] - REACH
    low_first = (lax.axis_index("slab") % 4) // 2 == 0
    outer = jnp.where(low_first, cur[:REACH], cur[top:])
    return jnp.concatenate([outer, sent[REACH:]], axis=0)


def solution(mesh):
    in_specs = (
        P("particle", "slab", None, None),
        P("particle", "slab", None, None),
        P("particle", "slab", None, None),
        P("particle", "slab", None, None),
        P("particle", "slab", None, None),
        P("particle"),
        P("particle"),
        P(),
        P(),
        P(),
    )
    out_specs = (P("particle", "slab", None, None), P("particle", None, None))
    return jax.shard_map(
        on_device, mesh=mesh, in_specs=in_specs, out_specs=out_specs, check_vma=False
    )
```

```python
import jax
import jax.numpy as jnp
from jax import lax
from jax.experimental import pallas as pl
from jax.experimental.pallas import tpu as pltpu
from jax.sharding import PartitionSpec as P


STENCIL_WEIGHTS = (-205.0 / 72.0, 8.0 / 5.0, -1.0 / 5.0, 8.0 / 315.0, -1.0 / 560.0)
COURANT_FACTOR = 0.1
REACH = 4
PITCH = 32
HIGHEST = lax.Precision.HIGHEST


def resident(block):
    return pltpu.with_memory_space_constraint(block, pltpu.MemorySpace.VMEM)


def is_fast(slabs, count):
    return slabs == 4 and count == 8


def swap(block, axis, pairs):
    both = [(a, b) for a, b in pairs] + [(b, a) for a, b in pairs]
    return lax.ppermute(block, axis, both)


def twice(model):
    flat = model.reshape(model.shape[0] * model.shape[1], model.shape[2])
    return jnp.concatenate([flat, flat], axis=1)


def pack_kernel(prev, cur, near, far, vel, to_one, to_two, to_far):
    width = prev.shape[0]
    place = lax.axis_index("slab")
    odd = place % 2
    top = width - REACH
    model = twice(vel[...]).reshape(-1, prev.shape[1], prev.shape[2])
    for ref, low in ((to_one, odd), (to_two, 1 - odd)):
        ref[0:width] = prev[...]
        ref[width : 2 * width] = cur[...]
        ref[2 * width : 3 * width] = near[...]
        ref[3 * width : 3 * width + REACH] = far[pl.ds((1 - low) * top, REACH)]
        ref[3 * width + REACH :] = model
    to_far[0:REACH] = cur[pl.ds((1 - (place % 4) // 2) * top, REACH)]
    to_far[REACH:] = model


def split3(values):
    high = values.astype(jnp.bfloat16)
    rest = values - high.astype(jnp.float32)
    middle = rest.astype(jnp.bfloat16)
    low = (rest - middle.astype(jnp.float32)).astype(jnp.bfloat16)
    return (high, middle, low)


def wave_kernel(
    src_cell, src_step, wavelet, prev, cur, far, near, vel, rec, obs, one, two, *rest, n_far, with_models
):
    fars = rest[:n_far]
    rest = rest[n_far:]
    if with_models:
        ends, rest = rest[0], rest[1:]
    pay, samples = rest[:2]
    cur_s, prev_s, near_s, far_s, first_s, sec_s, two_s, vel_s, c2_s, img_s = rest[2:]
    width, size_y, size_z = prev.shape
    half = width // 2
    coarse_y = size_y // 2
    place = lax.axis_index("slab")
    odd = place % 2
    f32 = jnp.float32
    data = pl.ds(8, size_y)
    for ref in (cur_s, first_s, near_s, two_s):
        ref[:, 0:8, :] = jnp.zeros((ref.shape[0], 8, size_z), f32)
        ref[:, 8 + size_y : PITCH, :] = jnp.zeros((ref.shape[0], PITCH - 8 - size_y, size_z), f32)
    wide = 2 * REACH
    cur_s[wide + REACH : wide + REACH + width, data, :] = cur[...]
    prev_s[wide : wide + width] = prev[...]
    near_s[wide : wide + width, data, :] = near[...]
    far_s[REACH : REACH + width] = far[...]
    own_vel = twice(vel[...])
    rows = half * coarse_y
    vel_s[rows : 2 * rows] = own_vel

    def put(block, high):
        base = high * (width + wide)
        prev_s[pl.ds(base, width)] = block[0:width]
        cur_s[pl.ds(base + REACH, width), data, :] = block[width : 2 * width]
        near_s[pl.ds(base, width), data, :] = block[2 * width : 3 * width]
        far_s[pl.ds(high * (width + REACH), REACH)] = block[3 * width : 3 * width + REACH]
        model = block[3 * width + REACH :].reshape(rows, size_z)
        vel_s[pl.ds(high * 2 * rows, rows)] = model
        return model

    model_one = put(one, 1 - odd)
    put(two, odd)
    far_high = 1 - (place % 4) // 2
    edge = 2 * wide + width + REACH
    models_far = []
    if n_far == 1:
        zero = jnp.zeros((REACH, size_y, size_z), f32)
        cur_s[pl.ds((1 - far_high) * edge, REACH), data, :] = zero
    for index, block in enumerate(fars):
        high = far_high if index == 0 else 1 - far_high
        cur_s[pl.ds(high * edge, REACH), data, :] = block[0:REACH]
        models_far.append(block[REACH:].reshape(rows, size_z))

    lane = lax.broadcasted_iota(jnp.int32, (1, size_z), 1)
    up_w = [None] + [jnp.where(lane >= k, STENCIL_WEIGHTS[k], 0.0).astype(f32) for k in range(1, 5)]
    down_w = [None] + [
        jnp.where(lane < size_z - k, STENCIL_WEIGHTS[k], 0.0).astype(f32) for k in range(1, 5)
    ]

    grid_r = lax.broadcasted_iota(jnp.int32, (size_z, size_z), 0)
    grid_c = lax.broadcasted_iota(jnp.int32, (size_z, size_z), 1)
    spread = jnp.where(grid_r == grid_c // 2, 1.0, 0.0).astype(f32)
    gather = jnp.where(grid_r // 2 == grid_c, 1.0, 0.0).astype(f32)
    scaled = COURANT_FACTOR * vel_s[...]
    fine_z = jnp.dot(scaled * scaled, spread, precision=HIGHEST, preferred_element_type=f32)
    count = fine_z.shape[0]
    c2_s[pl.ds(0, count, stride=2), :] = fine_z
    c2_s[pl.ds(1, count, stride=2), :] = fine_z

    step = 4

    def courant(layer):
        block = c2_s[layer // 2 * size_y : (layer + step) // 2 * size_y, :]
        block = block.reshape(step // 2, 1, size_y, size_z)
        return jnp.broadcast_to(block, (step // 2, 2, size_y, size_z)).reshape(step, size_y, size_z)

    def laplace(ref, at):
        centre = ref[at : at + step, data, :]
        flat = centre.reshape(step * size_y, size_z)
        total = (3.0 * STENCIL_WEIGHTS[0]) * centre
        for k in range(1, 5):
            pairs = (
                ref[at + k : at + k + step, data, :]
                + ref[at - k : at - k + step, data, :]
                + (ref[at : at + step, pl.ds(8 + k, size_y), :] + ref[at : at + step, pl.ds(8 - k, size_y), :])
            )
            along = pltpu.roll(flat, k, 1) * up_w[k] + pltpu.roll(flat, size_z - k, 1) * down_w[k]
            total = total + STENCIL_WEIGHTS[k] * pairs + along.reshape(step, size_y, size_z)
        return centre, total

    plane = size_y * size_z
    cell = src_cell[0]
    now = src_step[0]
    src_y = (cell % plane) // size_z
    src_z = cell % size_z

    def inject(ref, start, layers, offset, pulse):
        layer = cell // plane - (place * width - start)
        inside = (layer >= 0) & (layer < layers)
        layer = jnp.clip(layer, 0, layers - 1)
        value = jnp.where(inside, pulse, 0.0)
        at = pl.ds(offset + src_y, 1)
        ref[layer, at, :] = ref[layer, at, :] + jnp.where(lane == src_z, value, 0.0)

    for ch in range(0, width + 2 * wide, step):
        centre, total = laplace(cur_s, ch + REACH)
        first_s[ch : ch + step, data, :] = 2.0 * centre - prev_s[ch : ch + step] + courant(ch) * total
    inject(first_s, wide, width + 2 * wide, 8, wavelet[now + 1])
    for ch in range(0, width + 2 * REACH, step):
        centre, total = laplace(first_s, ch + REACH)
        older = cur_s[ch + wide : ch + wide + step, data, :]
        sec_s[ch : ch + step] = 2.0 * centre - older + courant(ch + REACH) * total
    inject(sec_s, REACH, width + 2 * REACH, 0, wavelet[now + 2])

    region = (width + 2 * REACH) * size_y
    cells = rec[...]
    row = (cells - (place * width - REACH) * plane) // size_z
    hot = row == lax.broadcasted_iota(jnp.int32, (region, cells.shape[1]), 0)
    hot = jnp.where(hot, 1.0, 0.0).astype(jnp.bfloat16)
    lanes = lax.broadcasted_iota(jnp.int32, (size_z, cells.shape[1]), 0) == cells % size_z
    lo = REACH * size_y
    hi = lo + width * size_y
    own = (row >= lo) & (row < hi)

    def read(field, marks):
        turned = field.T
        total = sum(jnp.dot(part, marks, preferred_element_type=f32) for part in split3(turned))
        return jnp.sum(jnp.where(lanes, total, 0.0), axis=0, keepdims=True)

    def spread_out(values, marks):
        placed = jnp.where(lanes, values, 0.0)
        dims = (((1,), (1,)), ((), ()))
        return sum(lax.dot_general(marks, part, dims, preferred_element_type=f32) for part in split3(placed))

    first_own = first_s[wide : wide + width, data, :].reshape(width * size_y, size_z)
    read_one = read(first_own, hot[lo:hi])
    read_two = read(sec_s[...].reshape(region, size_z), hot)
    samples[0:1, :] = read_one
    samples[1:2, :] = jnp.where(own, read_two, 0.0)
    add_one = spread_out(read_one - obs[0:1, :], hot[lo:hi])
    add_two = spread_out(read_two - obs[1:2, :], hot)

    for ch in range(0, width + 2 * REACH, step):
        centre, total = laplace(near_s, ch + REACH)
        extra = add_two[ch * size_y : (ch + step) * size_y].reshape(step, size_y, size_z)
        two_s[ch : ch + step, data, :] = (
            2.0 * centre - far_s[ch : ch + step] + courant(ch + REACH) * total + extra
        )
    for ch in range(0, width, step):
        centre, total = laplace(two_s, ch + REACH)
        extra = add_one[ch * size_y : (ch + step) * size_y].reshape(step, size_y, size_z)
        older = near_s[ch + wide : ch + wide + step, data, :]
        adj_one = 2.0 * centre - older + courant(ch + wide) * total + extra
        first = first_s[ch + wide : ch + wide + step, data, :]
        now_field = cur_s[ch + wide + REACH : ch + wide + REACH + step, data, :]
        bend_two = sec_s[ch + REACH : ch + REACH + step] - 2.0 * first + now_field
        bend_one = first - 2.0 * now_field + prev_s[ch + wide : ch + wide + step]
        image = centre * bend_two + adj_one * bend_one
        image = image.reshape(step // 2, 2, size_y, size_z)
        image = image[:, 0] + image[:, 1]
        img_s[ch // 2 * size_y : (ch + step) // 2 * size_y, :] = image.reshape(step // 2 * size_y, size_z)
    folded = img_s[pl.ds(0, rows, stride=2), :] + img_s[pl.ds(1, rows, stride=2), :]
    blocks = jnp.dot(folded, gather, precision=HIGHEST, preferred_element_type=f32)
    factor = 2.0 / (own_vel * own_vel * own_vel)
    left = lane < size_z // 2
    pay[0:rows, :] = jnp.where(left, factor * blocks, own_vel)
    if with_models:
        pay[rows : 2 * rows, :] = jnp.where(left, model_one, models_far[0])
        pay[2 * rows : 3 * rows, :] = jnp.where(left, twice(ends[...]), 0.0)


def mix_kernel(*refs, cells):
    count = len(refs) - 5
    pays = refs[:count]
    part, other, obs, update, misfit = refs[count:]
    f32 = jnp.float32
    misfit[...] = part[...] + other[...] - obs[...]
    rows = update.shape[0] * update.shape[1]
    lane = lax.broadcasted_iota(jnp.int32, (1, pays[0].shape[1]), 1)
    half = update.shape[2]
    model_lane = lane >= half
    total = pays[0].shape[0]
    mean = sum(ref[...] for ref in pays[1:]) + pays[0][...]
    mean = mean * (1.0 / count)

    def norm(diff):
        sq = diff * diff
        sq = jnp.concatenate([jnp.where(model_lane, sq[0:rows], 0.0), sq[rows:]], axis=0)
        sq = jnp.sum(sq.reshape(total // 8, 8, sq.shape[1]), axis=0)
        return jnp.sum(jnp.sum(sq, axis=1, keepdims=True), axis=0, keepdims=True)

    spread = jnp.zeros(mean.shape, f32)
    for ref in pays:
        diff = ref[...] - mean
        spread = spread + diff * diff
    spread = jnp.concatenate([jnp.where(model_lane, spread[0:rows], 0.0), spread[rows:]], axis=0)
    spread = jnp.sum(spread.reshape(total // 8, 8, spread.shape[1]), axis=0)
    spread = jnp.sum(jnp.sum(spread, axis=1, keepdims=True), axis=0, keepdims=True)
    band = (2.0 * count / (count * (count - 1))) * spread
    own = pays[0][...]
    mixed = own[0:rows]
    kernel_sum = jnp.ones((1, 1), f32)
    for ref in pays[1:]:
        weight = jnp.exp(-norm(ref[...] - own) / band)
        mixed = mixed + weight * ref[0:rows, :]
        kernel_sum = kernel_sum + weight
    coef = (2.0 * cells) / band
    pull = coef * (own[0:rows, half:] * kernel_sum - mixed[:, half:])
    update[...] = ((mixed[:, 0:half] + pull) * (1.0 / count)).reshape(update.shape)


def device_step(
    vel_coarse,
    fwd_prev,
    fwd_cur,
    adj_far,
    adj_near,
    src_cell,
    src_step,
    wavelet,
    rec_cell,
    observed,
):
    f32 = jnp.float32
    slabs = lax.axis_size("slab")
    count = lax.axis_size("particle")
    fast = is_fast(slabs, count)
    model = vel_coarse[0]
    prev, cur, far, near = fwd_prev[0], fwd_cur[0], adj_far[0], adj_near[0]
    width, size_y, size_z = prev.shape
    half, coarse_y, coarse_z = model.shape
    rows = half * coarse_y
    model_layers = rows // size_y
    near_layers = 3 * width + REACH + model_layers
    far_layers = REACH + model_layers
    in_vmem = pl.BlockSpec(memory_space=pltpu.VMEM)
    if fast:
        beside = swap(model, "slab", [(0, 1), (2, 3)])
    pack = pl.pallas_call(
        pack_kernel,
        out_shape=(
            pltpu.VMEM((near_layers, size_y, size_z), f32),
            pltpu.VMEM((near_layers, size_y, size_z), f32),
            pltpu.VMEM((far_layers, size_y, size_z), f32),
        ),
        in_specs=[in_vmem] * 5,
        out_specs=(in_vmem,) * 3,
        name="pack_halos",
    )
    to_one, to_two, to_far = pack(prev, cur, near, far, model)
    one = swap(to_one, "slab", [(i, i + 1) for i in range(0, slabs - 1, 2)])
    two = swap(to_two, "slab", [(i, i + 1) for i in range(1, slabs - 1, 2)])
    fars = [swap(to_far, "slab", [(i, i + 2) for i in range(slabs - 2) if i % 4 < 2])]
    others = [(i, i + 2) for i in range(slabs - 2) if i % 4 >= 2]
    if others:
        fars.append(swap(other_side(cur, to_far), "slab", others))
    extra = []
    if fast:
        extra = [swap(beside, "slab", [(0, 2), (1, 3)])]
    in_smem = pl.BlockSpec(memory_space=pltpu.SMEM)
    receivers = rec_cell.shape[0]
    wide = 2 * REACH
    pay_rows = 3 * rows if fast else rows
    pay, samples = pl.pallas_call(
        lambda *refs: wave_kernel(*refs, n_far=len(fars), with_models=fast),
        out_shape=(
            pltpu.VMEM((pay_rows, size_z), f32),
            pltpu.VMEM((2, receivers), f32),
        ),
        in_specs=[in_smem] * 3 + [in_vmem] * (9 + len(fars) + len(extra)),
        out_specs=(in_vmem, in_vmem),
        scratch_shapes=[
            pltpu.VMEM((width + 2 * (wide + REACH), PITCH, size_z), f32),
            pltpu.VMEM((width + 2 * wide, size_y, size_z), f32),
            pltpu.VMEM((width + 2 * wide, PITCH, size_z), f32),
            pltpu.VMEM((width + 2 * REACH, size_y, size_z), f32),
            pltpu.VMEM((width + 2 * wide, PITCH, size_z), f32),
            pltpu.VMEM((width + 2 * REACH, size_y, size_z), f32),
            pltpu.VMEM((width + 2 * REACH, PITCH, size_z), f32),
            pltpu.VMEM((3 * rows, size_z), f32),
            pltpu.VMEM((6 * rows, size_z), f32),
            pltpu.VMEM((2 * rows, size_z), f32),
        ],
        name="wave_steps",
    )(
        src_cell, src_step, wavelet, prev, cur, far, near, model, rec_cell[None], observed,
        *[resident(block) for block in (one, two, *fars, *extra)],
    )
    cells_coarse = rows * slabs * coarse_z
    if not fast:
        residual = lax.psum(samples, "slab") - observed
        gathered = lax.all_gather(pay, "particle", axis=0)
        models = gathered[:, :, coarse_z:]
        deltas = models[:, None] - models[None]
        dist = lax.psum(jnp.sum(deltas * deltas, axis=(2, 3)), "slab")
        band = jnp.sum(dist) / (count * (count - 1))
        row = lax.dynamic_index_in_dim(dist, lax.axis_index("particle"), 0, keepdims=False)
        weights = jnp.exp(-row / band)
        mixed = jnp.einsum("q,qrz->rz", weights, gathered, precision=HIGHEST)
        own = pay[:, coarse_z:]
        pull = (2.0 * cells_coarse / band) * (own * jnp.sum(weights) - mixed[:, coarse_z:])
        update = (mixed[:, :coarse_z] + pull) / count
        return (update.reshape(model.shape)[None], residual[None])

    blocks = {0: pay}
    for flip in (6, 4, 2):
        blocks[flip] = swap(pay, "particle", [(i, i ^ flip) for i in range(count) if i < i ^ flip])
    for flip in (0, 6, 4, 2):
        pairs = [(i, i ^ 1) for i in range(0, count, 2)]
        blocks[flip + 1] = swap(blocks[flip], "particle", pairs)
    part = samples + swap(samples, "slab", [(0, 1), (2, 3)])
    other = swap(part, "slab", [(0, 2), (1, 3)])
    update, residual = pl.pallas_call(
        lambda *refs: mix_kernel(*refs, cells=cells_coarse),
        out_shape=(
            jax.ShapeDtypeStruct(model.shape, f32),
            jax.ShapeDtypeStruct((2, receivers), f32),
        ),
        in_specs=[in_vmem] * 11,
        out_specs=(in_vmem, in_vmem),
        name="mix_particles",
    )(*[resident(blocks[i]) for i in range(count)], resident(part), resident(other), observed)
    return (update[None], residual[None])


def other_side(cur, sent):
    top = cur.shape[0] - REACH
    low_first = (lax.axis_index("slab") % 4) // 2 == 0
    outer = jnp.where(low_first, cur[:REACH], cur[top:])
    return jnp.concatenate([outer, sent[REACH:]], axis=0)


def solution(mesh):
    in_specs = (
        P("particle", "slab", None, None),
        P("particle", "slab", None, None),
        P("particle", "slab", None, None),
        P("particle", "slab", None, None),
        P("particle", "slab", None, None),
        P("particle"),
        P("particle"),
        P(),
        P(),
        P(),
    )
    out_specs = (P("particle", "slab", None, None), P("particle", None, None))
    return jax.shard_map(
        device_step, mesh=mesh, in_specs=in_specs, out_specs=out_specs, check_vma=False
    )
```

```python
import jax
import jax.numpy as jnp
from jax import lax
from jax.experimental import pallas as pl
from jax.experimental.pallas import tpu as pltpu
from jax.sharding import PartitionSpec as P


STENCIL_WEIGHTS = (-205.0 / 72.0, 8.0 / 5.0, -1.0 / 5.0, 8.0 / 315.0, -1.0 / 560.0)
COURANT_FACTOR = 0.1
REACH = 4
STEP = 4
PITCH = 32
HIGHEST = lax.Precision.HIGHEST


def resident(block):
    return pltpu.with_memory_space_constraint(block, pltpu.MemorySpace.VMEM)


def is_fast(slabs, count):
    return slabs == 4 and count == 8


def swap(block, axis, pairs):
    both = [(a, b) for a, b in pairs] + [(b, a) for a, b in pairs]
    return lax.ppermute(block, axis, both)


def twice(model):
    flat = model.reshape(model.shape[0] * model.shape[1], model.shape[2])
    return jnp.concatenate([flat, flat], axis=1)


def lane_weights(size_z):
    lane = lax.broadcasted_iota(jnp.int32, (1, size_z), 1)
    below = [jnp.where(lane >= k, w, 0.0).astype(jnp.float32) for k, w in enumerate(STENCIL_WEIGHTS)]
    above = [
        jnp.where(lane < size_z - k, w, 0.0).astype(jnp.float32) for k, w in enumerate(STENCIL_WEIGHTS)
    ]
    return below, above


def clear_margins(ref, size_y):
    ref[:, 0:8, :] = jnp.zeros((ref.shape[0], 8, ref.shape[2]), jnp.float32)
    rest = PITCH - 8 - size_y
    ref[:, 8 + size_y : PITCH, :] = jnp.zeros((ref.shape[0], rest, ref.shape[2]), jnp.float32)


def laplace(ref, at, size_y, weights):
    below, above = weights
    data = pl.ds(8, size_y)
    size_z = ref.shape[2]
    centre = ref[at : at + STEP, data, :]
    flat = centre.reshape(STEP * size_y, size_z)
    total = (3.0 * STENCIL_WEIGHTS[0]) * centre
    for k in range(1, 5):
        pairs = (
            ref[at + k : at + k + STEP, data, :]
            + ref[at - k : at - k + STEP, data, :]
            + (ref[at : at + STEP, pl.ds(8 + k, size_y), :] + ref[at : at + STEP, pl.ds(8 - k, size_y), :])
        )
        along = pltpu.roll(flat, k, 1) * below[k] + pltpu.roll(flat, size_z - k, 1) * above[k]
        total = total + STENCIL_WEIGHTS[k] * pairs + along.reshape(STEP, size_y, size_z)
    return centre, total


def fill_courant(c2_ref, packed, size_z):
    grid_r = lax.broadcasted_iota(jnp.int32, (size_z, 2 * size_z), 0)
    grid_c = lax.broadcasted_iota(jnp.int32, (size_z, 2 * size_z), 1)
    spread = jnp.where(grid_r == grid_c // 2, 1.0, 0.0).astype(jnp.float32)
    scaled = COURANT_FACTOR * packed
    fine = jnp.dot(scaled * scaled, spread, precision=HIGHEST, preferred_element_type=jnp.float32)
    count = packed.shape[0]
    part = count if count < 16 else 16
    for start in range(0, count, part):
        for side in range(2):
            rows = fine[start : start + part, side * size_z : (side + 1) * size_z]
            base = 4 * start + 2 * part * side
            c2_ref[pl.ds(base, part, stride=2), :] = rows
            c2_ref[pl.ds(base + 1, part, stride=2), :] = rows


def courant(c2_ref, layer, count, size_y):
    size_z = c2_ref.shape[1]
    block = c2_ref[layer // 2 * size_y : (layer + count) // 2 * size_y, :]
    block = block.reshape(count // 2, 1, size_y, size_z)
    return jnp.broadcast_to(block, (count // 2, 2, size_y, size_z)).reshape(count, size_y, size_z)


def start_kernel(
    prev, cur, far, near, vel, to_one, to_two, to_far, packed, near_part, cur_s, near_s, c2_s
):
    width, size_y, size_z = prev.shape
    place = lax.axis_index("slab")
    odd = place % 2
    top = width - REACH
    data = pl.ds(8, size_y)
    weights = lane_weights(size_z)
    for ref, field in ((cur_s, cur), (near_s, near)):
        clear_margins(ref, size_y)
        for start in (0, REACH + width):
            ref[start : start + REACH, data, :] = jnp.zeros((REACH, size_y, size_z), jnp.float32)
        ref[REACH : REACH + width, data, :] = field[...]
    rows = vel.shape[0] * vel.shape[1]
    flat = vel[...].reshape(rows, vel.shape[2])
    packed[...] = jnp.concatenate([flat[: rows // 2], flat[rows // 2 :]], axis=1)
    fill_courant(c2_s, packed[...], size_z)
    for ch in range(0, width, STEP):
        factor = courant(c2_s, ch, STEP, size_y)
        centre, total = laplace(cur_s, ch + REACH, size_y, weights)
        part = 2.0 * centre - prev[ch : ch + STEP] + factor * total
        to_one[ch : ch + STEP] = part
        to_two[ch : ch + STEP] = part
        centre, total = laplace(near_s, ch + REACH, size_y, weights)
        near_part[ch : ch + STEP] = 2.0 * centre - far[ch : ch + STEP] + factor * total
    for ref, low in ((to_one, odd), (to_two, 1 - odd)):
        outer = pl.ds((1 - low) * top, REACH)
        ref[width : width + REACH] = cur[outer]
        ref[width + REACH : width + 2 * REACH] = near_part[outer]
        ref[width + 2 * REACH : width + 3 * REACH] = near[outer]
    to_far[0:REACH] = cur[pl.ds((1 - (place % 4) // 2) * top, REACH)]
    to_far[REACH:] = packed[...].reshape(to_far.shape[0] - REACH, size_y, size_z)


def split3(values):
    high = values.astype(jnp.bfloat16)
    rest = values - high.astype(jnp.float32)
    middle = rest.astype(jnp.bfloat16)
    low = (rest - middle.astype(jnp.float32)).astype(jnp.bfloat16)
    return (high, middle, low)


def wave_kernel(
    src_cell, src_step, wavelet, prev, cur, near, vel, rec, obs, own_part, near_part, packed,
    one, two, model_one, model_two, *rest, n_far, with_models
):
    fars = rest[:n_far]
    pay, samples = rest[n_far : n_far + 2]
    cur_s, near_s, hop_s, first_s, sec_s, two_s, vel_s, c2_s, img_s = rest[n_far + 2 :]
    width, size_y, size_z = prev.shape
    rows = vel.shape[0] * vel.shape[1]
    place = lax.axis_index("slab")
    odd = place % 2
    f32 = jnp.float32
    data = pl.ds(8, size_y)
    lane = lax.broadcasted_iota(jnp.int32, (1, size_z), 1)
    weights = lane_weights(size_z)
    wide = 2 * REACH
    clear_margins(first_s, size_y)
    clear_margins(two_s, size_y)
    cur_s[REACH : REACH + width] = cur[...]
    near_s[REACH : REACH + width] = near[...]
    first_s[wide : wide + width, data, :] = own_part[0:width]
    two_s[REACH : REACH + width, data, :] = near_part[...]
    short = packed.shape[0]
    vel_s[short : 2 * short] = packed[...]

    def put(block, model, high):
        outer = pl.ds(high * (width + REACH), REACH)
        first_s[pl.ds(high * (width + wide), width), data, :] = block[0:width]
        cur_s[outer] = block[width : width + REACH]
        two_s[outer, data, :] = block[width + REACH : width + 2 * REACH]
        near_s[outer] = block[width + 2 * REACH : width + 3 * REACH]
        vel_s[pl.ds(high * 2 * short, short)] = model

    put(one, model_one[...], 1 - odd)
    inner = (place > 0) & (place < lax.axis_size("slab") - 1)
    put(two, jnp.where(inner, model_two[...], 0.0), odd)
    far_high = 1 - (place % 4) // 2
    if n_far == 1:
        hop_s[pl.ds((1 - far_high) * REACH, REACH)] = jnp.zeros((REACH, size_y, size_z), f32)
    for index, block in enumerate(fars):
        high = far_high if index == 0 else 1 - far_high
        hop_s[pl.ds(high * REACH, REACH)] = block[0:REACH]
    fill_courant(c2_s, vel_s[...], size_z)

    def crossing(sources, depth):
        terms = [STENCIL_WEIGHTS[depth + 1 + j] * sources[j] for j in range(REACH - depth)]
        return sum(terms[1:], terms[0])

    def cross(ref, at, shift, upward, read):
        for depth in range(REACH):
            layer = at + depth if upward else at - 1 - depth
            sources = [read(j) for j in range(REACH - depth)]
            fine = (layer + shift) // 2 * size_y
            factor = c2_s[fine : fine + size_y, :]
            ref[layer, data, :] = ref[layer, data, :] + factor * crossing(sources, depth)

    cross(first_s, 0, 0, True, lambda j: hop_s[REACH - 1 - j])
    cross(first_s, wide, 0, False, lambda j: cur_s[REACH + j])
    cross(first_s, wide, 0, True, lambda j: cur_s[REACH - 1 - j])
    cross(first_s, wide + width, 0, False, lambda j: cur_s[REACH + width + j])
    cross(first_s, wide + width, 0, True, lambda j: cur_s[REACH + width - 1 - j])
    cross(first_s, 2 * wide + width, 0, False, lambda j: hop_s[REACH + j])
    cross(two_s, REACH, REACH, False, lambda j: near_s[REACH + j])
    cross(two_s, REACH, REACH, True, lambda j: near_s[REACH - 1 - j])
    cross(two_s, REACH + width, REACH, False, lambda j: near_s[REACH + width + j])
    cross(two_s, REACH + width, REACH, True, lambda j: near_s[REACH + width - 1 - j])

    plane = size_y * size_z
    cell = src_cell[0]
    now = src_step[0]
    src_y = (cell % plane) // size_z
    src_z = cell % size_z

    def inject(ref, start, layers, offset, pulse):
        layer = cell // plane - (place * width - start)
        inside = (layer >= 0) & (layer < layers)
        layer = jnp.clip(layer, 0, layers - 1)
        value = jnp.where(inside, pulse, 0.0)
        at = pl.ds(offset + src_y, 1)
        ref[layer, at, :] = ref[layer, at, :] + jnp.where(lane == src_z, value, 0.0)

    inject(first_s, wide, width + 2 * wide, 8, wavelet[now + 1])
    for ch in range(0, width + 2 * REACH, STEP):
        centre, total = laplace(first_s, ch + REACH, size_y, weights)
        factor = courant(c2_s, ch + REACH, STEP, size_y)
        sec_s[ch : ch + STEP] = 2.0 * centre - cur_s[ch : ch + STEP] + factor * total
    inject(sec_s, REACH, width + 2 * REACH, 0, wavelet[now + 2])

    region = (width + 2 * REACH) * size_y
    cells = rec[...]
    row = (cells - (place * width - REACH) * plane) // size_z
    hot = row == lax.broadcasted_iota(jnp.int32, (region, cells.shape[1]), 0)
    hot = jnp.where(hot, 1.0, 0.0).astype(jnp.bfloat16)
    lanes = lax.broadcasted_iota(jnp.int32, (size_z, cells.shape[1]), 0) == cells % size_z
    lo = REACH * size_y
    hi = lo + width * size_y
    own = (row >= lo) & (row < hi)

    def read(field, marks):
        turned = field.T
        total = sum(jnp.dot(part, marks, preferred_element_type=f32) for part in split3(turned))
        return jnp.sum(jnp.where(lanes, total, 0.0), axis=0, keepdims=True)

    def spread_out(values, marks):
        placed = jnp.where(lanes, values, 0.0)
        dims = (((1,), (1,)), ((), ()))
        return sum(lax.dot_general(marks, part, dims, preferred_element_type=f32) for part in split3(placed))

    first_own = first_s[wide : wide + width, data, :].reshape(width * size_y, size_z)
    read_one = read(first_own, hot[lo:hi])
    read_two = read(sec_s[...].reshape(region, size_z), hot)
    samples[0:1, :] = read_one
    samples[1:2, :] = jnp.where(own, read_two, 0.0)
    add_one = spread_out(read_one - obs[0:1, :], hot[lo:hi])
    add_two = spread_out(read_two - obs[1:2, :], hot)

    for ch in range(0, width + 2 * REACH, STEP):
        extra = add_two[ch * size_y : (ch + STEP) * size_y].reshape(STEP, size_y, size_z)
        two_s[ch : ch + STEP, data, :] = two_s[ch : ch + STEP, data, :] + extra
    for ch in range(0, width, STEP):
        centre, total = laplace(two_s, ch + REACH, size_y, weights)
        extra = add_one[ch * size_y : (ch + STEP) * size_y].reshape(STEP, size_y, size_z)
        factor = courant(c2_s, ch + wide, STEP, size_y)
        adj_one = 2.0 * centre - near[ch : ch + STEP] + factor * total + extra
        first = first_s[ch + wide : ch + wide + STEP, data, :]
        now_field = cur[ch : ch + STEP]
        bend_two = sec_s[ch + REACH : ch + REACH + STEP] - 2.0 * first + now_field
        bend_one = first - 2.0 * now_field + prev[ch : ch + STEP]
        image = centre * bend_two + adj_one * bend_one
        image = image.reshape(STEP // 2, 2, size_y, size_z)
        image = image[:, 0] + image[:, 1]
        img_s[ch // 2 * size_y : (ch + STEP) // 2 * size_y, :] = image.reshape(STEP // 2 * size_y, size_z)
    grid_r = lax.broadcasted_iota(jnp.int32, (size_z, size_z), 0)
    grid_c = lax.broadcasted_iota(jnp.int32, (size_z, size_z), 1)
    gather = jnp.where(grid_r // 2 == grid_c, 1.0, 0.0).astype(f32)
    folded = img_s[pl.ds(0, rows, stride=2), :] + img_s[pl.ds(1, rows, stride=2), :]
    blocks = jnp.dot(folded, gather, precision=HIGHEST, preferred_element_type=f32)
    own_vel = twice(vel[...])
    factor = 2.0 / (own_vel * own_vel * own_vel)
    pay[0:rows, :] = jnp.where(lane < size_z // 2, factor * blocks, own_vel)
    if with_models:
        pay[rows : rows + short, :] = model_one[...]
        pay[rows + short : rows + 2 * short, :] = model_two[...]
        pay[rows + 2 * short :, :] = fars[0][REACH:].reshape(short, size_z)


def mix_kernel(*refs, cells):
    count = len(refs) - 5
    pays = refs[:count]
    part, other, obs, update, misfit = refs[count:]
    f32 = jnp.float32
    misfit[...] = part[...] + other[...] - obs[...]
    rows = update.shape[0] * update.shape[1]
    lane = lax.broadcasted_iota(jnp.int32, (1, pays[0].shape[1]), 1)
    half = update.shape[2]
    model_lane = lane >= half
    total = pays[0].shape[0]
    mean = sum(ref[...] for ref in pays[1:]) + pays[0][...]
    mean = mean * (1.0 / count)

    def norm(diff):
        sq = diff * diff
        sq = jnp.concatenate([jnp.where(model_lane, sq[0:rows], 0.0), sq[rows:]], axis=0)
        sq = jnp.sum(sq.reshape(total // 8, 8, sq.shape[1]), axis=0)
        return jnp.sum(jnp.sum(sq, axis=1, keepdims=True), axis=0, keepdims=True)

    spread = jnp.zeros(mean.shape, f32)
    for ref in pays:
        diff = ref[...] - mean
        spread = spread + diff * diff
    spread = jnp.concatenate([jnp.where(model_lane, spread[0:rows], 0.0), spread[rows:]], axis=0)
    spread = jnp.sum(spread.reshape(total // 8, 8, spread.shape[1]), axis=0)
    spread = jnp.sum(jnp.sum(spread, axis=1, keepdims=True), axis=0, keepdims=True)
    band = (2.0 * count / (count * (count - 1))) * spread
    own = pays[0][...]
    mixed = own[0:rows]
    kernel_sum = jnp.ones((1, 1), f32)
    for ref in pays[1:]:
        weight = jnp.exp(-norm(ref[...] - own) / band)
        mixed = mixed + weight * ref[0:rows, :]
        kernel_sum = kernel_sum + weight
    coef = (2.0 * cells) / band
    pull = coef * (own[0:rows, half:] * kernel_sum - mixed[:, half:])
    update[...] = ((mixed[:, 0:half] + pull) * (1.0 / count)).reshape(update.shape)


def device_step(
    vel_coarse,
    fwd_prev,
    fwd_cur,
    adj_far,
    adj_near,
    src_cell,
    src_step,
    wavelet,
    rec_cell,
    observed,
):
    f32 = jnp.float32
    slabs = lax.axis_size("slab")
    count = lax.axis_size("particle")
    fast = is_fast(slabs, count)
    model = vel_coarse[0]
    prev, cur, far, near = fwd_prev[0], fwd_cur[0], adj_far[0], adj_near[0]
    width, size_y, size_z = prev.shape
    half, coarse_y, coarse_z = model.shape
    rows = half * coarse_y
    short = rows // 2
    near_layers = width + 3 * REACH
    far_layers = REACH + short // size_y
    in_vmem = pl.BlockSpec(memory_space=pltpu.VMEM)
    in_smem = pl.BlockSpec(memory_space=pltpu.SMEM)
    padded = pltpu.VMEM((width + 2 * REACH, PITCH, size_z), f32)
    start = pl.pallas_call(
        start_kernel,
        out_shape=(
            pltpu.VMEM((near_layers, size_y, size_z), f32),
            pltpu.VMEM((near_layers, size_y, size_z), f32),
            pltpu.VMEM((far_layers, size_y, size_z), f32),
            pltpu.VMEM((short, size_z), f32),
            pltpu.VMEM((width, size_y, size_z), f32),
        ),
        in_specs=[in_vmem] * 5,
        out_specs=(in_vmem,) * 5,
        scratch_shapes=[padded, padded, pltpu.VMEM((2 * rows, size_z), f32)],
        name="start_steps",
    )
    to_one, to_two, to_far, packed, near_part = start(prev, cur, far, near, model)
    even = [(i, i + 1) for i in range(0, slabs - 1, 2)]
    model_one = swap(packed, "slab", even)
    one = swap(to_one, "slab", even)
    uneven = [(i, i + 1) for i in range(1, slabs - 1, 2)]
    two = swap(to_two, "slab", uneven)
    fars = [swap(to_far, "slab", [(i, i + 2) for i in range(slabs - 2) if i % 4 < 2])]
    if fast:
        model_two = swap(model_one, "slab", [(0, 2), (1, 3)])
    else:
        model_two = swap(packed, "slab", uneven)
        others = [(i, i + 2) for i in range(slabs - 2) if i % 4 >= 2]
        if others:
            fars.append(swap(other_side(cur, to_far), "slab", others))
    receivers = rec_cell.shape[0]
    wide = 2 * REACH
    pay_rows = rows + 3 * short if fast else rows
    operands = (
        prev, cur, near, model, rec_cell[None], observed, to_one, near_part, packed,
        one, two, model_one, model_two, *fars,
    )
    plain = pltpu.VMEM((width + 2 * REACH, size_y, size_z), f32)
    pay, samples = pl.pallas_call(
        lambda *refs: wave_kernel(*refs, n_far=len(fars), with_models=fast),
        out_shape=(
            pltpu.VMEM((pay_rows, size_z), f32),
            pltpu.VMEM((2, receivers), f32),
        ),
        in_specs=[in_smem] * 3 + [in_vmem] * len(operands),
        out_specs=(in_vmem, in_vmem),
        scratch_shapes=[
            plain,
            plain,
            pltpu.VMEM((2 * REACH, size_y, size_z), f32),
            pltpu.VMEM((width + 2 * wide, PITCH, size_z), f32),
            plain,
            padded,
            pltpu.VMEM((3 * short, size_z), f32),
            pltpu.VMEM((6 * rows, size_z), f32),
            pltpu.VMEM((2 * rows, size_z), f32),
        ],
        name="wave_steps",
    )(src_cell, src_step, wavelet, *[resident(block) for block in operands])
    cells_coarse = rows * slabs * coarse_z
    if not fast:
        residual = lax.psum(samples, "slab") - observed
        gathered = lax.all_gather(pay, "particle", axis=0)
        models = gathered[:, :, coarse_z:]
        deltas = models[:, None] - models[None]
        dist = lax.psum(jnp.sum(deltas * deltas, axis=(2, 3)), "slab")
        band = jnp.sum(dist) / (count * (count - 1))
        row = lax.dynamic_index_in_dim(dist, lax.axis_index("particle"), 0, keepdims=False)
        weights = jnp.exp(-row / band)
        mixed = jnp.einsum("q,qrz->rz", weights, gathered, precision=HIGHEST)
        own = pay[:, coarse_z:]
        pull = (2.0 * cells_coarse / band) * (own * jnp.sum(weights) - mixed[:, coarse_z:])
        update = (mixed[:, :coarse_z] + pull) / count
        return (update.reshape(model.shape)[None], residual[None])

    blocks = {0: pay}
    for flip in (6, 4, 2):
        blocks[flip] = swap(pay, "particle", [(i, i ^ flip) for i in range(count) if i < i ^ flip])
    for flip in (0, 6, 4, 2):
        pairs = [(i, i ^ 1) for i in range(0, count, 2)]
        blocks[flip + 1] = swap(blocks[flip], "particle", pairs)
    part = samples + swap(samples, "slab", [(0, 1), (2, 3)])
    other = swap(part, "slab", [(0, 2), (1, 3)])
    update, residual = pl.pallas_call(
        lambda *refs: mix_kernel(*refs, cells=cells_coarse),
        out_shape=(
            jax.ShapeDtypeStruct(model.shape, f32),
            jax.ShapeDtypeStruct((2, receivers), f32),
        ),
        in_specs=[in_vmem] * 11,
        out_specs=(in_vmem, in_vmem),
        name="mix_particles",
    )(*[resident(blocks[i]) for i in range(count)], resident(part), resident(other), resident(observed))
    return (update[None], residual[None])


def other_side(cur, sent):
    top = cur.shape[0] - REACH
    low_first = (lax.axis_index("slab") % 4) // 2 == 0
    outer = jnp.where(low_first, cur[:REACH], cur[top:])
    return jnp.concatenate([outer, sent[REACH:]], axis=0)


def solution(mesh):
    in_specs = (
        P("particle", "slab", None, None),
        P("particle", "slab", None, None),
        P("particle", "slab", None, None),
        P("particle", "slab", None, None),
        P("particle", "slab", None, None),
        P("particle"),
        P("particle"),
        P(),
        P(),
        P(),
    )
    out_specs = (P("particle", "slab", None, None), P("particle", None, None))
    return jax.shard_map(
        device_step, mesh=mesh, in_specs=in_specs, out_specs=out_specs, check_vma=False
    )
```

```python
import jax
import jax.numpy as jnp
from jax import lax
from jax.experimental import pallas as pl
from jax.experimental.pallas import tpu as pltpu
from jax.sharding import PartitionSpec as P


STENCIL_WEIGHTS = (-205.0 / 72.0, 8.0 / 5.0, -1.0 / 5.0, 8.0 / 315.0, -1.0 / 560.0)
COURANT_FACTOR = 0.1
REACH = 4
STEP = 4
PITCH = 32
HIGHEST = lax.Precision.HIGHEST


def resident(block):
    return pltpu.with_memory_space_constraint(block, pltpu.MemorySpace.VMEM)


def is_fast(slabs, count):
    return slabs == 4 and count == 8


def swap(block, axis, pairs):
    both = [(a, b) for a, b in pairs] + [(b, a) for a, b in pairs]
    return lax.ppermute(block, axis, both)


def twice(model):
    flat = model.reshape(model.shape[0] * model.shape[1], model.shape[2])
    return jnp.concatenate([flat, flat], axis=1)


def lane_weights(size_z):
    lane = lax.broadcasted_iota(jnp.int32, (1, size_z), 1)
    below = [jnp.where(lane >= k, w, 0.0).astype(jnp.float32) for k, w in enumerate(STENCIL_WEIGHTS)]
    above = [
        jnp.where(lane < size_z - k, w, 0.0).astype(jnp.float32) for k, w in enumerate(STENCIL_WEIGHTS)
    ]
    return below, above


def clear_margins(ref, size_y):
    ref[:, 0:8, :] = jnp.zeros((ref.shape[0], 8, ref.shape[2]), jnp.float32)
    rest = PITCH - 8 - size_y
    ref[:, 8 + size_y : PITCH, :] = jnp.zeros((ref.shape[0], rest, ref.shape[2]), jnp.float32)


def laplace(ref, at, size_y, weights):
    below, above = weights
    data = pl.ds(8, size_y)
    size_z = ref.shape[2]
    centre = ref[at : at + STEP, data, :]
    flat = centre.reshape(STEP * size_y, size_z)
    total = (3.0 * STENCIL_WEIGHTS[0]) * centre
    for k in range(1, 5):
        pairs = (
            ref[at + k : at + k + STEP, data, :]
            + ref[at - k : at - k + STEP, data, :]
            + (ref[at : at + STEP, pl.ds(8 + k, size_y), :] + ref[at : at + STEP, pl.ds(8 - k, size_y), :])
        )
        along = pltpu.roll(flat, k, 1) * below[k] + pltpu.roll(flat, size_z - k, 1) * above[k]
        total = total + STENCIL_WEIGHTS[k] * pairs + along.reshape(STEP, size_y, size_z)
    return centre, total


def fill_courant(c2_ref, packed, size_z):
    grid_r = lax.broadcasted_iota(jnp.int32, (size_z, 2 * size_z), 0)
    grid_c = lax.broadcasted_iota(jnp.int32, (size_z, 2 * size_z), 1)
    spread = jnp.where(grid_r == grid_c // 2, 1.0, 0.0).astype(jnp.float32)
    scaled = COURANT_FACTOR * packed
    fine = jnp.dot(scaled * scaled, spread, precision=HIGHEST, preferred_element_type=jnp.float32)
    count = packed.shape[0]
    part = count if count < 16 else 16
    for start in range(0, count, part):
        for side in range(2):
            rows = fine[start : start + part, side * size_z : (side + 1) * size_z]
            base = 4 * start + 2 * part * side
            c2_ref[pl.ds(base, part, stride=2), :] = rows
            c2_ref[pl.ds(base + 1, part, stride=2), :] = rows


def courant(c2_ref, layer, count, size_y):
    size_z = c2_ref.shape[1]
    block = c2_ref[layer // 2 * size_y : (layer + count) // 2 * size_y, :]
    block = block.reshape(count // 2, 1, size_y, size_z)
    return jnp.broadcast_to(block, (count // 2, 2, size_y, size_z)).reshape(count, size_y, size_z)


def split3(values):
    high = values.astype(jnp.bfloat16)
    rest = values - high.astype(jnp.float32)
    middle = rest.astype(jnp.bfloat16)
    low = (rest - middle.astype(jnp.float32)).astype(jnp.bfloat16)
    return (high, middle, low)


def start_kernel(
    prev, cur, far, near, vel, rec, obs, wavelet, to_one, to_two, to_far, packed,
    own_part, near_part, lanes_out, rec_out, wavelet_out, obs_out, cur_s, near_s, c2_s
):
    width, size_y, size_z = prev.shape
    f32 = jnp.float32
    place = lax.axis_index("slab")
    odd = place % 2
    top = width - REACH
    plane = size_y * size_z
    data = pl.ds(8, size_y)
    weights = lane_weights(size_z)
    for ref, field in ((cur_s, cur), (near_s, near)):
        clear_margins(ref, size_y)
        for start in (0, REACH + width):
            ref[start : start + REACH, data, :] = jnp.zeros((REACH, size_y, size_z), f32)
        ref[REACH : REACH + width, data, :] = field[...]
    rows = vel.shape[0] * vel.shape[1]
    flat = vel[...].reshape(rows, vel.shape[2])
    packed[...] = jnp.concatenate([flat[: rows // 2], flat[rows // 2 :]], axis=1)
    fill_courant(c2_s, packed[...], size_z)
    rec_out[...] = rec[...]
    obs_out[...] = obs[...]
    wavelet_out[...] = wavelet[...]
    for ch in range(0, width, STEP):
        factor = courant(c2_s, ch, STEP, size_y)
        centre, total = laplace(cur_s, ch + REACH, size_y, weights)
        part = 2.0 * centre - prev[ch : ch + STEP] + factor * total
        own_part[ch : ch + STEP] = part
        centre, total = laplace(near_s, ch + REACH, size_y, weights)
        near_part[ch : ch + STEP] = 2.0 * centre - far[ch : ch + STEP] + factor * total

    cells = rec[...]
    count = cells.shape[1]
    lanes = lax.broadcasted_iota(jnp.int32, (size_z, count), 0) == cells % size_z
    lanes = jnp.where(lanes, 1.0, 0.0).astype(jnp.bfloat16)
    lanes_out[...] = lanes
    in_row = lax.broadcasted_iota(jnp.int32, (size_y, count), 0) == cells % plane // size_z
    fields = jnp.concatenate(
        [own_part[...].reshape(width * size_y, size_z), c2_s[...], cur[...].reshape(width * size_y, size_z)],
        axis=0,
    )
    picked = sum(jnp.dot(part, lanes, preferred_element_type=f32) for part in split3(fields))
    picked = picked.reshape(-1, size_y, count)
    picked = jnp.sum(jnp.where(in_row[None], picked, 0.0), axis=1)
    half = width // 2
    columns = picked[width + half :]
    for ref, low in ((to_one, odd), (to_two, 1 - odd)):
        outer = pl.ds((1 - low) * top, REACH)
        ref[0:REACH] = own_part[outer]
        ref[REACH : 2 * REACH] = cur[outer]
        ref[2 * REACH : 3 * REACH] = near_part[outer]
        ref[3 * REACH : 4 * REACH] = near[outer]
        deep = jnp.where(low == 0, picked[0:REACH], picked[top:width])
        block = jnp.concatenate([deep, picked[width : width + half]], axis=0)
        ref[4 * REACH :] = fold(block, size_y, size_z)
    to_far[0:1] = fold(columns, size_y, size_z)
    to_far[1:] = packed[...].reshape(to_far.shape[0] - 1, size_y, size_z)


def fold(block, size_y, size_z):
    pieces = [block[:, at : at + size_z] for at in range(0, block.shape[1], size_z)]
    return jnp.concatenate(pieces, axis=0).reshape(-1, size_y, size_z)


def unfold(layer, count):
    flat = layer.reshape(-1, layer.shape[-1])
    rows = flat.shape[0] * flat.shape[1] // count
    return jnp.concatenate([flat[at : at + rows] for at in range(0, flat.shape[0], rows)], axis=1)


def wave_kernel(
    src_cell, src_step, prev, cur, near, vel, own_part, near_part, packed, lanes_in, rec, wavelet, obs,
    one, two, model_one, model_two, *rest, n_far, with_models
):
    fars = rest[:n_far]
    pay, samples = rest[n_far : n_far + 2]
    cur_s, near_s, first_s, sec_s, two_s, vel_s, c2_s, img_s = rest[n_far + 2 :]
    width, size_y, size_z = prev.shape
    rows = vel.shape[0] * vel.shape[1]
    receivers = rec.shape[1]
    plane = size_y * size_z
    place = lax.axis_index("slab")
    odd = place % 2
    f32 = jnp.float32
    data = pl.ds(8, size_y)
    lane = lax.broadcasted_iota(jnp.int32, (1, size_z), 1)
    weights = lane_weights(size_z)
    wide = 2 * REACH
    clear_margins(first_s, size_y)
    clear_margins(two_s, size_y)
    for start in (0, width + wide + REACH):
        first_s[start : start + REACH, data, :] = jnp.zeros((REACH, size_y, size_z), f32)
    cur_s[REACH : REACH + width] = cur[...]
    near_s[REACH : REACH + width] = near[...]
    first_s[wide : wide + width, data, :] = own_part[...]
    two_s[REACH : REACH + width, data, :] = near_part[...]
    short = packed.shape[0]
    vel_s[short : 2 * short] = packed[...]

    cell = src_cell[0]
    now = src_step[0]
    src_layer = cell // plane - place * width
    same_column = rec[...] % plane == cell % plane

    ticks = lax.broadcasted_iota(jnp.int32, wavelet.shape, 1)

    def pulse(ahead):
        return jnp.sum(jnp.where(ticks == now + ahead, wavelet[...], 0.0), axis=1, keepdims=True)

    pulse_one = pulse(1)

    def inject(ref, start, layers, offset, pulse):
        layer = src_layer + start
        inside = (layer >= 0) & (layer < layers)
        layer = jnp.clip(layer, 0, layers - 1)
        value = jnp.where(inside, pulse, 0.0)
        at = pl.ds(offset + cell % plane // size_z, 1)
        ref[layer, at, :] = ref[layer, at, :] + jnp.where(lane == cell % size_z, value, 0.0)

    far_high = 1 - (place % 4) // 2
    hops = [unfold(block[0:1], receivers) for block in fars]

    def put(block, model, high):
        outer = pl.ds(high * (width + REACH), REACH)
        first_s[pl.ds(high * (width + REACH) + REACH, REACH), data, :] = block[0:REACH]
        cur_s[outer] = block[REACH : 2 * REACH]
        two_s[outer, data, :] = block[2 * REACH : 3 * REACH]
        near_s[outer] = block[3 * REACH : 4 * REACH]
        vel_s[pl.ds(high * 2 * short, short)] = model
        up = high == 1
        columns = unfold(block[4 * REACH :], receivers)
        half = columns.shape[0] - REACH
        deep = [jnp.where(up, columns[j : j + 1], columns[3 - j : 4 - j]) for j in range(REACH)]
        factor = [
            jnp.where(up, columns[REACH + m : REACH + m + 1], columns[REACH + half - 1 - m : REACH + half - m])
            for m in range(half)
        ]
        beyond = [jnp.zeros((1, receivers), f32)] * REACH
        for index, hop in enumerate(hops):
            side = far_high if index == 0 else 1 - far_high
            last = hop.shape[0] - 1
            for u in range(REACH):
                seen = jnp.where(up, hop[u : u + 1], hop[last - u : last - u + 1])
                beyond[u] = jnp.where(side == high, seen, beyond[u])
        src_depth = high * (src_layer - width) + (1 - high) * (-1 - src_layer)
        for j in range(REACH):
            source = jnp.where(src_depth == REACH + j, pulse_one, 0.0)
            deep[j] = deep[j] + jnp.where(same_column, source, 0.0)
            more = sum(STENCIL_WEIGHTS[4 + u - j] * beyond[u] for u in range(j + 1))
            deep[j] = deep[j] + factor[(REACH + j) // 2] * more
        return [
            factor[depth // 2] * sum(STENCIL_WEIGHTS[4 + j - depth] * deep[j] for j in range(depth + 1))
            for depth in range(REACH)
        ]

    gains_one = put(one, model_one[...], 1 - odd)
    inner = (place > 0) & (place < lax.axis_size("slab") - 1)
    gains_two = put(two, jnp.where(inner, model_two[...], 0.0), odd)
    fill_courant(c2_s, vel_s[...], size_z)

    def crossing(sources, depth):
        terms = [STENCIL_WEIGHTS[depth + 1 + j] * sources[j] for j in range(REACH - depth)]
        return sum(terms[1:], terms[0])

    def cross(ref, at, shift, upward, read):
        for depth in range(REACH):
            layer = at + depth if upward else at - 1 - depth
            sources = [read(j) for j in range(REACH - depth)]
            fine = (layer + shift) // 2 * size_y
            factor = c2_s[fine : fine + size_y, :]
            ref[layer, data, :] = ref[layer, data, :] + factor * crossing(sources, depth)

    cross(first_s, wide, 0, False, lambda j: cur_s[REACH + j])
    cross(first_s, wide, 0, True, lambda j: cur_s[REACH - 1 - j])
    cross(first_s, wide + width, 0, False, lambda j: cur_s[REACH + width + j])
    cross(first_s, wide + width, 0, True, lambda j: cur_s[REACH + width - 1 - j])
    cross(two_s, REACH, REACH, False, lambda j: near_s[REACH + j])
    cross(two_s, REACH, REACH, True, lambda j: near_s[REACH - 1 - j])
    cross(two_s, REACH + width, REACH, False, lambda j: near_s[REACH + width + j])
    cross(two_s, REACH + width, REACH, True, lambda j: near_s[REACH + width - 1 - j])

    inject(first_s.at[pl.ds(REACH, width + wide)], REACH, width + wide, 8, pulse_one)
    for ch in range(0, width + 2 * REACH, STEP):
        centre, total = laplace(first_s, ch + REACH, size_y, weights)
        factor = courant(c2_s, ch + REACH, STEP, size_y)
        sec_s[ch : ch + STEP] = 2.0 * centre - cur_s[ch : ch + STEP] + factor * total
    inject(sec_s, REACH, width + wide, 0, pulse(2))

    region = (width + 2 * REACH) * size_y
    row = (rec[...] - (place * width - REACH) * plane) // size_z
    hot = row == lax.broadcasted_iota(jnp.int32, (region, receivers), 0)
    hot = jnp.where(hot, 1.0, 0.0).astype(jnp.bfloat16)
    lanes = lanes_in[...].astype(f32) > 0.5
    lo = REACH * size_y
    hi = lo + width * size_y
    own = (row >= lo) & (row < hi)
    layer = row // size_y
    gain = jnp.zeros((1, receivers), f32)
    for depth in range(REACH):
        low_layer = REACH - 1 - depth
        high_layer = REACH + width + depth
        one_side = layer == low_layer + (1 - odd) * (high_layer - low_layer)
        two_side = layer == low_layer + odd * (high_layer - low_layer)
        gain = jnp.where(one_side, gains_one[depth], jnp.where(two_side, gains_two[depth], gain))

    def read(field, marks):
        turned = field.T
        total = sum(jnp.dot(part, marks, preferred_element_type=f32) for part in split3(turned))
        return jnp.sum(jnp.where(lanes, total, 0.0), axis=0, keepdims=True)

    def spread_out(values, marks):
        placed = jnp.where(lanes, values, 0.0)
        dims = (((1,), (1,)), ((), ()))
        return sum(lax.dot_general(marks, part, dims, preferred_element_type=f32) for part in split3(placed))

    first_own = first_s[wide : wide + width, data, :].reshape(width * size_y, size_z)
    read_one = read(first_own, hot[lo:hi])
    read_two = read(sec_s[...].reshape(region, size_z), hot) + gain
    samples[0:1, :] = read_one
    samples[1:2, :] = jnp.where(own, read_two, 0.0)
    add_one = spread_out(read_one - obs[0:1, :], hot[lo:hi])
    add_two = spread_out(read_two - obs[1:2, :], hot)

    for ch in range(0, width + 2 * REACH, STEP):
        extra = add_two[ch * size_y : (ch + STEP) * size_y].reshape(STEP, size_y, size_z)
        two_s[ch : ch + STEP, data, :] = two_s[ch : ch + STEP, data, :] + extra
    for ch in range(0, width, STEP):
        centre, total = laplace(two_s, ch + REACH, size_y, weights)
        extra = add_one[ch * size_y : (ch + STEP) * size_y].reshape(STEP, size_y, size_z)
        factor = courant(c2_s, ch + wide, STEP, size_y)
        adj_one = 2.0 * centre - near[ch : ch + STEP] + factor * total + extra
        first = first_s[ch + wide : ch + wide + STEP, data, :]
        now_field = cur[ch : ch + STEP]
        bend_two = sec_s[ch + REACH : ch + REACH + STEP] - 2.0 * first + now_field
        bend_one = first - 2.0 * now_field + prev[ch : ch + STEP]
        image = centre * bend_two + adj_one * bend_one
        image = image.reshape(STEP // 2, 2, size_y, size_z)
        image = image[:, 0] + image[:, 1]
        img_s[ch // 2 * size_y : (ch + STEP) // 2 * size_y, :] = image.reshape(STEP // 2 * size_y, size_z)
    grid_r = lax.broadcasted_iota(jnp.int32, (size_z, size_z), 0)
    grid_c = lax.broadcasted_iota(jnp.int32, (size_z, size_z), 1)
    gather = jnp.where(grid_r // 2 == grid_c, 1.0, 0.0).astype(f32)
    folded = img_s[pl.ds(0, rows, stride=2), :] + img_s[pl.ds(1, rows, stride=2), :]
    blocks = jnp.dot(folded, gather, precision=HIGHEST, preferred_element_type=f32)
    own_vel = twice(vel[...])
    factor = 2.0 / (own_vel * own_vel * own_vel)
    pay[0:rows, :] = jnp.where(lane < size_z // 2, factor * blocks, own_vel)
    if with_models:
        pay[rows : rows + short, :] = model_one[...]
        pay[rows + short : rows + 2 * short, :] = model_two[...]
        pay[rows + 2 * short :, :] = fars[0][1:].reshape(short, size_z)


def mix_kernel(*refs, cells):
    count = len(refs) - 5
    pays = refs[:count]
    part, other, obs, update, misfit = refs[count:]
    f32 = jnp.float32
    misfit[...] = part[...] + other[...] - obs[...]
    rows = update.shape[0] * update.shape[1]
    lane = lax.broadcasted_iota(jnp.int32, (1, pays[0].shape[1]), 1)
    half = update.shape[2]
    model_lane = lane >= half
    total = pays[0].shape[0]
    mean = sum(ref[...] for ref in pays[1:]) + pays[0][...]
    mean = mean * (1.0 / count)

    def norm(diff):
        sq = diff * diff
        sq = jnp.concatenate([jnp.where(model_lane, sq[0:rows], 0.0), sq[rows:]], axis=0)
        sq = jnp.sum(sq.reshape(total // 8, 8, sq.shape[1]), axis=0)
        return jnp.sum(jnp.sum(sq, axis=1, keepdims=True), axis=0, keepdims=True)

    spread = jnp.zeros(mean.shape, f32)
    for ref in pays:
        diff = ref[...] - mean
        spread = spread + diff * diff
    spread = jnp.concatenate([jnp.where(model_lane, spread[0:rows], 0.0), spread[rows:]], axis=0)
    spread = jnp.sum(spread.reshape(total // 8, 8, spread.shape[1]), axis=0)
    spread = jnp.sum(jnp.sum(spread, axis=1, keepdims=True), axis=0, keepdims=True)
    band = (2.0 * count / (count * (count - 1))) * spread
    own = pays[0][...]
    mixed = own[0:rows]
    kernel_sum = jnp.ones((1, 1), f32)
    for ref in pays[1:]:
        weight = jnp.exp(-norm(ref[...] - own) / band)
        mixed = mixed + weight * ref[0:rows, :]
        kernel_sum = kernel_sum + weight
    coef = (2.0 * cells) / band
    pull = coef * (own[0:rows, half:] * kernel_sum - mixed[:, half:])
    update[...] = ((mixed[:, 0:half] + pull) * (1.0 / count)).reshape(update.shape)


def device_step(
    vel_coarse,
    fwd_prev,
    fwd_cur,
    adj_far,
    adj_near,
    src_cell,
    src_step,
    wavelet,
    rec_cell,
    observed,
):
    f32 = jnp.float32
    slabs = lax.axis_size("slab")
    count = lax.axis_size("particle")
    fast = is_fast(slabs, count)
    model = vel_coarse[0]
    prev, cur, far, near = fwd_prev[0], fwd_cur[0], adj_far[0], adj_near[0]
    width, size_y, size_z = prev.shape
    half, coarse_y, coarse_z = model.shape
    rows = half * coarse_y
    short = rows // 2
    near_layers = 4 * REACH + 1
    far_layers = 1 + short // size_y
    receivers = rec_cell.shape[0]
    in_vmem = pl.BlockSpec(memory_space=pltpu.VMEM)
    padded = pltpu.VMEM((width + 2 * REACH, PITCH, size_z), f32)
    start = pl.pallas_call(
        start_kernel,
        out_shape=(
            pltpu.VMEM((near_layers, size_y, size_z), f32),
            pltpu.VMEM((near_layers, size_y, size_z), f32),
            pltpu.VMEM((far_layers, size_y, size_z), f32),
            pltpu.VMEM((short, size_z), f32),
            pltpu.VMEM((width, size_y, size_z), f32),
            pltpu.VMEM((width, size_y, size_z), f32),
            pltpu.VMEM((size_z, receivers), jnp.bfloat16),
            pltpu.VMEM((1, receivers), jnp.int32),
            pltpu.VMEM((1, wavelet.shape[0]), f32),
            pltpu.VMEM((2, receivers), f32),
        ),
        in_specs=[in_vmem] * 8,
        out_specs=(in_vmem,) * 10,
        scratch_shapes=[padded, padded, pltpu.VMEM((2 * rows, size_z), f32)],
        name="start_steps",
    )
    to_one, to_two, to_far, packed, *kept, obs = start(
        prev, cur, far, near, model, rec_cell[None], observed, wavelet[None]
    )
    even = [(i, i + 1) for i in range(0, slabs - 1, 2)]
    model_one = swap(packed, "slab", even)
    one = swap(to_one, "slab", even)
    uneven = [(i, i + 1) for i in range(1, slabs - 1, 2)]
    two = swap(to_two, "slab", uneven)
    fars = [swap(to_far, "slab", [(i, i + 2) for i in range(slabs - 2) if i % 4 < 2])]
    if fast:
        model_two = swap(model_one, "slab", [(0, 2), (1, 3)])
    else:
        model_two = swap(packed, "slab", uneven)
        others = [(i, i + 2) for i in range(slabs - 2) if i % 4 >= 2]
        if others:
            fars.append(swap(to_far, "slab", others))
    wide = 2 * REACH
    pay_rows = rows + 3 * short if fast else rows
    own_part, near_part, *small = kept
    operands = (
        prev, cur, near, model, own_part, near_part, packed, *small, obs,
        one, two, model_one, model_two, *fars,
    )
    plain = pltpu.VMEM((width + 2 * REACH, size_y, size_z), f32)
    pay, samples = pl.pallas_call(
        lambda *refs: wave_kernel(*refs, n_far=len(fars), with_models=fast),
        out_shape=(
            pltpu.VMEM((pay_rows, size_z), f32),
            pltpu.VMEM((2, receivers), f32),
        ),
        in_specs=[pl.BlockSpec(memory_space=pltpu.SMEM)] * 2 + [in_vmem] * len(operands),
        out_specs=(in_vmem, in_vmem),
        scratch_shapes=[
            plain,
            plain,
            pltpu.VMEM((width + 2 * wide, PITCH, size_z), f32),
            plain,
            padded,
            pltpu.VMEM((3 * short, size_z), f32),
            pltpu.VMEM((6 * rows, size_z), f32),
            pltpu.VMEM((2 * rows, size_z), f32),
        ],
        name="wave_steps",
    )(src_cell, src_step, *[resident(block) for block in operands])
    cells_coarse = rows * slabs * coarse_z
    if not fast:
        residual = lax.psum(samples, "slab") - observed
        gathered = lax.all_gather(pay, "particle", axis=0)
        models = gathered[:, :, coarse_z:]
        deltas = models[:, None] - models[None]
        dist = lax.psum(jnp.sum(deltas * deltas, axis=(2, 3)), "slab")
        band = jnp.sum(dist) / (count * (count - 1))
        row = lax.dynamic_index_in_dim(dist, lax.axis_index("particle"), 0, keepdims=False)
        weights = jnp.exp(-row / band)
        mixed = jnp.einsum("q,qrz->rz", weights, gathered, precision=HIGHEST)
        own = pay[:, coarse_z:]
        pull = (2.0 * cells_coarse / band) * (own * jnp.sum(weights) - mixed[:, coarse_z:])
        update = (mixed[:, :coarse_z] + pull) / count
        return (update.reshape(model.shape)[None], residual[None])

    blocks = {0: pay}
    for flip in (6, 4, 2):
        blocks[flip] = swap(pay, "particle", [(i, i ^ flip) for i in range(count) if i < i ^ flip])
    for flip in (0, 6, 4, 2):
        pairs = [(i, i ^ 1) for i in range(0, count, 2)]
        blocks[flip + 1] = swap(blocks[flip], "particle", pairs)
    part = samples + swap(samples, "slab", [(0, 1), (2, 3)])
    other = swap(part, "slab", [(0, 2), (1, 3)])
    update, residual = pl.pallas_call(
        lambda *refs: mix_kernel(*refs, cells=cells_coarse),
        out_shape=(
            jax.ShapeDtypeStruct(model.shape, f32),
            jax.ShapeDtypeStruct((2, receivers), f32),
        ),
        in_specs=[in_vmem] * 11,
        out_specs=(in_vmem, in_vmem),
        name="mix_particles",
    )(*[resident(blocks[i]) for i in range(count)], resident(part), resident(other), resident(obs))
    return (update[None], residual[None])


def solution(mesh):
    in_specs = (
        P("particle", "slab", None, None),
        P("particle", "slab", None, None),
        P("particle", "slab", None, None),
        P("particle", "slab", None, None),
        P("particle", "slab", None, None),
        P("particle"),
        P("particle"),
        P(),
        P(),
        P(),
    )
    out_specs = (P("particle", "slab", None, None), P("particle", None, None))
    return jax.shard_map(device_step, mesh=mesh, in_specs=in_specs, out_specs=out_specs, check_vma=False)
```

```python
import jax
import jax.numpy as jnp
from jax import lax
from jax.experimental import pallas as pl
from jax.experimental.pallas import tpu as pltpu
from jax.sharding import PartitionSpec as P


STENCIL_WEIGHTS = (-205.0 / 72.0, 8.0 / 5.0, -1.0 / 5.0, 8.0 / 315.0, -1.0 / 560.0)
COURANT_FACTOR = 0.1
REACH = 4
STEP = 4
PITCH = 32
HIGHEST = lax.Precision.HIGHEST


def swap_uneven(block, slabs, count):
    pairs = []
    for particle in range(count):
        base = particle * slabs
        pairs += [(base + i, base + i + 1) for i in range(1, slabs - 1, 2)]
        if particle % 2 == 0:
            pairs += [(base, base + slabs), (base + slabs - 1, base + 2 * slabs - 1)]
    return swap(block, ("particle", "slab"), pairs)


def resident(block):
    return pltpu.with_memory_space_constraint(block, pltpu.MemorySpace.VMEM)


def is_fast(slabs, count):
    return slabs == 4 and count == 8


def swap(block, axis, pairs):
    both = [(a, b) for a, b in pairs] + [(b, a) for a, b in pairs]
    return lax.ppermute(block, axis, both)


def twice(model):
    flat = model.reshape(model.shape[0] * model.shape[1], model.shape[2])
    return jnp.concatenate([flat, flat], axis=1)


def lane_weights(size_z):
    lane = lax.broadcasted_iota(jnp.int32, (1, size_z), 1)
    below = [jnp.where(lane >= k, w, 0.0).astype(jnp.float32) for k, w in enumerate(STENCIL_WEIGHTS)]
    above = [
        jnp.where(lane < size_z - k, w, 0.0).astype(jnp.float32) for k, w in enumerate(STENCIL_WEIGHTS)
    ]
    return below, above


def clear_margins(ref, size_y):
    ref[:, 0:8, :] = jnp.zeros((ref.shape[0], 8, ref.shape[2]), jnp.float32)
    rest = PITCH - 8 - size_y
    ref[:, 8 + size_y : PITCH, :] = jnp.zeros((ref.shape[0], rest, ref.shape[2]), jnp.float32)


def laplace(ref, at, size_y, weights):
    below, above = weights
    data = pl.ds(8, size_y)
    size_z = ref.shape[2]
    centre = ref[at : at + STEP, data, :]
    flat = centre.reshape(STEP * size_y, size_z)
    total = (3.0 * STENCIL_WEIGHTS[0]) * centre
    for k in range(1, 5):
        pairs = (
            ref[at + k : at + k + STEP, data, :]
            + ref[at - k : at - k + STEP, data, :]
            + (ref[at : at + STEP, pl.ds(8 + k, size_y), :] + ref[at : at + STEP, pl.ds(8 - k, size_y), :])
        )
        along = pltpu.roll(flat, k, 1) * below[k] + pltpu.roll(flat, size_z - k, 1) * above[k]
        total = total + STENCIL_WEIGHTS[k] * pairs + along.reshape(STEP, size_y, size_z)
    return centre, total


def fill_courant(c2_ref, packed, size_z):
    grid_r = lax.broadcasted_iota(jnp.int32, (size_z, 2 * size_z), 0)
    grid_c = lax.broadcasted_iota(jnp.int32, (size_z, 2 * size_z), 1)
    spread = jnp.where(grid_r == grid_c // 2, 1.0, 0.0).astype(jnp.float32)
    scaled = COURANT_FACTOR * packed
    fine = jnp.dot(scaled * scaled, spread, precision=HIGHEST, preferred_element_type=jnp.float32)
    count = packed.shape[0]
    part = count if count < 16 else 16
    for start in range(0, count, part):
        for side in range(2):
            rows = fine[start : start + part, side * size_z : (side + 1) * size_z]
            base = 4 * start + 2 * part * side
            c2_ref[pl.ds(base, part, stride=2), :] = rows
            c2_ref[pl.ds(base + 1, part, stride=2), :] = rows


def courant(c2_ref, layer, count, size_y):
    size_z = c2_ref.shape[1]
    block = c2_ref[layer // 2 * size_y : (layer + count) // 2 * size_y, :]
    block = block.reshape(count // 2, 1, size_y, size_z)
    return jnp.broadcast_to(block, (count // 2, 2, size_y, size_z)).reshape(count, size_y, size_z)


def split3(values):
    high = values.astype(jnp.bfloat16)
    rest = values - high.astype(jnp.float32)
    middle = rest.astype(jnp.bfloat16)
    low = (rest - middle.astype(jnp.float32)).astype(jnp.bfloat16)
    return (high, middle, low)


def start_kernel(
    prev, cur, far, near, vel, rec, obs, wavelet, to_one, to_two, to_far, packed,
    own_part, near_part, lanes_out, rec_out, wavelet_out, obs_out, cur_s, near_s, c2_s
):
    width, size_y, size_z = prev.shape
    f32 = jnp.float32
    place = lax.axis_index("slab")
    odd = place % 2
    top = width - REACH
    plane = size_y * size_z
    data = pl.ds(8, size_y)
    weights = lane_weights(size_z)
    for ref, field in ((cur_s, cur), (near_s, near)):
        clear_margins(ref, size_y)
        for start in (0, REACH + width):
            ref[start : start + REACH, data, :] = jnp.zeros((REACH, size_y, size_z), f32)
        ref[REACH : REACH + width, data, :] = field[...]
    rows = vel.shape[0] * vel.shape[1]
    flat = vel[...].reshape(rows, vel.shape[2])
    packed[...] = jnp.concatenate([flat[: rows // 2], flat[rows // 2 :]], axis=1)
    fill_courant(c2_s, packed[...], size_z)
    rec_out[...] = rec[...]
    obs_out[...] = obs[...]
    wavelet_out[...] = wavelet[...]
    for ch in range(0, width, STEP):
        factor = courant(c2_s, ch, STEP, size_y)
        centre, total = laplace(cur_s, ch + REACH, size_y, weights)
        part = 2.0 * centre - prev[ch : ch + STEP] + factor * total
        own_part[ch : ch + STEP] = part
        centre, total = laplace(near_s, ch + REACH, size_y, weights)
        near_part[ch : ch + STEP] = 2.0 * centre - far[ch : ch + STEP] + factor * total

    cells = rec[...]
    count = cells.shape[1]
    lanes = lax.broadcasted_iota(jnp.int32, (size_z, count), 0) == cells % size_z
    lanes = jnp.where(lanes, 1.0, 0.0).astype(jnp.bfloat16)
    lanes_out[...] = lanes
    in_row = lax.broadcasted_iota(jnp.int32, (size_y, count), 0) == cells % plane // size_z
    fields = jnp.concatenate(
        [own_part[...].reshape(width * size_y, size_z), c2_s[...], cur[...].reshape(width * size_y, size_z)],
        axis=0,
    )
    picked = sum(jnp.dot(part, lanes, preferred_element_type=f32) for part in split3(fields))
    picked = picked.reshape(-1, size_y, count)
    picked = jnp.sum(jnp.where(in_row[None], picked, 0.0), axis=1)
    half = width // 2
    columns = picked[width + half :]
    for ref, low in ((to_one, odd), (to_two, 1 - odd)):
        outer = pl.ds((1 - low) * top, REACH)
        ref[0:REACH] = own_part[outer]
        ref[REACH : 2 * REACH] = cur[outer]
        ref[2 * REACH : 3 * REACH] = near_part[outer]
        ref[3 * REACH : 4 * REACH] = near[outer]
        deep = jnp.where(low == 0, picked[0:REACH], picked[top:width])
        block = jnp.concatenate([deep, picked[width : width + half]], axis=0)
        ref[4 * REACH :] = fold(block, size_y, size_z)
    to_far[0:1] = fold(columns, size_y, size_z)
    to_far[1:] = packed[...].reshape(to_far.shape[0] - 1, size_y, size_z)


def join_kernel(first, second, out):
    out[0 : first.shape[0]] = first[...]
    out[first.shape[0] :] = second[...].reshape(-1, out.shape[1], out.shape[2])


def fold(block, size_y, size_z):
    pieces = [block[:, at : at + size_z] for at in range(0, block.shape[1], size_z)]
    return jnp.concatenate(pieces, axis=0).reshape(-1, size_y, size_z)


def unfold(layer, count):
    flat = layer.reshape(-1, layer.shape[-1])
    rows = flat.shape[0] * flat.shape[1] // count
    return jnp.concatenate([flat[at : at + rows] for at in range(0, flat.shape[0], rows)], axis=1)


def wave_kernel(
    src_cell, src_step, prev, cur, near, vel, own_part, near_part, packed, lanes_in, rec, wavelet, obs,
    one, two, model_one, *rest, n_far, with_models
):
    if not with_models:
        model_two, rest = rest[0], rest[1:]
    fars = rest[:n_far]
    pay, samples = rest[n_far : n_far + 2]
    cur_s, near_s, first_s, sec_s, two_s, vel_s, c2_s, img_s = rest[n_far + 2 :]
    width, size_y, size_z = prev.shape
    rows = vel.shape[0] * vel.shape[1]
    receivers = rec.shape[1]
    plane = size_y * size_z
    place = lax.axis_index("slab")
    odd = place % 2
    f32 = jnp.float32
    data = pl.ds(8, size_y)
    lane = lax.broadcasted_iota(jnp.int32, (1, size_z), 1)
    weights = lane_weights(size_z)
    wide = 2 * REACH
    clear_margins(first_s, size_y)
    clear_margins(two_s, size_y)
    for start in (0, width + wide + REACH):
        first_s[start : start + REACH, data, :] = jnp.zeros((REACH, size_y, size_z), f32)
    cur_s[REACH : REACH + width] = cur[...]
    near_s[REACH : REACH + width] = near[...]
    first_s[wide : wide + width, data, :] = own_part[...]
    two_s[REACH : REACH + width, data, :] = near_part[...]
    short = packed.shape[0]
    vel_s[short : 2 * short] = packed[...]

    cell = src_cell[0]
    now = src_step[0]
    src_layer = cell // plane - place * width
    same_column = rec[...] % plane == cell % plane

    ticks = lax.broadcasted_iota(jnp.int32, wavelet.shape, 1)

    def pulse(ahead):
        return jnp.sum(jnp.where(ticks == now + ahead, wavelet[...], 0.0), axis=1, keepdims=True)

    pulse_one = pulse(1)

    def inject(ref, start, layers, offset, pulse):
        layer = src_layer + start
        inside = (layer >= 0) & (layer < layers)
        layer = jnp.clip(layer, 0, layers - 1)
        value = jnp.where(inside, pulse, 0.0)
        at = pl.ds(offset + cell % plane // size_z, 1)
        ref[layer, at, :] = ref[layer, at, :] + jnp.where(lane == cell % size_z, value, 0.0)

    far_high = 1 - (place % 4) // 2
    hops = [unfold(block[0:1], receivers) for block in fars]

    def put(block, model, high):
        outer = pl.ds(high * (width + REACH), REACH)
        first_s[pl.ds(high * (width + REACH) + REACH, REACH), data, :] = block[0:REACH]
        cur_s[outer] = block[REACH : 2 * REACH]
        two_s[outer, data, :] = block[2 * REACH : 3 * REACH]
        near_s[outer] = block[3 * REACH : 4 * REACH]
        vel_s[pl.ds(high * 2 * short, short)] = model
        up = high == 1
        columns = unfold(block[4 * REACH :], receivers)
        half = columns.shape[0] - REACH
        deep = [jnp.where(up, columns[j : j + 1], columns[3 - j : 4 - j]) for j in range(REACH)]
        factor = [
            jnp.where(up, columns[REACH + m : REACH + m + 1], columns[REACH + half - 1 - m : REACH + half - m])
            for m in range(half)
        ]
        beyond = [jnp.zeros((1, receivers), f32)] * REACH
        for index, hop in enumerate(hops):
            side = far_high if index == 0 else 1 - far_high
            last = hop.shape[0] - 1
            for u in range(REACH):
                seen = jnp.where(up, hop[u : u + 1], hop[last - u : last - u + 1])
                beyond[u] = jnp.where(side == high, seen, beyond[u])
        src_depth = high * (src_layer - width) + (1 - high) * (-1 - src_layer)
        for j in range(REACH):
            source = jnp.where(src_depth == REACH + j, pulse_one, 0.0)
            deep[j] = deep[j] + jnp.where(same_column, source, 0.0)
            more = sum(STENCIL_WEIGHTS[4 + u - j] * beyond[u] for u in range(j + 1))
            deep[j] = deep[j] + factor[(REACH + j) // 2] * more
        return [
            factor[depth // 2] * sum(STENCIL_WEIGHTS[4 + j - depth] * deep[j] for j in range(depth + 1))
            for depth in range(REACH)
        ]

    gains_one = put(one, model_one[...], 1 - odd)
    inner = (place > 0) & (place < lax.axis_size("slab") - 1)
    if with_models:
        model_two = fars[0][2:].reshape(short, size_z)
    gains_two = put(jnp.where(inner, two[...], 0.0), jnp.where(inner, model_two[...], 0.0), odd)
    fill_courant(c2_s, vel_s[...], size_z)

    def crossing(sources, depth):
        terms = [STENCIL_WEIGHTS[depth + 1 + j] * sources[j] for j in range(REACH - depth)]
        return sum(terms[1:], terms[0])

    def cross(ref, at, shift, upward, read):
        for depth in range(REACH):
            layer = at + depth if upward else at - 1 - depth
            sources = [read(j) for j in range(REACH - depth)]
            fine = (layer + shift) // 2 * size_y
            factor = c2_s[fine : fine + size_y, :]
            ref[layer, data, :] = ref[layer, data, :] + factor * crossing(sources, depth)

    cross(first_s, wide, 0, False, lambda j: cur_s[REACH + j])
    cross(first_s, wide, 0, True, lambda j: cur_s[REACH - 1 - j])
    cross(first_s, wide + width, 0, False, lambda j: cur_s[REACH + width + j])
    cross(first_s, wide + width, 0, True, lambda j: cur_s[REACH + width - 1 - j])
    cross(two_s, REACH, REACH, False, lambda j: near_s[REACH + j])
    cross(two_s, REACH, REACH, True, lambda j: near_s[REACH - 1 - j])
    cross(two_s, REACH + width, REACH, False, lambda j: near_s[REACH + width + j])
    cross(two_s, REACH + width, REACH, True, lambda j: near_s[REACH + width - 1 - j])

    inject(first_s.at[pl.ds(REACH, width + wide)], REACH, width + wide, 8, pulse_one)
    for ch in range(0, width + 2 * REACH, STEP):
        centre, total = laplace(first_s, ch + REACH, size_y, weights)
        factor = courant(c2_s, ch + REACH, STEP, size_y)
        sec_s[ch : ch + STEP] = 2.0 * centre - cur_s[ch : ch + STEP] + factor * total
    inject(sec_s, REACH, width + wide, 0, pulse(2))

    region = (width + 2 * REACH) * size_y
    row = (rec[...] - (place * width - REACH) * plane) // size_z
    hot = row == lax.broadcasted_iota(jnp.int32, (region, receivers), 0)
    hot = jnp.where(hot, 1.0, 0.0).astype(jnp.bfloat16)
    lanes = lanes_in[...].astype(f32) > 0.5
    lo = REACH * size_y
    hi = lo + width * size_y
    own = (row >= lo) & (row < hi)
    layer = row // size_y
    gain = jnp.zeros((1, receivers), f32)
    for depth in range(REACH):
        low_layer = REACH - 1 - depth
        high_layer = REACH + width + depth
        one_side = layer == low_layer + (1 - odd) * (high_layer - low_layer)
        two_side = layer == low_layer + odd * (high_layer - low_layer)
        gain = jnp.where(one_side, gains_one[depth], jnp.where(two_side, gains_two[depth], gain))

    def read(field, marks):
        turned = field.T
        total = sum(jnp.dot(part, marks, preferred_element_type=f32) for part in split3(turned))
        return jnp.sum(jnp.where(lanes, total, 0.0), axis=0, keepdims=True)

    def spread_out(values, marks):
        placed = jnp.where(lanes, values, 0.0)
        dims = (((1,), (1,)), ((), ()))
        return sum(lax.dot_general(marks, part, dims, preferred_element_type=f32) for part in split3(placed))

    first_own = first_s[wide : wide + width, data, :].reshape(width * size_y, size_z)
    read_one = read(first_own, hot[lo:hi])
    read_two = read(sec_s[...].reshape(region, size_z), hot) + gain
    samples[0:1, :] = read_one
    samples[1:2, :] = jnp.where(own, read_two, 0.0)
    add_one = spread_out(read_one - obs[0:1, :], hot[lo:hi])
    add_two = spread_out(read_two - obs[1:2, :], hot)

    for ch in range(0, width + 2 * REACH, STEP):
        extra = add_two[ch * size_y : (ch + STEP) * size_y].reshape(STEP, size_y, size_z)
        two_s[ch : ch + STEP, data, :] = two_s[ch : ch + STEP, data, :] + extra
    for ch in range(0, width, STEP):
        centre, total = laplace(two_s, ch + REACH, size_y, weights)
        extra = add_one[ch * size_y : (ch + STEP) * size_y].reshape(STEP, size_y, size_z)
        factor = courant(c2_s, ch + wide, STEP, size_y)
        adj_one = 2.0 * centre - near[ch : ch + STEP] + factor * total + extra
        first = first_s[ch + wide : ch + wide + STEP, data, :]
        now_field = cur[ch : ch + STEP]
        bend_two = sec_s[ch + REACH : ch + REACH + STEP] - 2.0 * first + now_field
        bend_one = first - 2.0 * now_field + prev[ch : ch + STEP]
        image = centre * bend_two + adj_one * bend_one
        image = image.reshape(STEP // 2, 2, size_y, size_z)
        image = image[:, 0] + image[:, 1]
        img_s[ch // 2 * size_y : (ch + STEP) // 2 * size_y, :] = image.reshape(STEP // 2 * size_y, size_z)
    grid_r = lax.broadcasted_iota(jnp.int32, (size_z, size_z), 0)
    grid_c = lax.broadcasted_iota(jnp.int32, (size_z, size_z), 1)
    gather = jnp.where(grid_r // 2 == grid_c, 1.0, 0.0).astype(f32)
    folded = img_s[pl.ds(0, rows, stride=2), :] + img_s[pl.ds(1, rows, stride=2), :]
    blocks = jnp.dot(folded, gather, precision=HIGHEST, preferred_element_type=f32)
    own_vel = twice(vel[...])
    factor = 2.0 / (own_vel * own_vel * own_vel)
    pay[0:rows, :] = jnp.where(lane < size_z // 2, factor * blocks, own_vel)
    if with_models:
        pay[rows : rows + short, :] = model_one[...]
        pay[rows + short :, :] = fars[0][1:].reshape(2 * short, size_z)


def mix_kernel(*refs, cells):
    count = len(refs) - 5
    pays = refs[:count]
    part, other, obs, update, misfit = refs[count:]
    f32 = jnp.float32
    misfit[...] = part[...] + other[...] - obs[...]
    rows = update.shape[0] * update.shape[1]
    lane = lax.broadcasted_iota(jnp.int32, (1, pays[0].shape[1]), 1)
    half = update.shape[2]
    model_lane = lane >= half
    total = pays[0].shape[0]
    mean = sum(ref[...] for ref in pays[1:]) + pays[0][...]
    mean = mean * (1.0 / count)

    def norm(diff):
        sq = diff * diff
        sq = jnp.concatenate([jnp.where(model_lane, sq[0:rows], 0.0), sq[rows:]], axis=0)
        sq = jnp.sum(sq.reshape(total // 8, 8, sq.shape[1]), axis=0)
        return jnp.sum(jnp.sum(sq, axis=1, keepdims=True), axis=0, keepdims=True)

    spread = jnp.zeros(mean.shape, f32)
    for ref in pays:
        diff = ref[...] - mean
        spread = spread + diff * diff
    spread = jnp.concatenate([jnp.where(model_lane, spread[0:rows], 0.0), spread[rows:]], axis=0)
    spread = jnp.sum(spread.reshape(total // 8, 8, spread.shape[1]), axis=0)
    spread = jnp.sum(jnp.sum(spread, axis=1, keepdims=True), axis=0, keepdims=True)
    band = (2.0 * count / (count * (count - 1))) * spread
    own = pays[0][...]
    mixed = own[0:rows]
    kernel_sum = jnp.ones((1, 1), f32)
    for ref in pays[1:]:
        weight = jnp.exp(-norm(ref[...] - own) / band)
        mixed = mixed + weight * ref[0:rows, :]
        kernel_sum = kernel_sum + weight
    coef = (2.0 * cells) / band
    pull = coef * (own[0:rows, half:] * kernel_sum - mixed[:, half:])
    update[...] = ((mixed[:, 0:half] + pull) * (1.0 / count)).reshape(update.shape)


def device_step(
    vel_coarse,
    fwd_prev,
    fwd_cur,
    adj_far,
    adj_near,
    src_cell,
    src_step,
    wavelet,
    rec_cell,
    observed,
):
    f32 = jnp.float32
    slabs = lax.axis_size("slab")
    count = lax.axis_size("particle")
    fast = is_fast(slabs, count)
    model = vel_coarse[0]
    prev, cur, far, near = fwd_prev[0], fwd_cur[0], adj_far[0], adj_near[0]
    width, size_y, size_z = prev.shape
    half, coarse_y, coarse_z = model.shape
    rows = half * coarse_y
    short = rows // 2
    near_layers = 4 * REACH + 1
    far_layers = 1 + short // size_y
    receivers = rec_cell.shape[0]
    in_vmem = pl.BlockSpec(memory_space=pltpu.VMEM)
    padded = pltpu.VMEM((width + 2 * REACH, PITCH, size_z), f32)
    start = pl.pallas_call(
        start_kernel,
        out_shape=(
            pltpu.VMEM((near_layers, size_y, size_z), f32),
            pltpu.VMEM((near_layers, size_y, size_z), f32),
            pltpu.VMEM((far_layers, size_y, size_z), f32),
            pltpu.VMEM((short, size_z), f32),
            pltpu.VMEM((width, size_y, size_z), f32),
            pltpu.VMEM((width, size_y, size_z), f32),
            pltpu.VMEM((size_z, receivers), jnp.bfloat16),
            pltpu.VMEM((1, receivers), jnp.int32),
            pltpu.VMEM((1, wavelet.shape[0]), f32),
            pltpu.VMEM((2, receivers), f32),
        ),
        in_specs=[in_vmem] * 8,
        out_specs=(in_vmem,) * 10,
        scratch_shapes=[padded, padded, pltpu.VMEM((2 * rows, size_z), f32)],
        name="start_steps",
    )
    to_one, to_two, to_far, packed, *kept, obs = start(
        prev, cur, far, near, model, rec_cell[None], observed, wavelet[None]
    )
    even = [(i, i + 1) for i in range(0, slabs - 1, 2)]
    model_one = swap(packed, "slab", even)
    one = swap(to_one, "slab", even)
    two = swap_uneven(to_two, slabs, count)
    if fast:
        to_far = pl.pallas_call(
            join_kernel,
            out_shape=pltpu.VMEM((far_layers + short // size_y, size_y, size_z), f32),
            in_specs=[in_vmem] * 2,
            out_specs=in_vmem,
            name="join_messages",
        )(resident(to_far), resident(model_one))
    fars = [swap(to_far, "slab", [(i, i + 2) for i in range(slabs - 2) if i % 4 < 2])]
    models = [model_one]
    if not fast:
        models.append(swap_uneven(packed, slabs, count))
        others = [(i, i + 2) for i in range(slabs - 2) if i % 4 >= 2]
        if others:
            fars.append(swap(to_far, "slab", others))
    wide = 2 * REACH
    pay_rows = rows + 3 * short if fast else rows
    own_part, near_part, *small = kept
    operands = (
        prev, cur, near, model, own_part, near_part, packed, *small, obs,
        one, two, *models, *fars,
    )
    plain = pltpu.VMEM((width + 2 * REACH, size_y, size_z), f32)
    pay, samples = pl.pallas_call(
        lambda *refs: wave_kernel(*refs, n_far=len(fars), with_models=fast),
        out_shape=(
            pltpu.VMEM((pay_rows, size_z), f32),
            pltpu.VMEM((2, receivers), f32),
        ),
        in_specs=[pl.BlockSpec(memory_space=pltpu.SMEM)] * 2 + [in_vmem] * len(operands),
        out_specs=(in_vmem, in_vmem),
        scratch_shapes=[
            plain,
            plain,
            pltpu.VMEM((width + 2 * wide, PITCH, size_z), f32),
            plain,
            padded,
            pltpu.VMEM((3 * short, size_z), f32),
            pltpu.VMEM((6 * rows, size_z), f32),
            pltpu.VMEM((2 * rows, size_z), f32),
        ],
        name="wave_steps",
    )(src_cell, src_step, *[resident(block) for block in operands])
    cells_coarse = rows * slabs * coarse_z
    if not fast:
        residual = lax.psum(samples, "slab") - observed
        gathered = lax.all_gather(pay, "particle", axis=0)
        models = gathered[:, :, coarse_z:]
        deltas = models[:, None] - models[None]
        dist = lax.psum(jnp.sum(deltas * deltas, axis=(2, 3)), "slab")
        band = jnp.sum(dist) / (count * (count - 1))
        row = lax.dynamic_index_in_dim(dist, lax.axis_index("particle"), 0, keepdims=False)
        weights = jnp.exp(-row / band)
        mixed = jnp.einsum("q,qrz->rz", weights, gathered, precision=HIGHEST)
        own = pay[:, coarse_z:]
        pull = (2.0 * cells_coarse / band) * (own * jnp.sum(weights) - mixed[:, coarse_z:])
        update = (mixed[:, :coarse_z] + pull) / count
        return (update.reshape(model.shape)[None], residual[None])

    blocks = {0: pay}
    for flip in (6, 4, 2):
        blocks[flip] = swap(pay, "particle", [(i, i ^ flip) for i in range(count) if i < i ^ flip])
    for flip in (0, 6, 4, 2):
        pairs = [(i, i ^ 1) for i in range(0, count, 2)]
        blocks[flip + 1] = swap(blocks[flip], "particle", pairs)
    part = samples + swap(samples, "slab", [(0, 1), (2, 3)])
    other = swap(part, "slab", [(0, 2), (1, 3)])
    update, residual = pl.pallas_call(
        lambda *refs: mix_kernel(*refs, cells=cells_coarse),
        out_shape=(
            jax.ShapeDtypeStruct(model.shape, f32),
            jax.ShapeDtypeStruct((2, receivers), f32),
        ),
        in_specs=[in_vmem] * 11,
        out_specs=(in_vmem, in_vmem),
        name="mix_particles",
    )(*[resident(blocks[i]) for i in range(count)], resident(part), resident(other), resident(obs))
    return (update[None], residual[None])


def solution(mesh):
    in_specs = (
        P("particle", "slab", None, None),
        P("particle", "slab", None, None),
        P("particle", "slab", None, None),
        P("particle", "slab", None, None),
        P("particle", "slab", None, None),
        P("particle"),
        P("particle"),
        P(),
        P(),
        P(),
    )
    out_specs = (P("particle", "slab", None, None), P("particle", None, None))
    return jax.shard_map(
        device_step, mesh=mesh, in_specs=in_specs, out_specs=out_specs, check_vma=False
    )
```

```python
import jax
import jax.numpy as jnp
from jax import lax
from jax.experimental import pallas as pl
from jax.experimental.pallas import tpu as pltpu
from jax.sharding import PartitionSpec as P


STENCIL_WEIGHTS = (-205.0 / 72.0, 8.0 / 5.0, -1.0 / 5.0, 8.0 / 315.0, -1.0 / 560.0)
COURANT_FACTOR = 0.1
REACH = 4
STEP = 4
PITCH = 32
HIGHEST = lax.Precision.HIGHEST


def swap_uneven(block, slabs, count):
    pairs = []
    for particle in range(count):
        base = particle * slabs
        pairs += [(base + i, base + i + 1) for i in range(1, slabs - 1, 2)]
        if particle % 2 == 0:
            pairs += [(base, base + slabs), (base + slabs - 1, base + 2 * slabs - 1)]
    return swap(block, ("particle", "slab"), pairs)


def resident(block):
    return pltpu.with_memory_space_constraint(block, pltpu.MemorySpace.VMEM)


def is_fast(slabs, count):
    return slabs == 4 and count == 8


def swap(block, axis, pairs):
    both = [(a, b) for a, b in pairs] + [(b, a) for a, b in pairs]
    return lax.ppermute(block, axis, both)


def lane_weights(size_z):
    lane = lax.broadcasted_iota(jnp.int32, (1, size_z), 1)
    below = [jnp.where(lane >= k, w, 0.0).astype(jnp.float32) for k, w in enumerate(STENCIL_WEIGHTS)]
    above = [
        jnp.where(lane < size_z - k, w, 0.0).astype(jnp.float32) for k, w in enumerate(STENCIL_WEIGHTS)
    ]
    return below, above


def clear_margins(ref, size_y):
    ref[:, 0:8, :] = jnp.zeros((ref.shape[0], 8, ref.shape[2]), jnp.float32)
    rest = PITCH - 8 - size_y
    ref[:, 8 + size_y : PITCH, :] = jnp.zeros((ref.shape[0], rest, ref.shape[2]), jnp.float32)


def laplace(ref, at, size_y, weights):
    below, above = weights
    data = pl.ds(8, size_y)
    size_z = ref.shape[2]
    centre = ref[at : at + STEP, data, :]
    flat = centre.reshape(STEP * size_y, size_z)
    total = (3.0 * STENCIL_WEIGHTS[0]) * centre
    for k in range(1, 5):
        pairs = (
            ref[at + k : at + k + STEP, data, :]
            + ref[at - k : at - k + STEP, data, :]
            + (ref[at : at + STEP, pl.ds(8 + k, size_y), :] + ref[at : at + STEP, pl.ds(8 - k, size_y), :])
        )
        along = pltpu.roll(flat, k, 1) * below[k] + pltpu.roll(flat, size_z - k, 1) * above[k]
        total = total + STENCIL_WEIGHTS[k] * pairs + along.reshape(STEP, size_y, size_z)
    return centre, total


def fill_courant(c2_ref, packed, size_z):
    grid_r = lax.broadcasted_iota(jnp.int32, (size_z, 2 * size_z), 0)
    grid_c = lax.broadcasted_iota(jnp.int32, (size_z, 2 * size_z), 1)
    spread = jnp.where(grid_r == grid_c // 2, 1.0, 0.0).astype(jnp.float32)
    scaled = COURANT_FACTOR * packed
    fine = jnp.dot(scaled * scaled, spread, precision=HIGHEST, preferred_element_type=jnp.float32)
    count = packed.shape[0]
    part = count if count < 16 else 16
    for start in range(0, count, part):
        for side in range(2):
            rows = fine[start : start + part, side * size_z : (side + 1) * size_z]
            base = 4 * start + 2 * part * side
            c2_ref[pl.ds(base, part, stride=2), :] = rows
            c2_ref[pl.ds(base + 1, part, stride=2), :] = rows


def courant(c2_ref, layer, count, size_y):
    size_z = c2_ref.shape[1]
    block = c2_ref[layer // 2 * size_y : (layer + count) // 2 * size_y, :]
    block = block.reshape(count // 2, 1, size_y, size_z)
    return jnp.broadcast_to(block, (count // 2, 2, size_y, size_z)).reshape(count, size_y, size_z)


def split3(values):
    high = values.astype(jnp.bfloat16)
    rest = values - high.astype(jnp.float32)
    middle = rest.astype(jnp.bfloat16)
    low = (rest - middle.astype(jnp.float32)).astype(jnp.bfloat16)
    return (high, middle, low)


def start_kernel(
    prev, cur, far, near, vel, rec, obs, wavelet, to_one, to_two, to_far, packed,
    own_part, near_part, lanes_out, rec_out, wavelet_out, obs_out, cur_s, near_s, c2_s
):
    width, size_y, size_z = prev.shape
    f32 = jnp.float32
    place = lax.axis_index("slab")
    odd = place % 2
    top = width - REACH
    plane = size_y * size_z
    data = pl.ds(8, size_y)
    weights = lane_weights(size_z)
    for ref, field in ((cur_s, cur), (near_s, near)):
        clear_margins(ref, size_y)
        for start in (0, REACH + width):
            ref[start : start + REACH, data, :] = jnp.zeros((REACH, size_y, size_z), f32)
        ref[REACH : REACH + width, data, :] = field[...]
    packed[...] = pack(vel[...])
    fill_courant(c2_s, packed[...], size_z)
    rec_out[...] = rec[...]
    obs_out[...] = obs[...]
    wavelet_out[...] = wavelet[...]
    for ch in range(0, width, STEP):
        factor = courant(c2_s, ch, STEP, size_y)
        centre, total = laplace(cur_s, ch + REACH, size_y, weights)
        part = 2.0 * centre - prev[ch : ch + STEP] + factor * total
        own_part[ch : ch + STEP] = part
        centre, total = laplace(near_s, ch + REACH, size_y, weights)
        near_part[ch : ch + STEP] = 2.0 * centre - far[ch : ch + STEP] + factor * total

    cells = rec[...]
    count = cells.shape[1]
    lanes = lax.broadcasted_iota(jnp.int32, (size_z, count), 0) == cells % size_z
    lanes = jnp.where(lanes, 1.0, 0.0).astype(jnp.bfloat16)
    lanes_out[...] = lanes
    in_row = lax.broadcasted_iota(jnp.int32, (size_y, count), 0) == cells % plane // size_z
    fields = jnp.concatenate(
        [own_part[...].reshape(width * size_y, size_z), c2_s[...], cur[...].reshape(width * size_y, size_z)],
        axis=0,
    )
    picked = sum(jnp.dot(part, lanes, preferred_element_type=f32) for part in split3(fields))
    picked = picked.reshape(-1, size_y, count)
    picked = jnp.sum(jnp.where(in_row[None], picked, 0.0), axis=1)
    half = width // 2
    columns = picked[width + half :]
    for ref, low in ((to_one, odd), (to_two, 1 - odd)):
        outer = pl.ds((1 - low) * top, REACH)
        ref[0:REACH] = own_part[outer]
        ref[REACH : 2 * REACH] = cur[outer]
        ref[2 * REACH : 3 * REACH] = near_part[outer]
        ref[3 * REACH : 4 * REACH] = near[outer]
        deep = jnp.where(low == 0, picked[0:REACH], picked[top:width])
        block = jnp.concatenate([deep, picked[width : width + half]], axis=0)
        ref[4 * REACH : 4 * REACH + 1] = fold(block, size_y, size_z)
        ref[4 * REACH + 1 :] = packed[...].reshape(-1, size_y, size_z)
    to_far[0:1] = fold(columns, size_y, size_z)
    to_far[1:] = packed[...].reshape(to_far.shape[0] - 1, size_y, size_z)


def pack(model):
    flat = model.reshape(model.shape[0] * model.shape[1], model.shape[2])
    half = flat.shape[0] // 2
    return jnp.concatenate([flat[:half], flat[half:]], axis=1)


def far_kernel(message, model, out, packed):
    packed[...] = pack(model[...])
    out[0 : message.shape[0]] = message[...]
    out[message.shape[0] :] = packed[...].reshape(-1, *out.shape[1:])


def fold(block, size_y, size_z):
    pieces = [block[:, at : at + size_z] for at in range(0, block.shape[1], size_z)]
    return jnp.concatenate(pieces, axis=0).reshape(-1, size_y, size_z)


def unfold(layer, count):
    flat = layer.reshape(-1, layer.shape[-1])
    rows = flat.shape[0] * flat.shape[1] // count
    return jnp.concatenate([flat[at : at + rows] for at in range(0, flat.shape[0], rows)], axis=1)


def crossing(sources, depth):
    terms = [STENCIL_WEIGHTS[depth + 1 + j] * sources[j] for j in range(REACH - depth)]
    return sum(terms[1:], terms[0])


def cross(ref, c2_s, size_y, at, shift, upward, read):
    data = pl.ds(8, size_y)
    for depth in range(REACH):
        layer = at + depth if upward else at - 1 - depth
        sources = [read(j) for j in range(REACH - depth)]
        fine = (layer + shift) // 2 * size_y
        factor = c2_s[fine : fine + size_y, :]
        ref[layer, data, :] = ref[layer, data, :] + factor * crossing(sources, depth)


def pulse_of(wavelet, at):
    ticks = lax.broadcasted_iota(jnp.int32, wavelet.shape, 1)
    return jnp.sum(jnp.where(ticks == at, wavelet[...], 0.0), axis=1, keepdims=True)


def masked(block, inner):
    return jnp.where(inner, block[...], 0.0)


def place_of_slab():
    place = lax.axis_index("slab")
    inner = (place > 0) & (place < lax.axis_size("slab") - 1)
    return place, place % 2, inner


def forward_kernel(
    src_cell, src_step, cur, own_part, packed, lanes_in, rec, wavelet, one, two,
    samples, values, first_s, sec_s, c2_s, hot_out, cur_s, vel_s
):
    width, size_y, size_z = cur.shape
    receivers = rec.shape[1]
    plane = size_y * size_z
    place, odd, inner = place_of_slab()
    f32 = jnp.float32
    data = pl.ds(8, size_y)
    lane = lax.broadcasted_iota(jnp.int32, (1, size_z), 1)
    weights = lane_weights(size_z)
    wide = 2 * REACH
    clear_margins(first_s, size_y)
    for start in (0, width + wide + REACH):
        first_s[start : start + REACH, data, :] = jnp.zeros((REACH, size_y, size_z), f32)
    cur_s[REACH : REACH + width] = cur[...]
    first_s[wide : wide + width, data, :] = own_part[...]
    short = packed.shape[0]
    vel_s[short : 2 * short] = packed[...]

    def put(block, high):
        outer = pl.ds(high * (width + REACH), REACH)
        first_s[pl.ds(high * (width + REACH) + REACH, REACH), data, :] = block[0:REACH]
        cur_s[outer] = block[REACH : 2 * REACH]
        vel_s[pl.ds(high * 2 * short, short)] = block[4 * REACH + 1 :].reshape(short, size_z)

    put(one, 1 - odd)
    put(masked(two, inner), odd)
    fill_courant(c2_s, vel_s[...], size_z)
    cross(first_s, c2_s, size_y, wide, 0, False, lambda j: cur_s[REACH + j])
    cross(first_s, c2_s, size_y, wide, 0, True, lambda j: cur_s[REACH - 1 - j])
    cross(first_s, c2_s, size_y, wide + width, 0, False, lambda j: cur_s[REACH + width + j])
    cross(first_s, c2_s, size_y, wide + width, 0, True, lambda j: cur_s[REACH + width - 1 - j])

    cell = src_cell[0]
    now = src_step[0]
    src_layer = cell // plane - place * width

    def inject(ref, start, layers, offset, pulse):
        layer = src_layer + start
        inside = (layer >= 0) & (layer < layers)
        layer = jnp.clip(layer, 0, layers - 1)
        value = jnp.where(inside, pulse, 0.0)
        at = pl.ds(offset + cell % plane // size_z, 1)
        ref[layer, at, :] = ref[layer, at, :] + jnp.where(lane == cell % size_z, value, 0.0)

    inject(first_s.at[pl.ds(REACH, width + wide)], REACH, width + wide, 8, pulse_of(wavelet, now + 1))
    for ch in range(0, width + 2 * REACH, STEP):
        centre, total = laplace(first_s, ch + REACH, size_y, weights)
        factor = courant(c2_s, ch + REACH, STEP, size_y)
        sec_s[ch : ch + STEP] = 2.0 * centre - cur_s[ch : ch + STEP] + factor * total
    inject(sec_s, REACH, width + wide, 0, pulse_of(wavelet, now + 2))

    region = (width + 2 * REACH) * size_y
    row = (rec[...] - (place * width - REACH) * plane) // size_z
    hot = row == lax.broadcasted_iota(jnp.int32, (region, receivers), 0)
    hot = jnp.where(hot, 1.0, 0.0).astype(jnp.bfloat16)
    hot_out[...] = hot
    lanes = lanes_in[...].astype(f32) > 0.5
    lo = REACH * size_y
    hi = lo + width * size_y

    def read(field, marks):
        turned = field.T
        total = sum(jnp.dot(part, marks, preferred_element_type=f32) for part in split3(turned))
        return jnp.sum(jnp.where(lanes, total, 0.0), axis=0, keepdims=True)

    first_own = first_s[wide : wide + width, data, :].reshape(width * size_y, size_z)
    read_one = read(first_own, hot[lo:hi])
    read_two = read(sec_s[...].reshape(region, size_z), hot)
    values[0:1, :] = read_one
    values[1:2, :] = read_two
    samples[0:1, :] = read_one
    samples[1:2, :] = jnp.where((row >= lo) & (row < hi), read_two, 0.0)


def adjoint_kernel(
    src_cell, src_step, prev, cur, near, packed, near_part, lanes_in, rec, wavelet, obs, one, two,
    values, first_s, sec_s, c2_s, hot_in, *rest, n_far, with_models
):
    fars = rest[:n_far]
    rest = rest[n_far:]
    if with_models:
        model_one, rest = rest[0], rest[1:]
    pay, near_s, two_s, img_s = rest
    width, size_y, size_z = prev.shape
    short = packed.shape[0]
    rows = 2 * short
    receivers = rec.shape[1]
    plane = size_y * size_z
    place, odd, inner = place_of_slab()
    f32 = jnp.float32
    data = pl.ds(8, size_y)
    lane = lax.broadcasted_iota(jnp.int32, (1, size_z), 1)
    weights = lane_weights(size_z)
    wide = 2 * REACH
    clear_margins(two_s, size_y)
    near_s[REACH : REACH + width] = near[...]
    two_s[REACH : REACH + width, data, :] = near_part[...]
    cell = src_cell[0]
    src_layer = cell // plane - place * width
    same_column = rec[...] % plane == cell % plane
    pulse_one = pulse_of(wavelet, src_step[0] + 1)
    far_high = 1 - (place % 4) // 2
    hops = [unfold(block[0:1], receivers) for block in fars]

    def put(block, high):
        outer = pl.ds(high * (width + REACH), REACH)
        two_s[outer, data, :] = block[2 * REACH : 3 * REACH]
        near_s[outer] = block[3 * REACH : 4 * REACH]
        up = high == 1
        columns = unfold(block[4 * REACH : 4 * REACH + 1], receivers)
        half = columns.shape[0] - REACH
        deep = [jnp.where(up, columns[j : j + 1], columns[3 - j : 4 - j]) for j in range(REACH)]
        factor = [
            jnp.where(up, columns[REACH + m : REACH + m + 1], columns[REACH + half - 1 - m : REACH + half - m])
            for m in range(half)
        ]
        beyond = [jnp.zeros((1, receivers), f32)] * REACH
        for index, hop in enumerate(hops):
            side = far_high if index == 0 else 1 - far_high
            last = hop.shape[0] - 1
            for u in range(REACH):
                seen = jnp.where(up, hop[u : u + 1], hop[last - u : last - u + 1])
                beyond[u] = jnp.where(side == high, seen, beyond[u])
        src_depth = high * (src_layer - width) + (1 - high) * (-1 - src_layer)
        for j in range(REACH):
            source = jnp.where(src_depth == REACH + j, pulse_one, 0.0)
            deep[j] = deep[j] + jnp.where(same_column, source, 0.0)
            more = sum(STENCIL_WEIGHTS[4 + u - j] * beyond[u] for u in range(j + 1))
            deep[j] = deep[j] + factor[(REACH + j) // 2] * more
        return [
            factor[depth // 2] * sum(STENCIL_WEIGHTS[4 + j - depth] * deep[j] for j in range(depth + 1))
            for depth in range(REACH)
        ]

    gains_one = put(one, 1 - odd)
    gains_two = put(masked(two, inner), odd)
    cross(two_s, c2_s, size_y, REACH, REACH, False, lambda j: near_s[REACH + j])
    cross(two_s, c2_s, size_y, REACH, REACH, True, lambda j: near_s[REACH - 1 - j])
    cross(two_s, c2_s, size_y, REACH + width, REACH, False, lambda j: near_s[REACH + width + j])
    cross(two_s, c2_s, size_y, REACH + width, REACH, True, lambda j: near_s[REACH + width - 1 - j])

    lanes = lanes_in[...].astype(f32) > 0.5
    lo = REACH * size_y
    hi = lo + width * size_y
    layer = (rec[...] - (place * width - REACH) * plane) // plane
    gain = jnp.zeros((1, receivers), f32)
    for depth in range(REACH):
        low_layer = REACH - 1 - depth
        high_layer = REACH + width + depth
        one_side = layer == low_layer + (1 - odd) * (high_layer - low_layer)
        two_side = layer == low_layer + odd * (high_layer - low_layer)
        gain = jnp.where(one_side, gains_one[depth], jnp.where(two_side, gains_two[depth], gain))

    def spread_out(value, marks):
        placed = jnp.where(lanes, value, 0.0)
        dims = (((1,), (1,)), ((), ()))
        return sum(lax.dot_general(marks, part, dims, preferred_element_type=f32) for part in split3(placed))

    hot = hot_in[...]
    add_one = spread_out(values[0:1, :] - obs[0:1, :], hot[lo:hi])
    add_two = spread_out(values[1:2, :] + gain - obs[1:2, :], hot)
    for ch in range(0, width + 2 * REACH, STEP):
        extra = add_two[ch * size_y : (ch + STEP) * size_y].reshape(STEP, size_y, size_z)
        two_s[ch : ch + STEP, data, :] = two_s[ch : ch + STEP, data, :] + extra
    for ch in range(0, width, STEP):
        centre, total = laplace(two_s, ch + REACH, size_y, weights)
        extra = add_one[ch * size_y : (ch + STEP) * size_y].reshape(STEP, size_y, size_z)
        factor = courant(c2_s, ch + wide, STEP, size_y)
        adj_one = 2.0 * centre - near[ch : ch + STEP] + factor * total + extra
        first = first_s[ch + wide : ch + wide + STEP, data, :]
        now_field = cur[ch : ch + STEP]
        bend_two = sec_s[ch + REACH : ch + REACH + STEP] - 2.0 * first + now_field
        bend_one = first - 2.0 * now_field + prev[ch : ch + STEP]
        image = centre * bend_two + adj_one * bend_one
        image = image.reshape(STEP // 2, 2, size_y, size_z)
        image = image[:, 0] + image[:, 1]
        img_s[ch // 2 * size_y : (ch + STEP) // 2 * size_y, :] = image.reshape(STEP // 2 * size_y, size_z)
    grid_r = lax.broadcasted_iota(jnp.int32, (size_z, size_z), 0)
    grid_c = lax.broadcasted_iota(jnp.int32, (size_z, size_z), 1)
    gather = jnp.where(grid_r // 2 == grid_c, 1.0, 0.0).astype(f32)
    folded = img_s[pl.ds(0, rows, stride=2), :] + img_s[pl.ds(1, rows, stride=2), :]
    blocks = jnp.dot(folded, gather, precision=HIGHEST, preferred_element_type=f32)
    left = lane < size_z // 2
    turned = pltpu.roll(packed[...], size_z // 2, 1)
    own_vel = jnp.concatenate(
        [jnp.where(left, packed[...], turned), jnp.where(left, turned, packed[...])], axis=0
    )
    factor = 2.0 / (own_vel * own_vel * own_vel)
    pay[0:rows, :] = jnp.where(left, factor * blocks, own_vel)
    if with_models:
        pay[rows : rows + short, :] = model_one[...]
        pay[rows + short :, :] = fars[0][1:].reshape(2 * short, size_z)


def mix_kernel(*refs, cells):
    count = len(refs) - 5
    pays = refs[:count]
    part, other, obs, update, misfit = refs[count:]
    f32 = jnp.float32
    misfit[...] = part[...] + other[...] - obs[...]
    rows = update.shape[0] * update.shape[1]
    lane = lax.broadcasted_iota(jnp.int32, (1, pays[0].shape[1]), 1)
    half = update.shape[2]
    model_lane = lane >= half
    total = pays[0].shape[0]
    mean = sum(ref[...] for ref in pays[1:]) + pays[0][...]
    mean = mean * (1.0 / count)

    def norm(diff):
        sq = diff * diff
        sq = jnp.concatenate([jnp.where(model_lane, sq[0:rows], 0.0), sq[rows:]], axis=0)
        sq = jnp.sum(sq.reshape(total // 8, 8, sq.shape[1]), axis=0)
        return jnp.sum(jnp.sum(sq, axis=1, keepdims=True), axis=0, keepdims=True)

    spread = jnp.zeros(mean.shape, f32)
    for ref in pays:
        diff = ref[...] - mean
        spread = spread + diff * diff
    spread = jnp.concatenate([jnp.where(model_lane, spread[0:rows], 0.0), spread[rows:]], axis=0)
    spread = jnp.sum(spread.reshape(total // 8, 8, spread.shape[1]), axis=0)
    spread = jnp.sum(jnp.sum(spread, axis=1, keepdims=True), axis=0, keepdims=True)
    band = (2.0 * count / (count * (count - 1))) * spread
    own = pays[0][...]
    mixed = own[0:rows]
    kernel_sum = jnp.ones((1, 1), f32)
    for ref in pays[1:]:
        weight = jnp.exp(-norm(ref[...] - own) / band)
        mixed = mixed + weight * ref[0:rows, :]
        kernel_sum = kernel_sum + weight
    coef = (2.0 * cells) / band
    pull = coef * (own[0:rows, half:] * kernel_sum - mixed[:, half:])
    update[...] = ((mixed[:, 0:half] + pull) * (1.0 / count)).reshape(update.shape)


def device_step(
    vel_coarse,
    fwd_prev,
    fwd_cur,
    adj_far,
    adj_near,
    src_cell,
    src_step,
    wavelet,
    rec_cell,
    observed,
):
    f32 = jnp.float32
    slabs = lax.axis_size("slab")
    count = lax.axis_size("particle")
    fast = is_fast(slabs, count)
    model = vel_coarse[0]
    prev, cur, far, near = fwd_prev[0], fwd_cur[0], adj_far[0], adj_near[0]
    width, size_y, size_z = prev.shape
    half, coarse_y, coarse_z = model.shape
    rows = half * coarse_y
    short = rows // 2
    near_layers = 4 * REACH + 1 + short // size_y
    far_layers = 1 + short // size_y
    receivers = rec_cell.shape[0]
    in_vmem = pl.BlockSpec(memory_space=pltpu.VMEM)
    padded = pltpu.VMEM((width + 2 * REACH, PITCH, size_z), f32)
    start = pl.pallas_call(
        start_kernel,
        out_shape=(
            pltpu.VMEM((near_layers, size_y, size_z), f32),
            pltpu.VMEM((near_layers, size_y, size_z), f32),
            pltpu.VMEM((far_layers, size_y, size_z), f32),
            pltpu.VMEM((short, size_z), f32),
            pltpu.VMEM((width, size_y, size_z), f32),
            pltpu.VMEM((width, size_y, size_z), f32),
            pltpu.VMEM((size_z, receivers), jnp.bfloat16),
            pltpu.VMEM((1, receivers), jnp.int32),
            pltpu.VMEM((1, wavelet.shape[0]), f32),
            pltpu.VMEM((2, receivers), f32),
        ),
        in_specs=[in_vmem] * 8,
        out_specs=(in_vmem,) * 10,
        scratch_shapes=[padded, padded, pltpu.VMEM((2 * rows, size_z), f32)],
        name="start_steps",
    )
    even = [(i, i + 1) for i in range(0, slabs - 1, 2)]
    if fast:
        model_one = swap(model, "slab", even)
    to_one, to_two, to_far, packed, *kept, obs = start(
        prev, cur, far, near, model, rec_cell[None], observed, wavelet[None]
    )
    one = swap(to_one, "slab", even)
    two = swap_uneven(to_two, slabs, count)
    if fast:
        to_far, model_one = pl.pallas_call(
            far_kernel,
            out_shape=(
                pltpu.VMEM((far_layers + short // size_y, size_y, size_z), f32),
                pltpu.VMEM((short, size_z), f32),
            ),
            in_specs=[in_vmem] * 2,
            out_specs=(in_vmem, in_vmem),
            name="join_messages",
        )(resident(to_far), resident(model_one))
    fars = [swap(to_far, "slab", [(i, i + 2) for i in range(slabs - 2) if i % 4 < 2])]
    others = [(i, i + 2) for i in range(slabs - 2) if i % 4 >= 2]
    if others:
        fars.append(swap(to_far, "slab", others))
    wide = 2 * REACH
    region = (width + wide) * size_y
    own_part, near_part, lanes, rec, pulses = kept
    in_smem = pl.BlockSpec(memory_space=pltpu.SMEM)
    plain = pltpu.VMEM((width + wide, size_y, size_z), f32)
    operands = (cur, own_part, packed, lanes, rec, pulses, one, two)
    forward = pl.pallas_call(
        forward_kernel,
        out_shape=(
            pltpu.VMEM((2, receivers), f32),
            pltpu.VMEM((2, receivers), f32),
            pltpu.VMEM((width + 2 * wide, PITCH, size_z), f32),
            plain,
            pltpu.VMEM((6 * rows, size_z), f32),
            pltpu.VMEM((region, receivers), jnp.bfloat16),
        ),
        in_specs=[in_smem] * 2 + [in_vmem] * len(operands),
        out_specs=(in_vmem,) * 6,
        scratch_shapes=[plain, pltpu.VMEM((3 * short, size_z), f32)],
        name="forward_steps",
    )
    samples, *waves = forward(src_cell, src_step, *[resident(block) for block in operands])
    if fast:
        part = samples + swap(samples, "slab", [(0, 1), (2, 3)])
    pay_rows = rows + 3 * short if fast else rows
    operands = (
        prev, cur, near, packed, near_part, lanes, rec, pulses, obs, one, two, *waves, *fars,
        *([model_one] if fast else []),
    )
    adjoint = pl.pallas_call(
        lambda *refs: adjoint_kernel(*refs, n_far=len(fars), with_models=fast),
        out_shape=pltpu.VMEM((pay_rows, size_z), f32),
        in_specs=[in_smem] * 2 + [in_vmem] * len(operands),
        out_specs=in_vmem,
        scratch_shapes=[plain, padded, pltpu.VMEM((2 * rows, size_z), f32)],
        name="adjoint_steps",
    )
    pay = adjoint(src_cell, src_step, *[resident(block) for block in operands])
    cells_coarse = rows * slabs * coarse_z
    if not fast:
        residual = lax.psum(samples, "slab") - observed
        gathered = lax.all_gather(pay, "particle", axis=0)
        models = gathered[:, :, coarse_z:]
        deltas = models[:, None] - models[None]
        dist = lax.psum(jnp.sum(deltas * deltas, axis=(2, 3)), "slab")
        band = jnp.sum(dist) / (count * (count - 1))
        row = lax.dynamic_index_in_dim(dist, lax.axis_index("particle"), 0, keepdims=False)
        weights = jnp.exp(-row / band)
        mixed = jnp.einsum("q,qrz->rz", weights, gathered, precision=HIGHEST)
        own = pay[:, coarse_z:]
        pull = (2.0 * cells_coarse / band) * (own * jnp.sum(weights) - mixed[:, coarse_z:])
        update = (mixed[:, :coarse_z] + pull) / count
        return (update.reshape(model.shape)[None], residual[None])

    blocks = {0: pay}
    for flip in (6, 4, 2):
        blocks[flip] = swap(pay, "particle", [(i, i ^ flip) for i in range(count) if i < i ^ flip])
    for flip in (0, 6, 4, 2):
        pairs = [(i, i ^ 1) for i in range(0, count, 2)]
        blocks[flip + 1] = swap(blocks[flip], "particle", pairs)
    other = swap(part, "slab", [(0, 2), (1, 3)])
    update, residual = pl.pallas_call(
        lambda *refs: mix_kernel(*refs, cells=cells_coarse),
        out_shape=(
            jax.ShapeDtypeStruct(model.shape, f32),
            jax.ShapeDtypeStruct((2, receivers), f32),
        ),
        in_specs=[in_vmem] * 11,
        out_specs=(in_vmem, in_vmem),
        name="mix_particles",
    )(*[resident(blocks[i]) for i in range(count)], resident(part), resident(other), resident(obs))
    return (update[None], residual[None])


def solution(mesh):
    in_specs = (
        P("particle", "slab", None, None),
        P("particle", "slab", None, None),
        P("particle", "slab", None, None),
        P("particle", "slab", None, None),
        P("particle", "slab", None, None),
        P("particle"),
        P("particle"),
        P(),
        P(),
        P(),
    )
    out_specs = (P("particle", "slab", None, None), P("particle", None, None))
    return jax.shard_map(
        device_step, mesh=mesh, in_specs=in_specs, out_specs=out_specs, check_vma=False
    )
```

```python
import jax
import jax.numpy as jnp
from jax import lax
from jax.experimental import pallas as pl
from jax.experimental.pallas import tpu as pltpu
from jax.sharding import PartitionSpec as P


STENCIL_WEIGHTS = (-205.0 / 72.0, 8.0 / 5.0, -1.0 / 5.0, 8.0 / 315.0, -1.0 / 560.0)
COURANT_FACTOR = 0.1
REACH = 4
STEP = 4
PITCH = 32
HIGHEST = lax.Precision.HIGHEST


def swap_uneven(block, slabs, count):
    pairs = []
    for particle in range(count):
        base = particle * slabs
        pairs += [(base + i, base + i + 1) for i in range(1, slabs - 1, 2)]
        if particle % 2 == 0:
            pairs += [(base, base + slabs), (base + slabs - 1, base + 2 * slabs - 1)]
    return swap(block, ("particle", "slab"), pairs)


def resident(block):
    return pltpu.with_memory_space_constraint(block, pltpu.MemorySpace.VMEM)


def is_fast(slabs, count):
    return slabs == 4 and count == 8


def swap(block, axis, pairs):
    both = [(a, b) for a, b in pairs] + [(b, a) for a, b in pairs]
    return lax.ppermute(block, axis, both)


def lane_weights(size_z):
    lane = lax.broadcasted_iota(jnp.int32, (1, size_z), 1)
    below = [jnp.where(lane >= k, w, 0.0).astype(jnp.float32) for k, w in enumerate(STENCIL_WEIGHTS)]
    above = [
        jnp.where(lane < size_z - k, w, 0.0).astype(jnp.float32) for k, w in enumerate(STENCIL_WEIGHTS)
    ]
    return below, above


def clear_margins(ref, size_y):
    ref[:, 0:8, :] = jnp.zeros((ref.shape[0], 8, ref.shape[2]), jnp.float32)
    rest = PITCH - 8 - size_y
    ref[:, 8 + size_y : PITCH, :] = jnp.zeros((ref.shape[0], rest, ref.shape[2]), jnp.float32)


def laplace(ref, at, size_y, weights):
    below, above = weights
    data = pl.ds(8, size_y)
    size_z = ref.shape[2]
    centre = ref[at : at + STEP, data, :]
    flat = centre.reshape(STEP * size_y, size_z)
    total = (3.0 * STENCIL_WEIGHTS[0]) * centre
    for k in range(1, 5):
        pairs = (
            ref[at + k : at + k + STEP, data, :]
            + ref[at - k : at - k + STEP, data, :]
            + (ref[at : at + STEP, pl.ds(8 + k, size_y), :] + ref[at : at + STEP, pl.ds(8 - k, size_y), :])
        )
        along = pltpu.roll(flat, k, 1) * below[k] + pltpu.roll(flat, size_z - k, 1) * above[k]
        total = total + STENCIL_WEIGHTS[k] * pairs + along.reshape(STEP, size_y, size_z)
    return centre, total


def fill_courant(c2_ref, packed, size_z):
    grid_r = lax.broadcasted_iota(jnp.int32, (size_z, 2 * size_z), 0)
    grid_c = lax.broadcasted_iota(jnp.int32, (size_z, 2 * size_z), 1)
    spread = jnp.where(grid_r == grid_c // 2, 1.0, 0.0).astype(jnp.float32)
    scaled = COURANT_FACTOR * packed
    fine = jnp.dot(scaled * scaled, spread, precision=HIGHEST, preferred_element_type=jnp.float32)
    count = packed.shape[0]
    part = count if count < 16 else 16
    for start in range(0, count, part):
        for side in range(2):
            rows = fine[start : start + part, side * size_z : (side + 1) * size_z]
            base = 4 * start + 2 * part * side
            c2_ref[pl.ds(base, part, stride=2), :] = rows
            c2_ref[pl.ds(base + 1, part, stride=2), :] = rows


def courant(c2_ref, layer, count, size_y):
    size_z = c2_ref.shape[1]
    block = c2_ref[layer // 2 * size_y : (layer + count) // 2 * size_y, :]
    block = block.reshape(count // 2, 1, size_y, size_z)
    return jnp.broadcast_to(block, (count // 2, 2, size_y, size_z)).reshape(count, size_y, size_z)


def split3(values):
    high = values.astype(jnp.bfloat16)
    rest = values - high.astype(jnp.float32)
    middle = rest.astype(jnp.bfloat16)
    low = (rest - middle.astype(jnp.float32)).astype(jnp.bfloat16)
    return (high, middle, low)


def start_kernel(
    prev, cur, far, near, vel, rec, obs, wavelet, to_one, to_two, to_far, packed,
    own_part, near_part, lanes_out, rec_out, wavelet_out, obs_out, cur_s, near_s, c2_s
):
    width, size_y, size_z = prev.shape
    f32 = jnp.float32
    place = lax.axis_index("slab")
    odd = place % 2
    top = width - REACH
    plane = size_y * size_z
    data = pl.ds(8, size_y)
    weights = lane_weights(size_z)
    for ref, field in ((cur_s, cur), (near_s, near)):
        clear_margins(ref, size_y)
        for start in (0, REACH + width):
            ref[start : start + REACH, data, :] = jnp.zeros((REACH, size_y, size_z), f32)
        ref[REACH : REACH + width, data, :] = field[...]
    packed[...] = pack(vel[...])
    fill_courant(c2_s, packed[...], size_z)
    rec_out[...] = rec[...]
    obs_out[...] = obs[...]
    wavelet_out[...] = wavelet[...]
    for ch in range(0, width, STEP):
        factor = courant(c2_s, ch, STEP, size_y)
        centre, total = laplace(cur_s, ch + REACH, size_y, weights)
        part = 2.0 * centre - prev[ch : ch + STEP] + factor * total
        own_part[ch : ch + STEP] = part
        centre, total = laplace(near_s, ch + REACH, size_y, weights)
        near_part[ch : ch + STEP] = 2.0 * centre - far[ch : ch + STEP] + factor * total

    cells = rec[...]
    count = cells.shape[1]
    lanes = lax.broadcasted_iota(jnp.int32, (size_z, count), 0) == cells % size_z
    lanes = jnp.where(lanes, 1.0, 0.0).astype(jnp.bfloat16)
    lanes_out[...] = lanes
    in_row = lax.broadcasted_iota(jnp.int32, (size_y, count), 0) == cells % plane // size_z
    fields = jnp.concatenate(
        [own_part[...].reshape(width * size_y, size_z), c2_s[...], cur[...].reshape(width * size_y, size_z)],
        axis=0,
    )
    picked = sum(jnp.dot(part, lanes, preferred_element_type=f32) for part in split3(fields))
    picked = picked.reshape(-1, size_y, count)
    picked = jnp.sum(jnp.where(in_row[None], picked, 0.0), axis=1)
    half = width // 2
    columns = picked[width + half :]
    for ref, low in ((to_one, odd), (to_two, 1 - odd)):
        outer = pl.ds((1 - low) * top, REACH)
        ref[0:REACH] = own_part[outer]
        ref[REACH : 2 * REACH] = cur[outer]
        ref[2 * REACH : 3 * REACH] = near_part[outer]
        ref[3 * REACH : 4 * REACH] = near[outer]
        deep = jnp.where(low == 0, picked[0:REACH], picked[top:width])
        block = jnp.concatenate([deep, picked[width : width + half]], axis=0)
        ref[4 * REACH : 4 * REACH + 1] = fold(block, size_y, size_z)
        ref[4 * REACH + 1 :] = packed[...].reshape(-1, size_y, size_z)
    to_far[0:1] = fold(columns, size_y, size_z)
    to_far[1:] = packed[...].reshape(to_far.shape[0] - 1, size_y, size_z)


def pack(model):
    flat = model.reshape(model.shape[0] * model.shape[1], model.shape[2])
    half = flat.shape[0] // 2
    return jnp.concatenate([flat[:half], flat[half:]], axis=1)


def far_kernel(message, model, out, packed):
    packed[...] = pack(model[...])
    out[0 : message.shape[0]] = message[...]
    out[message.shape[0] :] = packed[...].reshape(-1, *out.shape[1:])


def join_kernel(first, second, out):
    out[0 : first.shape[0]] = first[...]
    out[first.shape[0] :] = second[...].reshape(-1, *out.shape[1:])


def fold(block, size_y, size_z):
    pieces = [block[:, at : at + size_z] for at in range(0, block.shape[1], size_z)]
    return jnp.concatenate(pieces, axis=0).reshape(-1, size_y, size_z)


def unfold(layer, count):
    flat = layer.reshape(-1, layer.shape[-1])
    rows = flat.shape[0] * flat.shape[1] // count
    return jnp.concatenate([flat[at : at + rows] for at in range(0, flat.shape[0], rows)], axis=1)


def crossing(sources, depth):
    terms = [STENCIL_WEIGHTS[depth + 1 + j] * sources[j] for j in range(REACH - depth)]
    return sum(terms[1:], terms[0])


def cross(ref, c2_s, size_y, at, shift, upward, read):
    data = pl.ds(8, size_y)
    for depth in range(REACH):
        layer = at + depth if upward else at - 1 - depth
        sources = [read(j) for j in range(REACH - depth)]
        fine = (layer + shift) // 2 * size_y
        factor = c2_s[fine : fine + size_y, :]
        ref[layer, data, :] = ref[layer, data, :] + factor * crossing(sources, depth)


def pulse_of(wavelet, at):
    ticks = lax.broadcasted_iota(jnp.int32, wavelet.shape, 1)
    return jnp.sum(jnp.where(ticks == at, wavelet[...], 0.0), axis=1, keepdims=True)


def masked(block, inner):
    return jnp.where(inner, block[...], 0.0)


def place_of_slab():
    place = lax.axis_index("slab")
    inner = (place > 0) & (place < lax.axis_size("slab") - 1)
    return place, place % 2, inner


def forward_kernel(
    src_cell, src_step, cur, own_part, packed, lanes_in, rec, wavelet, one, two,
    samples, values, first_s, sec_s, c2_s, hot_out, cur_s, vel_s
):
    width, size_y, size_z = cur.shape
    receivers = rec.shape[1]
    plane = size_y * size_z
    place, odd, inner = place_of_slab()
    f32 = jnp.float32
    data = pl.ds(8, size_y)
    lane = lax.broadcasted_iota(jnp.int32, (1, size_z), 1)
    weights = lane_weights(size_z)
    wide = 2 * REACH
    clear_margins(first_s, size_y)
    for start in (0, width + wide + REACH):
        first_s[start : start + REACH, data, :] = jnp.zeros((REACH, size_y, size_z), f32)
    cur_s[REACH : REACH + width] = cur[...]
    first_s[wide : wide + width, data, :] = own_part[...]
    short = packed.shape[0]
    vel_s[short : 2 * short] = packed[...]

    def put(block, high):
        outer = pl.ds(high * (width + REACH), REACH)
        first_s[pl.ds(high * (width + REACH) + REACH, REACH), data, :] = block[0:REACH]
        cur_s[outer] = block[REACH : 2 * REACH]
        vel_s[pl.ds(high * 2 * short, short)] = block[4 * REACH + 1 :].reshape(short, size_z)

    put(one, 1 - odd)
    put(masked(two, inner), odd)
    fill_courant(c2_s, vel_s[...], size_z)
    cross(first_s, c2_s, size_y, wide, 0, False, lambda j: cur_s[REACH + j])
    cross(first_s, c2_s, size_y, wide, 0, True, lambda j: cur_s[REACH - 1 - j])
    cross(first_s, c2_s, size_y, wide + width, 0, False, lambda j: cur_s[REACH + width + j])
    cross(first_s, c2_s, size_y, wide + width, 0, True, lambda j: cur_s[REACH + width - 1 - j])

    cell = src_cell[0]
    now = src_step[0]
    src_layer = cell // plane - place * width

    def inject(ref, start, layers, offset, pulse):
        layer = src_layer + start
        inside = (layer >= 0) & (layer < layers)
        layer = jnp.clip(layer, 0, layers - 1)
        value = jnp.where(inside, pulse, 0.0)
        at = pl.ds(offset + cell % plane // size_z, 1)
        ref[layer, at, :] = ref[layer, at, :] + jnp.where(lane == cell % size_z, value, 0.0)

    inject(first_s.at[pl.ds(REACH, width + wide)], REACH, width + wide, 8, pulse_of(wavelet, now + 1))
    for ch in range(0, width + 2 * REACH, STEP):
        centre, total = laplace(first_s, ch + REACH, size_y, weights)
        factor = courant(c2_s, ch + REACH, STEP, size_y)
        sec_s[ch : ch + STEP] = 2.0 * centre - cur_s[ch : ch + STEP] + factor * total
    inject(sec_s, REACH, width + wide, 0, pulse_of(wavelet, now + 2))

    region = (width + 2 * REACH) * size_y
    row = (rec[...] - (place * width - REACH) * plane) // size_z
    hot = row == lax.broadcasted_iota(jnp.int32, (region, receivers), 0)
    hot = jnp.where(hot, 1.0, 0.0).astype(jnp.bfloat16)
    hot_out[...] = hot
    lanes = lanes_in[...].astype(f32) > 0.5
    lo = REACH * size_y
    hi = lo + width * size_y

    def read(field, marks):
        turned = field.T
        total = sum(jnp.dot(part, marks, preferred_element_type=f32) for part in split3(turned))
        return jnp.sum(jnp.where(lanes, total, 0.0), axis=0, keepdims=True)

    first_own = first_s[wide : wide + width, data, :].reshape(width * size_y, size_z)
    read_one = read(first_own, hot[lo:hi])
    read_two = read(sec_s[...].reshape(region, size_z), hot)
    values[0:1, :] = read_one
    values[1:2, :] = read_two
    samples[0:1, :] = read_one
    samples[1:2, :] = jnp.where((row >= lo) & (row < hi), read_two, 0.0)


def adjoint_kernel(
    src_cell, src_step, prev, cur, near, packed, near_part, lanes_in, rec, wavelet, obs, one, two,
    values, first_s, sec_s, c2_s, hot_in, *rest, n_far, with_models
):
    fars = rest[:n_far]
    rest = rest[n_far:]
    if with_models:
        model_one, rest = rest[0], rest[1:]
    pay, near_s, two_s, img_s = rest
    width, size_y, size_z = prev.shape
    short = packed.shape[0]
    rows = 2 * short
    receivers = rec.shape[1]
    plane = size_y * size_z
    place, odd, inner = place_of_slab()
    f32 = jnp.float32
    data = pl.ds(8, size_y)
    lane = lax.broadcasted_iota(jnp.int32, (1, size_z), 1)
    weights = lane_weights(size_z)
    wide = 2 * REACH
    clear_margins(two_s, size_y)
    near_s[REACH : REACH + width] = near[...]
    two_s[REACH : REACH + width, data, :] = near_part[...]
    cell = src_cell[0]
    src_layer = cell // plane - place * width
    same_column = rec[...] % plane == cell % plane
    pulse_one = pulse_of(wavelet, src_step[0] + 1)
    far_high = 1 - (place % 4) // 2
    hops = [unfold(block[0:1], receivers) for block in fars]

    def put(block, high):
        outer = pl.ds(high * (width + REACH), REACH)
        two_s[outer, data, :] = block[2 * REACH : 3 * REACH]
        near_s[outer] = block[3 * REACH : 4 * REACH]
        up = high == 1
        columns = unfold(block[4 * REACH : 4 * REACH + 1], receivers)
        half = columns.shape[0] - REACH
        deep = [jnp.where(up, columns[j : j + 1], columns[3 - j : 4 - j]) for j in range(REACH)]
        factor = [
            jnp.where(up, columns[REACH + m : REACH + m + 1], columns[REACH + half - 1 - m : REACH + half - m])
            for m in range(half)
        ]
        beyond = [jnp.zeros((1, receivers), f32)] * REACH
        for index, hop in enumerate(hops):
            side = far_high if index == 0 else 1 - far_high
            last = hop.shape[0] - 1
            for u in range(REACH):
                seen = jnp.where(up, hop[u : u + 1], hop[last - u : last - u + 1])
                beyond[u] = jnp.where(side == high, seen, beyond[u])
        src_depth = high * (src_layer - width) + (1 - high) * (-1 - src_layer)
        for j in range(REACH):
            source = jnp.where(src_depth == REACH + j, pulse_one, 0.0)
            deep[j] = deep[j] + jnp.where(same_column, source, 0.0)
            more = sum(STENCIL_WEIGHTS[4 + u - j] * beyond[u] for u in range(j + 1))
            deep[j] = deep[j] + factor[(REACH + j) // 2] * more
        return [
            factor[depth // 2] * sum(STENCIL_WEIGHTS[4 + j - depth] * deep[j] for j in range(depth + 1))
            for depth in range(REACH)
        ]

    gains_one = put(one, 1 - odd)
    gains_two = put(masked(two, inner), odd)
    cross(two_s, c2_s, size_y, REACH, REACH, False, lambda j: near_s[REACH + j])
    cross(two_s, c2_s, size_y, REACH, REACH, True, lambda j: near_s[REACH - 1 - j])
    cross(two_s, c2_s, size_y, REACH + width, REACH, False, lambda j: near_s[REACH + width + j])
    cross(two_s, c2_s, size_y, REACH + width, REACH, True, lambda j: near_s[REACH + width - 1 - j])

    lanes = lanes_in[...].astype(f32) > 0.5
    lo = REACH * size_y
    hi = lo + width * size_y
    layer = (rec[...] - (place * width - REACH) * plane) // plane
    gain = jnp.zeros((1, receivers), f32)
    for depth in range(REACH):
        low_layer = REACH - 1 - depth
        high_layer = REACH + width + depth
        one_side = layer == low_layer + (1 - odd) * (high_layer - low_layer)
        two_side = layer == low_layer + odd * (high_layer - low_layer)
        gain = jnp.where(one_side, gains_one[depth], jnp.where(two_side, gains_two[depth], gain))

    def spread_out(value, marks):
        placed = jnp.where(lanes, value, 0.0)
        dims = (((1,), (1,)), ((), ()))
        return sum(lax.dot_general(marks, part, dims, preferred_element_type=f32) for part in split3(placed))

    hot = hot_in[...]
    add_one = spread_out(values[0:1, :] - obs[0:1, :], hot[lo:hi])
    add_two = spread_out(values[1:2, :] + gain - obs[1:2, :], hot)
    for ch in range(0, width + 2 * REACH, STEP):
        extra = add_two[ch * size_y : (ch + STEP) * size_y].reshape(STEP, size_y, size_z)
        two_s[ch : ch + STEP, data, :] = two_s[ch : ch + STEP, data, :] + extra
    for ch in range(0, width, STEP):
        centre, total = laplace(two_s, ch + REACH, size_y, weights)
        extra = add_one[ch * size_y : (ch + STEP) * size_y].reshape(STEP, size_y, size_z)
        factor = courant(c2_s, ch + wide, STEP, size_y)
        adj_one = 2.0 * centre - near[ch : ch + STEP] + factor * total + extra
        first = first_s[ch + wide : ch + wide + STEP, data, :]
        now_field = cur[ch : ch + STEP]
        bend_two = sec_s[ch + REACH : ch + REACH + STEP] - 2.0 * first + now_field
        bend_one = first - 2.0 * now_field + prev[ch : ch + STEP]
        image = centre * bend_two + adj_one * bend_one
        image = image.reshape(STEP // 2, 2, size_y, size_z)
        image = image[:, 0] + image[:, 1]
        img_s[ch // 2 * size_y : (ch + STEP) // 2 * size_y, :] = image.reshape(STEP // 2 * size_y, size_z)
    grid_r = lax.broadcasted_iota(jnp.int32, (size_z, size_z), 0)
    grid_c = lax.broadcasted_iota(jnp.int32, (size_z, size_z), 1)
    gather = jnp.where(grid_r // 2 == grid_c, 1.0, 0.0).astype(f32)
    folded = img_s[pl.ds(0, rows, stride=2), :] + img_s[pl.ds(1, rows, stride=2), :]
    blocks = jnp.dot(folded, gather, precision=HIGHEST, preferred_element_type=f32)
    left = lane < size_z // 2
    turned = pltpu.roll(packed[...], size_z // 2, 1)
    own_vel = jnp.concatenate(
        [jnp.where(left, packed[...], turned), jnp.where(left, turned, packed[...])], axis=0
    )
    factor = 2.0 / (own_vel * own_vel * own_vel)
    pay[0:rows, :] = jnp.where(left, factor * blocks, own_vel)
    if with_models:
        pay[rows : rows + short, :] = model_one[...]
        pay[rows + short :, :] = fars[0][1:].reshape(2 * short, size_z)


def mix_kernel(*refs, cells):
    part, other, obs, update, misfit = refs[-5:]
    total = refs[0].shape[0]
    pays = [ref.at[at : at + total] for ref in refs[:-5] for at in range(0, ref.shape[0], total)]
    count = len(pays)
    f32 = jnp.float32
    misfit[...] = part[...] + other[...] - obs[...]
    rows = update.shape[0] * update.shape[1]
    lane = lax.broadcasted_iota(jnp.int32, (1, pays[0].shape[1]), 1)
    half = update.shape[2]
    model_lane = lane >= half
    mean = sum(ref[...] for ref in pays[1:]) + pays[0][...]
    mean = mean * (1.0 / count)

    def norm(diff):
        sq = diff * diff
        sq = jnp.concatenate([jnp.where(model_lane, sq[0:rows], 0.0), sq[rows:]], axis=0)
        sq = jnp.sum(sq.reshape(total // 8, 8, sq.shape[1]), axis=0)
        return jnp.sum(jnp.sum(sq, axis=1, keepdims=True), axis=0, keepdims=True)

    spread = jnp.zeros(mean.shape, f32)
    for ref in pays:
        diff = ref[...] - mean
        spread = spread + diff * diff
    spread = jnp.concatenate([jnp.where(model_lane, spread[0:rows], 0.0), spread[rows:]], axis=0)
    spread = jnp.sum(spread.reshape(total // 8, 8, spread.shape[1]), axis=0)
    spread = jnp.sum(jnp.sum(spread, axis=1, keepdims=True), axis=0, keepdims=True)
    band = (2.0 * count / (count * (count - 1))) * spread
    own = pays[0][...]
    mixed = own[0:rows]
    kernel_sum = jnp.ones((1, 1), f32)
    for ref in pays[1:]:
        weight = jnp.exp(-norm(ref[...] - own) / band)
        mixed = mixed + weight * ref[0:rows, :]
        kernel_sum = kernel_sum + weight
    coef = (2.0 * cells) / band
    pull = coef * (own[0:rows, half:] * kernel_sum - mixed[:, half:])
    update[...] = ((mixed[:, 0:half] + pull) * (1.0 / count)).reshape(update.shape)


def device_step(
    vel_coarse,
    fwd_prev,
    fwd_cur,
    adj_far,
    adj_near,
    src_cell,
    src_step,
    wavelet,
    rec_cell,
    observed,
):
    f32 = jnp.float32
    slabs = lax.axis_size("slab")
    count = lax.axis_size("particle")
    fast = is_fast(slabs, count)
    model = vel_coarse[0]
    prev, cur, far, near = fwd_prev[0], fwd_cur[0], adj_far[0], adj_near[0]
    width, size_y, size_z = prev.shape
    half, coarse_y, coarse_z = model.shape
    rows = half * coarse_y
    short = rows // 2
    near_layers = 4 * REACH + 1 + short // size_y
    far_layers = 1 + short // size_y
    receivers = rec_cell.shape[0]
    in_vmem = pl.BlockSpec(memory_space=pltpu.VMEM)
    padded = pltpu.VMEM((width + 2 * REACH, PITCH, size_z), f32)
    start = pl.pallas_call(
        start_kernel,
        out_shape=(
            pltpu.VMEM((near_layers, size_y, size_z), f32),
            pltpu.VMEM((near_layers, size_y, size_z), f32),
            pltpu.VMEM((far_layers, size_y, size_z), f32),
            pltpu.VMEM((short, size_z), f32),
            pltpu.VMEM((width, size_y, size_z), f32),
            pltpu.VMEM((width, size_y, size_z), f32),
            pltpu.VMEM((size_z, receivers), jnp.bfloat16),
            pltpu.VMEM((1, receivers), jnp.int32),
            pltpu.VMEM((1, wavelet.shape[0]), f32),
            pltpu.VMEM((2, receivers), f32),
        ),
        in_specs=[in_vmem] * 8,
        out_specs=(in_vmem,) * 10,
        scratch_shapes=[padded, padded, pltpu.VMEM((2 * rows, size_z), f32)],
        name="start_steps",
    )
    even = [(i, i + 1) for i in range(0, slabs - 1, 2)]
    if fast:
        model_one = swap(model, "slab", even)
    to_one, to_two, to_far, packed, *kept, obs = start(
        prev, cur, far, near, model, rec_cell[None], observed, wavelet[None]
    )
    one = swap(to_one, "slab", even)
    two = swap_uneven(to_two, slabs, count)
    if fast:
        to_far, model_one = pl.pallas_call(
            far_kernel,
            out_shape=(
                pltpu.VMEM((far_layers + short // size_y, size_y, size_z), f32),
                pltpu.VMEM((short, size_z), f32),
            ),
            in_specs=[in_vmem] * 2,
            out_specs=(in_vmem, in_vmem),
            name="join_messages",
        )(resident(to_far), resident(model_one))
    fars = [swap(to_far, "slab", [(i, i + 2) for i in range(slabs - 2) if i % 4 < 2])]
    others = [(i, i + 2) for i in range(slabs - 2) if i % 4 >= 2]
    if others:
        fars.append(swap(to_far, "slab", others))
    wide = 2 * REACH
    region = (width + wide) * size_y
    own_part, near_part, lanes, rec, pulses = kept
    in_smem = pl.BlockSpec(memory_space=pltpu.SMEM)
    plain = pltpu.VMEM((width + wide, size_y, size_z), f32)
    operands = (cur, own_part, packed, lanes, rec, pulses, one, two)
    forward = pl.pallas_call(
        forward_kernel,
        out_shape=(
            pltpu.VMEM((2, receivers), f32),
            pltpu.VMEM((2, receivers), f32),
            pltpu.VMEM((width + 2 * wide, PITCH, size_z), f32),
            plain,
            pltpu.VMEM((6 * rows, size_z), f32),
            pltpu.VMEM((region, receivers), jnp.bfloat16),
        ),
        in_specs=[in_smem] * 2 + [in_vmem] * len(operands),
        out_specs=(in_vmem,) * 6,
        scratch_shapes=[plain, pltpu.VMEM((3 * short, size_z), f32)],
        name="forward_steps",
    )
    samples, *waves = forward(src_cell, src_step, *[resident(block) for block in operands])
    if fast:
        part = samples + swap(samples, "slab", [(0, 1), (2, 3)])
    pay_rows = rows + 3 * short if fast else rows
    operands = (
        prev, cur, near, packed, near_part, lanes, rec, pulses, obs, one, two, *waves, *fars,
        *([model_one] if fast else []),
    )
    adjoint = pl.pallas_call(
        lambda *refs: adjoint_kernel(*refs, n_far=len(fars), with_models=fast),
        out_shape=pltpu.VMEM((pay_rows, size_z), f32),
        in_specs=[in_smem] * 2 + [in_vmem] * len(operands),
        out_specs=in_vmem,
        scratch_shapes=[plain, padded, pltpu.VMEM((2 * rows, size_z), f32)],
        name="adjoint_steps",
    )
    pay = adjoint(src_cell, src_step, *[resident(block) for block in operands])
    cells_coarse = rows * slabs * coarse_z
    if not fast:
        residual = lax.psum(samples, "slab") - observed
        gathered = lax.all_gather(pay, "particle", axis=0)
        models = gathered[:, :, coarse_z:]
        deltas = models[:, None] - models[None]
        dist = lax.psum(jnp.sum(deltas * deltas, axis=(2, 3)), "slab")
        band = jnp.sum(dist) / (count * (count - 1))
        row = lax.dynamic_index_in_dim(dist, lax.axis_index("particle"), 0, keepdims=False)
        weights = jnp.exp(-row / band)
        mixed = jnp.einsum("q,qrz->rz", weights, gathered, precision=HIGHEST)
        own = pay[:, coarse_z:]
        pull = (2.0 * cells_coarse / band) * (own * jnp.sum(weights) - mixed[:, coarse_z:])
        update = (mixed[:, :coarse_z] + pull) / count
        return (update.reshape(model.shape)[None], residual[None])

    cores = [(i, i ^ 1) for i in range(0, count, 2)]
    beside = swap(pay, "particle", cores)
    corner = swap(pay, "particle", [(i, i ^ 6) for i in range(count) if i < i ^ 6])
    both = pl.pallas_call(
        join_kernel,
        out_shape=pltpu.VMEM((2 * pay_rows, size_z), f32),
        in_specs=[in_vmem] * 2,
        out_specs=in_vmem,
        name="join_blocks",
    )(resident(pay), resident(beside))
    sides = [(i, i ^ 4) for i in (0, 2)] + [(i, i ^ 2) for i in (1, 5)]
    side = swap(both, "particle", sides)
    blocks = [pay, beside, corner, swap(corner, "particle", cores), side, swap(side, "particle", cores)]
    other = swap(part, "slab", [(0, 2), (1, 3)])
    update, residual = pl.pallas_call(
        lambda *refs: mix_kernel(*refs, cells=cells_coarse),
        out_shape=(
            jax.ShapeDtypeStruct(model.shape, f32),
            jax.ShapeDtypeStruct((2, receivers), f32),
        ),
        in_specs=[in_vmem] * (len(blocks) + 3),
        out_specs=(in_vmem, in_vmem),
        name="mix_particles",
    )(*[resident(block) for block in blocks], resident(part), resident(other), resident(obs))
    return (update[None], residual[None])


def solution(mesh):
    in_specs = (
        P("particle", "slab", None, None),
        P("particle", "slab", None, None),
        P("particle", "slab", None, None),
        P("particle", "slab", None, None),
        P("particle", "slab", None, None),
        P("particle"),
        P("particle"),
        P(),
        P(),
        P(),
    )
    out_specs = (P("particle", "slab", None, None), P("particle", None, None))
    return jax.shard_map(
        device_step, mesh=mesh, in_specs=in_specs, out_specs=out_specs, check_vma=False
    )
```

```python
import jax
import jax.numpy as jnp
from jax import lax
from jax.experimental import pallas as pl
from jax.experimental.pallas import tpu as pltpu
from jax.sharding import PartitionSpec as P


STENCIL_WEIGHTS = (-205.0 / 72.0, 8.0 / 5.0, -1.0 / 5.0, 8.0 / 315.0, -1.0 / 560.0)
COURANT_FACTOR = 0.1
REACH = 4
STEP = 4
PITCH = 32
HIGHEST = lax.Precision.HIGHEST


def swap_uneven(block, slabs, count):
    pairs = []
    for particle in range(count):
        base = particle * slabs
        pairs += [(base + i, base + i + 1) for i in range(1, slabs - 1, 2)]
        if particle % 2 == 0:
            pairs += [(base, base + slabs), (base + slabs - 1, base + 2 * slabs - 1)]
    return swap(block, ("particle", "slab"), pairs)


def resident(block):
    return pltpu.with_memory_space_constraint(block, pltpu.MemorySpace.VMEM)


def is_fast(slabs, count):
    return slabs == 4 and count == 8


def swap(block, axis, pairs):
    both = [(a, b) for a, b in pairs] + [(b, a) for a, b in pairs]
    return lax.ppermute(block, axis, both)


def lane_weights(size_z):
    lane = lax.broadcasted_iota(jnp.int32, (1, size_z), 1)
    below = [jnp.where(lane >= k, w, 0.0).astype(jnp.float32) for k, w in enumerate(STENCIL_WEIGHTS)]
    above = [
        jnp.where(lane < size_z - k, w, 0.0).astype(jnp.float32) for k, w in enumerate(STENCIL_WEIGHTS)
    ]
    return below, above


def clear_margins(ref, size_y):
    ref[:, 0:8, :] = jnp.zeros((ref.shape[0], 8, ref.shape[2]), jnp.float32)
    rest = PITCH - 8 - size_y
    ref[:, 8 + size_y : PITCH, :] = jnp.zeros((ref.shape[0], rest, ref.shape[2]), jnp.float32)


def laplace(ref, at, size_y, weights):
    below, above = weights
    data = pl.ds(8, size_y)
    size_z = ref.shape[2]
    centre = ref[at : at + STEP, data, :]
    flat = centre.reshape(STEP * size_y, size_z)
    total = (3.0 * STENCIL_WEIGHTS[0]) * centre
    for k in range(1, 5):
        pairs = (
            ref[at + k : at + k + STEP, data, :]
            + ref[at - k : at - k + STEP, data, :]
            + (ref[at : at + STEP, pl.ds(8 + k, size_y), :] + ref[at : at + STEP, pl.ds(8 - k, size_y), :])
        )
        along = pltpu.roll(flat, k, 1) * below[k] + pltpu.roll(flat, size_z - k, 1) * above[k]
        total = total + STENCIL_WEIGHTS[k] * pairs + along.reshape(STEP, size_y, size_z)
    return centre, total


def fill_courant(c2_ref, packed, size_z):
    grid_r = lax.broadcasted_iota(jnp.int32, (size_z, 2 * size_z), 0)
    grid_c = lax.broadcasted_iota(jnp.int32, (size_z, 2 * size_z), 1)
    spread = jnp.where(grid_r == grid_c // 2, 1.0, 0.0).astype(jnp.bfloat16)
    scaled = COURANT_FACTOR * packed
    parts = split3(scaled * scaled)
    fine = sum(jnp.dot(part, spread, preferred_element_type=jnp.float32) for part in parts)
    count = packed.shape[0]
    part = count if count < 16 else 16
    for start in range(0, count, part):
        for side in range(2):
            rows = fine[start : start + part, side * size_z : (side + 1) * size_z]
            base = 4 * start + 2 * part * side
            c2_ref[pl.ds(base, part, stride=2), :] = rows
            c2_ref[pl.ds(base + 1, part, stride=2), :] = rows


def courant(c2_ref, layer, count, size_y):
    size_z = c2_ref.shape[1]
    block = c2_ref[layer // 2 * size_y : (layer + count) // 2 * size_y, :]
    block = block.reshape(count // 2, 1, size_y, size_z)
    return jnp.broadcast_to(block, (count // 2, 2, size_y, size_z)).reshape(count, size_y, size_z)


def split3(values):
    high = values.astype(jnp.bfloat16)
    rest = values - high.astype(jnp.float32)
    middle = rest.astype(jnp.bfloat16)
    low = (rest - middle.astype(jnp.float32)).astype(jnp.bfloat16)
    return (high, middle, low)


def start_kernel(
    prev, cur, far, near, vel, rec, obs, wavelet, to_one, to_two, to_far, packed,
    own_part, near_part, lanes_out, rec_out, wavelet_out, obs_out, cur_s, near_s, c2_s
):
    width, size_y, size_z = prev.shape
    f32 = jnp.float32
    place = lax.axis_index("slab")
    odd = place % 2
    top = width - REACH
    plane = size_y * size_z
    data = pl.ds(8, size_y)
    weights = lane_weights(size_z)
    for ref, field in ((cur_s, cur), (near_s, near)):
        clear_margins(ref, size_y)
        for start in (0, REACH + width):
            ref[start : start + REACH, data, :] = jnp.zeros((REACH, size_y, size_z), f32)
        ref[REACH : REACH + width, data, :] = field[...]
    packed[...] = pack(vel[...])
    fill_courant(c2_s, packed[...], size_z)
    rec_out[...] = rec[...]
    obs_out[...] = obs[...]
    wavelet_out[...] = wavelet[...]
    for ch in range(0, width, STEP):
        factor = courant(c2_s, ch, STEP, size_y)
        centre, total = laplace(cur_s, ch + REACH, size_y, weights)
        part = 2.0 * centre - prev[ch : ch + STEP] + factor * total
        own_part[ch : ch + STEP] = part
        centre, total = laplace(near_s, ch + REACH, size_y, weights)
        near_part[ch : ch + STEP] = 2.0 * centre - far[ch : ch + STEP] + factor * total

    cells = rec[...]
    count = cells.shape[1]
    lanes = lax.broadcasted_iota(jnp.int32, (size_z, count), 0) == cells % size_z
    lanes = jnp.where(lanes, 1.0, 0.0).astype(jnp.bfloat16)
    lanes_out[...] = lanes
    in_row = lax.broadcasted_iota(jnp.int32, (size_y, count), 0) == cells % plane // size_z
    fields = jnp.concatenate(
        [own_part[...].reshape(width * size_y, size_z), c2_s[...], cur[...].reshape(width * size_y, size_z)],
        axis=0,
    )
    picked = sum(jnp.dot(part, lanes, preferred_element_type=f32) for part in split3(fields))
    picked = picked.reshape(-1, size_y, count)
    picked = jnp.sum(jnp.where(in_row[None], picked, 0.0), axis=1)
    half = width // 2
    columns = picked[width + half :]
    for ref, low in ((to_one, odd), (to_two, 1 - odd)):
        outer = pl.ds((1 - low) * top, REACH)
        ref[0:REACH] = own_part[outer]
        ref[REACH : 2 * REACH] = cur[outer]
        ref[2 * REACH : 3 * REACH] = near_part[outer]
        ref[3 * REACH : 4 * REACH] = near[outer]
        deep = jnp.where(low == 0, picked[0:REACH], picked[top:width])
        block = jnp.concatenate([deep, picked[width : width + half]], axis=0)
        ref[4 * REACH : 4 * REACH + 1] = fold(block, size_y, size_z)
        ref[4 * REACH + 1 :] = packed[...].reshape(-1, size_y, size_z)
    to_far[0:1] = fold(columns, size_y, size_z)
    to_far[1:] = packed[...].reshape(to_far.shape[0] - 1, size_y, size_z)


def pack(model):
    flat = model.reshape(model.shape[0] * model.shape[1], model.shape[2])
    half = flat.shape[0] // 2
    return jnp.concatenate([flat[:half], flat[half:]], axis=1)


def far_kernel(message, model, out, packed):
    packed[...] = pack(model[...])
    out[0 : message.shape[0]] = message[...]
    out[message.shape[0] :] = packed[...].reshape(-1, *out.shape[1:])


def fold(block, size_y, size_z):
    pieces = [block[:, at : at + size_z] for at in range(0, block.shape[1], size_z)]
    return jnp.concatenate(pieces, axis=0).reshape(-1, size_y, size_z)


def unfold(layer, count):
    flat = layer.reshape(-1, layer.shape[-1])
    rows = flat.shape[0] * flat.shape[1] // count
    return jnp.concatenate([flat[at : at + rows] for at in range(0, flat.shape[0], rows)], axis=1)


def crossing(sources, depth):
    terms = [STENCIL_WEIGHTS[depth + 1 + j] * sources[j] for j in range(REACH - depth)]
    return sum(terms[1:], terms[0])


def cross(ref, c2_s, size_y, at, shift, upward, read):
    data = pl.ds(8, size_y)
    for depth in range(REACH):
        layer = at + depth if upward else at - 1 - depth
        sources = [read(j) for j in range(REACH - depth)]
        fine = (layer + shift) // 2 * size_y
        factor = c2_s[fine : fine + size_y, :]
        ref[layer, data, :] = ref[layer, data, :] + factor * crossing(sources, depth)


def pulse_of(wavelet, at):
    ticks = lax.broadcasted_iota(jnp.int32, wavelet.shape, 1)
    return jnp.sum(jnp.where(ticks == at, wavelet[...], 0.0), axis=1, keepdims=True)


def masked(block, inner):
    return jnp.where(inner, block[...], 0.0)


def place_of_slab():
    place = lax.axis_index("slab")
    inner = (place > 0) & (place < lax.axis_size("slab") - 1)
    return place, place % 2, inner


def forward_kernel(
    src_cell, src_step, cur, own_part, packed, lanes_in, rec, wavelet, one, two,
    samples, values, first_s, sec_s, c2_s, hot_out, cur_s, vel_s
):
    width, size_y, size_z = cur.shape
    receivers = rec.shape[1]
    plane = size_y * size_z
    place, odd, inner = place_of_slab()
    f32 = jnp.float32
    data = pl.ds(8, size_y)
    lane = lax.broadcasted_iota(jnp.int32, (1, size_z), 1)
    weights = lane_weights(size_z)
    wide = 2 * REACH
    clear_margins(first_s, size_y)
    for start in (0, width + wide + REACH):
        first_s[start : start + REACH, data, :] = jnp.zeros((REACH, size_y, size_z), f32)
    cur_s[REACH : REACH + width] = cur[...]
    first_s[wide : wide + width, data, :] = own_part[...]
    short = packed.shape[0]
    vel_s[short : 2 * short] = packed[...]

    def put(block, high):
        outer = pl.ds(high * (width + REACH), REACH)
        first_s[pl.ds(high * (width + REACH) + REACH, REACH), data, :] = block[0:REACH]
        cur_s[outer] = block[REACH : 2 * REACH]
        vel_s[pl.ds(high * 2 * short, short)] = block[4 * REACH + 1 :].reshape(short, size_z)

    put(one, 1 - odd)
    put(masked(two, inner), odd)
    fill_courant(c2_s, vel_s[...], size_z)
    cross(first_s, c2_s, size_y, wide, 0, False, lambda j: cur_s[REACH + j])
    cross(first_s, c2_s, size_y, wide, 0, True, lambda j: cur_s[REACH - 1 - j])
    cross(first_s, c2_s, size_y, wide + width, 0, False, lambda j: cur_s[REACH + width + j])
    cross(first_s, c2_s, size_y, wide + width, 0, True, lambda j: cur_s[REACH + width - 1 - j])

    cell = src_cell[0]
    now = src_step[0]
    src_layer = cell // plane - place * width

    def inject(ref, start, layers, offset, pulse):
        layer = src_layer + start
        inside = (layer >= 0) & (layer < layers)
        layer = jnp.clip(layer, 0, layers - 1)
        value = jnp.where(inside, pulse, 0.0)
        at = pl.ds(offset + cell % plane // size_z, 1)
        ref[layer, at, :] = ref[layer, at, :] + jnp.where(lane == cell % size_z, value, 0.0)

    inject(first_s.at[pl.ds(REACH, width + wide)], REACH, width + wide, 8, pulse_of(wavelet, now + 1))
    for ch in range(0, width + 2 * REACH, STEP):
        centre, total = laplace(first_s, ch + REACH, size_y, weights)
        factor = courant(c2_s, ch + REACH, STEP, size_y)
        sec_s[ch : ch + STEP] = 2.0 * centre - cur_s[ch : ch + STEP] + factor * total
    inject(sec_s, REACH, width + wide, 0, pulse_of(wavelet, now + 2))

    region = (width + 2 * REACH) * size_y
    row = (rec[...] - (place * width - REACH) * plane) // size_z
    hot = row == lax.broadcasted_iota(jnp.int32, (region, receivers), 0)
    hot = jnp.where(hot, 1.0, 0.0).astype(jnp.bfloat16)
    hot_out[...] = hot
    lanes = lanes_in[...].astype(f32) > 0.5
    lo = REACH * size_y
    hi = lo + width * size_y

    def read(field, marks):
        turned = field.T
        total = sum(jnp.dot(part, marks, preferred_element_type=f32) for part in split3(turned))
        return jnp.sum(jnp.where(lanes, total, 0.0), axis=0, keepdims=True)

    first_own = first_s[wide : wide + width, data, :].reshape(width * size_y, size_z)
    read_one = read(first_own, hot[lo:hi])
    read_two = read(sec_s[...].reshape(region, size_z), hot)
    values[0:1, :] = read_one
    values[1:2, :] = read_two
    samples[0:1, :] = read_one
    samples[1:2, :] = jnp.where((row >= lo) & (row < hi), read_two, 0.0)


def adjoint_kernel(
    src_cell, src_step, prev, cur, near, packed, near_part, lanes_in, rec, wavelet, obs, one, two,
    values, first_s, sec_s, c2_s, hot_in, *rest, n_far, with_models
):
    fars = rest[:n_far]
    rest = rest[n_far:]
    if with_models:
        model_one, rest = rest[0], rest[1:]
    pay, near_s, two_s, img_s = rest
    width, size_y, size_z = prev.shape
    short = packed.shape[0]
    rows = 2 * short
    receivers = rec.shape[1]
    plane = size_y * size_z
    place, odd, inner = place_of_slab()
    f32 = jnp.float32
    data = pl.ds(8, size_y)
    lane = lax.broadcasted_iota(jnp.int32, (1, size_z), 1)
    weights = lane_weights(size_z)
    wide = 2 * REACH
    clear_margins(two_s, size_y)
    near_s[REACH : REACH + width] = near[...]
    two_s[REACH : REACH + width, data, :] = near_part[...]
    cell = src_cell[0]
    src_layer = cell // plane - place * width
    same_column = rec[...] % plane == cell % plane
    pulse_one = pulse_of(wavelet, src_step[0] + 1)
    far_high = 1 - (place % 4) // 2
    hops = [unfold(block[0:1], receivers) for block in fars]

    def put(block, high):
        outer = pl.ds(high * (width + REACH), REACH)
        two_s[outer, data, :] = block[2 * REACH : 3 * REACH]
        near_s[outer] = block[3 * REACH : 4 * REACH]
        up = high == 1
        columns = unfold(block[4 * REACH : 4 * REACH + 1], receivers)
        half = columns.shape[0] - REACH
        deep = [jnp.where(up, columns[j : j + 1], columns[3 - j : 4 - j]) for j in range(REACH)]
        factor = [
            jnp.where(up, columns[REACH + m : REACH + m + 1], columns[REACH + half - 1 - m : REACH + half - m])
            for m in range(half)
        ]
        beyond = [jnp.zeros((1, receivers), f32)] * REACH
        for index, hop in enumerate(hops):
            side = far_high if index == 0 else 1 - far_high
            last = hop.shape[0] - 1
            for u in range(REACH):
                seen = jnp.where(up, hop[u : u + 1], hop[last - u : last - u + 1])
                beyond[u] = jnp.where(side == high, seen, beyond[u])
        src_depth = high * (src_layer - width) + (1 - high) * (-1 - src_layer)
        for j in range(REACH):
            source = jnp.where(src_depth == REACH + j, pulse_one, 0.0)
            deep[j] = deep[j] + jnp.where(same_column, source, 0.0)
            more = sum(STENCIL_WEIGHTS[4 + u - j] * beyond[u] for u in range(j + 1))
            deep[j] = deep[j] + factor[(REACH + j) // 2] * more
        return [
            factor[depth // 2] * sum(STENCIL_WEIGHTS[4 + j - depth] * deep[j] for j in range(depth + 1))
            for depth in range(REACH)
        ]

    gains_one = put(one, 1 - odd)
    gains_two = put(masked(two, inner), odd)
    cross(two_s, c2_s, size_y, REACH, REACH, False, lambda j: near_s[REACH + j])
    cross(two_s, c2_s, size_y, REACH, REACH, True, lambda j: near_s[REACH - 1 - j])
    cross(two_s, c2_s, size_y, REACH + width, REACH, False, lambda j: near_s[REACH + width + j])
    cross(two_s, c2_s, size_y, REACH + width, REACH, True, lambda j: near_s[REACH + width - 1 - j])

    lanes = lanes_in[...].astype(f32) > 0.5
    lo = REACH * size_y
    hi = lo + width * size_y
    layer = (rec[...] - (place * width - REACH) * plane) // plane
    gain = jnp.zeros((1, receivers), f32)
    for depth in range(REACH):
        low_layer = REACH - 1 - depth
        high_layer = REACH + width + depth
        one_side = layer == low_layer + (1 - odd) * (high_layer - low_layer)
        two_side = layer == low_layer + odd * (high_layer - low_layer)
        gain = jnp.where(one_side, gains_one[depth], jnp.where(two_side, gains_two[depth], gain))

    def spread_out(value, marks):
        placed = jnp.where(lanes, value, 0.0)
        dims = (((1,), (1,)), ((), ()))
        return sum(lax.dot_general(marks, part, dims, preferred_element_type=f32) for part in split3(placed))

    hot = hot_in[...]
    add_one = spread_out(values[0:1, :] - obs[0:1, :], hot[lo:hi])
    add_two = spread_out(values[1:2, :] + gain - obs[1:2, :], hot)
    for ch in range(0, width + 2 * REACH, STEP):
        extra = add_two[ch * size_y : (ch + STEP) * size_y].reshape(STEP, size_y, size_z)
        two_s[ch : ch + STEP, data, :] = two_s[ch : ch + STEP, data, :] + extra
    for ch in range(0, width, STEP):
        centre, total = laplace(two_s, ch + REACH, size_y, weights)
        extra = add_one[ch * size_y : (ch + STEP) * size_y].reshape(STEP, size_y, size_z)
        factor = courant(c2_s, ch + wide, STEP, size_y)
        adj_one = 2.0 * centre - near[ch : ch + STEP] + factor * total + extra
        first = first_s[ch + wide : ch + wide + STEP, data, :]
        now_field = cur[ch : ch + STEP]
        bend_two = sec_s[ch + REACH : ch + REACH + STEP] - 2.0 * first + now_field
        bend_one = first - 2.0 * now_field + prev[ch : ch + STEP]
        image = centre * bend_two + adj_one * bend_one
        image = image.reshape(STEP // 2, 2, size_y, size_z)
        image = image[:, 0] + image[:, 1]
        img_s[ch // 2 * size_y : (ch + STEP) // 2 * size_y, :] = image.reshape(STEP // 2 * size_y, size_z)
    grid_r = lax.broadcasted_iota(jnp.int32, (size_z, size_z), 0)
    grid_c = lax.broadcasted_iota(jnp.int32, (size_z, size_z), 1)
    gather = jnp.where(grid_r // 2 == grid_c, 1.0, 0.0).astype(jnp.bfloat16)
    folded = img_s[pl.ds(0, rows, stride=2), :] + img_s[pl.ds(1, rows, stride=2), :]
    blocks = sum(jnp.dot(part, gather, preferred_element_type=f32) for part in split3(folded))
    left = lane < size_z // 2
    turned = pltpu.roll(packed[...], size_z // 2, 1)
    own_vel = jnp.concatenate(
        [jnp.where(left, packed[...], turned), jnp.where(left, turned, packed[...])], axis=0
    )
    factor = 2.0 / (own_vel * own_vel * own_vel)
    pay[0:rows, :] = jnp.where(left, factor * blocks, own_vel)
    if with_models:
        pay[rows : rows + short, :] = model_one[...]
        pay[rows + short :, :] = fars[0][1:].reshape(2 * short, size_z)


def mix_kernel(*refs, cells):
    count = len(refs) - 5
    pays = refs[:count]
    part, other, obs, update, misfit = refs[count:]
    f32 = jnp.float32
    misfit[...] = part[...] + other[...] - obs[...]
    rows = update.shape[0] * update.shape[1]
    lane = lax.broadcasted_iota(jnp.int32, (1, pays[0].shape[1]), 1)
    half = update.shape[2]
    model_lane = lane >= half
    total = pays[0].shape[0]
    mean = sum(ref[...] for ref in pays[1:]) + pays[0][...]
    mean = mean * (1.0 / count)

    def norm(diff):
        sq = diff * diff
        sq = jnp.concatenate([jnp.where(model_lane, sq[0:rows], 0.0), sq[rows:]], axis=0)
        sq = jnp.sum(sq.reshape(total // 8, 8, sq.shape[1]), axis=0)
        return jnp.sum(jnp.sum(sq, axis=1, keepdims=True), axis=0, keepdims=True)

    spread = jnp.zeros(mean.shape, f32)
    for ref in pays:
        diff = ref[...] - mean
        spread = spread + diff * diff
    spread = jnp.concatenate([jnp.where(model_lane, spread[0:rows], 0.0), spread[rows:]], axis=0)
    spread = jnp.sum(spread.reshape(total // 8, 8, spread.shape[1]), axis=0)
    spread = jnp.sum(jnp.sum(spread, axis=1, keepdims=True), axis=0, keepdims=True)
    band = (2.0 * count / (count * (count - 1))) * spread
    own = pays[0][...]
    mixed = own[0:rows]
    kernel_sum = jnp.ones((1, 1), f32)
    for ref in pays[1:]:
        weight = jnp.exp(-norm(ref[...] - own) / band)
        mixed = mixed + weight * ref[0:rows, :]
        kernel_sum = kernel_sum + weight
    coef = (2.0 * cells) / band
    pull = coef * (own[0:rows, half:] * kernel_sum - mixed[:, half:])
    update[...] = ((mixed[:, 0:half] + pull) * (1.0 / count)).reshape(update.shape)


def device_step(
    vel_coarse,
    fwd_prev,
    fwd_cur,
    adj_far,
    adj_near,
    src_cell,
    src_step,
    wavelet,
    rec_cell,
    observed,
):
    f32 = jnp.float32
    slabs = lax.axis_size("slab")
    count = lax.axis_size("particle")
    fast = is_fast(slabs, count)
    model = vel_coarse[0]
    prev, cur, far, near = fwd_prev[0], fwd_cur[0], adj_far[0], adj_near[0]
    width, size_y, size_z = prev.shape
    half, coarse_y, coarse_z = model.shape
    rows = half * coarse_y
    short = rows // 2
    near_layers = 4 * REACH + 1 + short // size_y
    far_layers = 1 + short // size_y
    receivers = rec_cell.shape[0]
    in_vmem = pl.BlockSpec(memory_space=pltpu.VMEM)
    padded = pltpu.VMEM((width + 2 * REACH, PITCH, size_z), f32)
    start = pl.pallas_call(
        start_kernel,
        out_shape=(
            pltpu.VMEM((near_layers, size_y, size_z), f32),
            pltpu.VMEM((near_layers, size_y, size_z), f32),
            pltpu.VMEM((far_layers, size_y, size_z), f32),
            pltpu.VMEM((short, size_z), f32),
            pltpu.VMEM((width, size_y, size_z), f32),
            pltpu.VMEM((width, size_y, size_z), f32),
            pltpu.VMEM((size_z, receivers), jnp.bfloat16),
            pltpu.VMEM((1, receivers), jnp.int32),
            pltpu.VMEM((1, wavelet.shape[0]), f32),
            pltpu.VMEM((2, receivers), f32),
        ),
        in_specs=[in_vmem] * 8,
        out_specs=(in_vmem,) * 10,
        scratch_shapes=[padded, padded, pltpu.VMEM((2 * rows, size_z), f32)],
        name="start_steps",
    )
    even = [(i, i + 1) for i in range(0, slabs - 1, 2)]
    if fast:
        model_one = swap(model, "slab", even)
    to_one, to_two, to_far, packed, *kept, obs = start(
        prev, cur, far, near, model, rec_cell[None], observed, wavelet[None]
    )
    one = swap(to_one, "slab", even)
    two = swap_uneven(to_two, slabs, count)
    if fast:
        to_far, model_one = pl.pallas_call(
            far_kernel,
            out_shape=(
                pltpu.VMEM((far_layers + short // size_y, size_y, size_z), f32),
                pltpu.VMEM((short, size_z), f32),
            ),
            in_specs=[in_vmem] * 2,
            out_specs=(in_vmem, in_vmem),
            name="join_messages",
        )(resident(to_far), resident(model_one))
    fars = [swap(to_far, "slab", [(i, i + 2) for i in range(slabs - 2) if i % 4 < 2])]
    others = [(i, i + 2) for i in range(slabs - 2) if i % 4 >= 2]
    if others:
        fars.append(swap(to_far, "slab", others))
    wide = 2 * REACH
    region = (width + wide) * size_y
    own_part, near_part, lanes, rec, pulses = kept
    in_smem = pl.BlockSpec(memory_space=pltpu.SMEM)
    plain = pltpu.VMEM((width + wide, size_y, size_z), f32)
    operands = (cur, own_part, packed, lanes, rec, pulses, one, two)
    forward = pl.pallas_call(
        forward_kernel,
        out_shape=(
            pltpu.VMEM((2, receivers), f32),
            pltpu.VMEM((2, receivers), f32),
            pltpu.VMEM((width + 2 * wide, PITCH, size_z), f32),
            plain,
            pltpu.VMEM((6 * rows, size_z), f32),
            pltpu.VMEM((region, receivers), jnp.bfloat16),
        ),
        in_specs=[in_smem] * 2 + [in_vmem] * len(operands),
        out_specs=(in_vmem,) * 6,
        scratch_shapes=[plain, pltpu.VMEM((3 * short, size_z), f32)],
        name="forward_steps",
    )
    samples, *waves = forward(src_cell, src_step, *[resident(block) for block in operands])
    if fast:
        part = samples + swap(samples, "slab", [(0, 1), (2, 3)])
    pay_rows = rows + 3 * short if fast else rows
    operands = (
        prev, cur, near, packed, near_part, lanes, rec, pulses, obs, one, two, *waves, *fars,
        *([model_one] if fast else []),
    )
    adjoint = pl.pallas_call(
        lambda *refs: adjoint_kernel(*refs, n_far=len(fars), with_models=fast),
        out_shape=pltpu.VMEM((pay_rows, size_z), f32),
        in_specs=[in_smem] * 2 + [in_vmem] * len(operands),
        out_specs=in_vmem,
        scratch_shapes=[plain, padded, pltpu.VMEM((2 * rows, size_z), f32)],
        name="adjoint_steps",
    )
    pay = adjoint(src_cell, src_step, *[resident(block) for block in operands])
    cells_coarse = rows * slabs * coarse_z
    if not fast:
        residual = lax.psum(samples, "slab") - observed
        gathered = lax.all_gather(pay, "particle", axis=0)
        models = gathered[:, :, coarse_z:]
        deltas = models[:, None] - models[None]
        dist = lax.psum(jnp.sum(deltas * deltas, axis=(2, 3)), "slab")
        band = jnp.sum(dist) / (count * (count - 1))
        row = lax.dynamic_index_in_dim(dist, lax.axis_index("particle"), 0, keepdims=False)
        weights = jnp.exp(-row / band)
        mixed = jnp.einsum("q,qrz->rz", weights, gathered, precision=HIGHEST)
        own = pay[:, coarse_z:]
        pull = (2.0 * cells_coarse / band) * (own * jnp.sum(weights) - mixed[:, coarse_z:])
        update = (mixed[:, :coarse_z] + pull) / count
        return (update.reshape(model.shape)[None], residual[None])

    blocks = {0: pay}
    for flip in (6, 4, 2):
        blocks[flip] = swap(pay, "particle", [(i, i ^ flip) for i in range(count) if i < i ^ flip])
    for flip in (0, 6, 4, 2):
        pairs = [(i, i ^ 1) for i in range(0, count, 2)]
        blocks[flip + 1] = swap(blocks[flip], "particle", pairs)
    other = swap(part, "slab", [(0, 2), (1, 3)])
    update, residual = pl.pallas_call(
        lambda *refs: mix_kernel(*refs, cells=cells_coarse),
        out_shape=(
            jax.ShapeDtypeStruct(model.shape, f32),
            jax.ShapeDtypeStruct((2, receivers), f32),
        ),
        in_specs=[in_vmem] * 11,
        out_specs=(in_vmem, in_vmem),
        name="mix_particles",
    )(*[resident(blocks[i]) for i in range(count)], resident(part), resident(other), resident(obs))
    return (update[None], residual[None])


def solution(mesh):
    in_specs = (
        P("particle", "slab", None, None),
        P("particle", "slab", None, None),
        P("particle", "slab", None, None),
        P("particle", "slab", None, None),
        P("particle", "slab", None, None),
        P("particle"),
        P("particle"),
        P(),
        P(),
        P(),
    )
    out_specs = (P("particle", "slab", None, None), P("particle", None, None))
    return jax.shard_map(
        device_step, mesh=mesh, in_specs=in_specs, out_specs=out_specs, check_vma=False
    )
```
